32 devices in a mesh: dp: 8 (over y, x, core), mp: 4 (over z).
Axes of the slice: x: 2, y: 2, z: 4, core: 2. Of those that a mesh axis runs over, the one named last changes fastest.
Arguments:
- tokens: bfloat16 [8192, 1152], P('dp'), may hold values from -6 to 6
- cotangent: bfloat16 [8192, 1152], P('dp'), may hold values from -6 to 6
- lengths: int32 [8], P('dp'), may hold values from 512 to 1024, as said below
- rates: float32 [6], replicated, as said below
- query_weight: float32 [1152, 1024], P('dp', 'mp'), may hold values from -0.1875 to 0.1875
- query_moment: float32 [1152, 1024], P('dp', 'mp'), may hold values from -256 to 256
- query_average: float32 [1152, 1024], P('dp', 'mp'), may hold values from -0.1875 to 0.1875
- output_weight: float32 [1024, 1152], P('mp', 'dp'), may hold values from -1.5 to 1.5
- output_moment: float32 [1024, 1152], P('mp', 'dp'), may hold values from -56 to 56
- output_average: float32 [1024, 1152], P('mp', 'dp'), may hold values from -1.5 to 1.5
- gating_weight: float32 [2, 1152, 6912], P(None, 'dp', 'mp'), may hold values from -0.1875 to 0.1875
- gating_moment: float32 [2, 1152, 6912], P(None, 'dp', 'mp'), may hold values from -128 to 128
- gating_average: float32 [2, 1152, 6912], P(None, 'dp', 'mp'), may hold values from -0.1875 to 0.1875
- down_weight: float32 [6912, 1152], P('mp', 'dp'), may hold values from -0.078125 to 0.078125
- down_moment: float32 [6912, 1152], P('mp', 'dp'), may hold values from -256 to 256
- down_average: float32 [6912, 1152], P('mp', 'dp'), may hold values from -0.078125 to 0.078125
- context_weight: float32 [2, 1152, 256], P(None, ('dp', 'mp')), may hold values from -0.1875 to 0.1875
- context_moment: float32 [2, 1152, 256], P(None, ('dp', 'mp')), may hold values from -512 to 512
- context_average: float32 [2, 1152, 256], P(None, ('dp', 'mp')), may hold values from -0.1875 to 0.1875
- gains_weight: float32 [2, 1152], P(None, ('dp', 'mp')), may hold values from 0.5 to 1.5
- gains_moment: float32 [2, 1152], P(None, ('dp', 'mp')), may hold values from -160 to 160
- gains_average: float32 [2, 1152], P(None, ('dp', 'mp')), may hold values from 0.5 to 1.5
Outputs:
- block_out: float32 [8192, 1152], P(('dp', 'mp'))
- tokens_grad: float32 [8192, 1152], P(('dp', 'mp'))
- query_grads: float32 [1152, 1024], P('dp', 'mp')
- query_moments: float32 [1152, 1024], P('dp', 'mp')
- query_averages: float32 [1152, 1024], P('dp', 'mp')
- query_updated: float32 [1152, 1024], P('dp', 'mp')
- output_grads: float32 [1024, 1152], P('mp', 'dp')
- output_moments: float32 [1024, 1152], P('mp', 'dp')
- output_averages: float32 [1024, 1152], P('mp', 'dp')
- output_updated: float32 [1024, 1152], P('mp', 'dp')
- gating_grads: float32 [2, 1152, 6912], P(None, 'dp', 'mp')
- gating_moments: float32 [2, 1152, 6912], P(None, 'dp', 'mp')
- gating_averages: float32 [2, 1152, 6912], P(None, 'dp', 'mp')
- gating_updated: float32 [2, 1152, 6912], P(None, 'dp', 'mp')
- down_grads: float32 [6912, 1152], P('mp', 'dp')
- down_moments: float32 [6912, 1152], P('mp', 'dp')
- down_averages: float32 [6912, 1152], P('mp', 'dp')
- down_updated: float32 [6912, 1152], P('mp', 'dp')
- context_grads: float32 [2, 1152, 256], P(None, ('dp', 'mp'))
- context_moments: float32 [2, 1152, 256], P(None, ('dp', 'mp'))
- context_averages: float32 [2, 1152, 256], P(None, ('dp', 'mp'))
- context_updated: float32 [2, 1152, 256], P(None, ('dp', 'mp'))
- gains_grads: float32 [2, 1152], P(None, ('dp', 'mp'))
- gains_moments: float32 [2, 1152], P(None, ('dp', 'mp'))
- gains_averages: float32 [2, 1152], P(None, ('dp', 'mp'))
- gains_updated: float32 [2, 1152], P(None, ('dp', 'mp'))
The draws below stay inside these ranges and needn't reach their ends.
Inputs may be any that keep to these rules, and one draw needn't show every extreme that they name: `lengths`: the true token count of each sequence; slots at and after it are padding; at least one sequence fills all 1024 slots. `rates`: one positive learning rate per parameter kind.
All inputs are finite; a program needn't handle non-finite values.
Results may differ from the reference program's by a relative error of at most 0.014.
Values may be sent and summed in bfloat16 or wider, within the bound.
No kernel may reach another device: no remote copies, remote signals or barrier semaphores. Data moves between devices by JAX's collectives and lax.ppermute only.
A program may use at most 192 MiB of HBM per device.

```python
import jax
import jax.numpy as jnp
from jax import lax

D = 1152
H = 4
HD = 256
FF = 6912
TOK_DEV = 1024
SEQS = 8
TOKENS = 8192


def draw_lengths(key, part):
    drawn_lengths = jax.random.randint(key, (SEQS,), TOK_DEV // 2, TOK_DEV + 1)
    chosen_slot = jax.random.randint(jax.random.fold_in(key, 7), (), 0, SEQS)
    slot_index = jnp.arange(SEQS)
    return jnp.where(slot_index == chosen_slot, TOK_DEV, drawn_lengths).astype(jnp.int32)


def draw_rates(key, part):
    token_root = float(TOKENS) ** 0.5
    grad_sizes = jnp.array([0.5, 0.1, 0.25, 0.5, 1.0, 0.3], jnp.float32) * token_root
    weight_spreads = jnp.array([D ** (-0.5), (H * HD // 64) ** (-0.5), D ** (-0.5), FF ** (-0.5), D ** (-0.5), 0.5], jnp.float32)
    jitter_factors = jax.random.uniform(key, (6,), jnp.float32, 0.7, 1.4)
    return (weight_spreads / (2.5 * grad_sizes) * jitter_factors).astype(jnp.float32)


def shard_levels(own_key, extent, shards, low, largest):
    def one(position, parts):
        steps = jax.random.uniform(jax.random.fold_in(jax.random.fold_in(own_key, 6), position), (parts,), jnp.float32, low / len(shards), largest / len(shards))
        return jnp.repeat(jnp.exp(steps), extent[position] // parts).reshape((-1,) + (1,) * (len(extent) - position - 1))

    loudness = one(*shards[0])
    for cut in shards[1:]:
        loudness = loudness * one(*cut)
    return loudness


def centred(own_key, shape, spread, reach, cuts=(), held_as=jnp.bfloat16):
    entries = jax.random.normal(own_key, shape, jnp.float32) * spread
    if len(cuts) > 0:
        entries = shard_levels(own_key, shape, cuts, -0.22, 0.18) * entries
    return jnp.clip(entries, min=-reach, max=reach).astype(held_as)


def setup_inputs(seed: int = 0) -> dict:
    streams_of = jax.random.split(jax.random.key(seed), 23)
    tokens = centred(streams_of[0], (TOKENS, D), 1.0, 6.0, ((0, 8),))
    cotangent = centred(streams_of[1], (TOKENS, D), 1.0, 6.0, ((0, 8),))
    lengths = draw_lengths(jax.random.fold_in(streams_of[22], 71), 0)
    rates = draw_rates(jax.random.fold_in(streams_of[22], 71), 0)
    query_weight = centred(streams_of[4], (D, H * HD), D ** -0.5, 0.1875, ((0, 8), (1, 4)), jnp.float32)
    query_moment = centred(streams_of[5], (D, H * HD), (0.5 * TOKENS ** 0.5), 256.0, ((0, 8), (1, 4)), jnp.float32)
    query_average = centred(streams_of[6], (D, H * HD), D ** -0.5, 0.1875, ((0, 8), (1, 4)), jnp.float32)
    output_weight = centred(streams_of[7], (H * HD, D), (H * HD // 64) ** -0.5, 1.5, ((0, 4), (1, 8)), jnp.float32)
    output_moment = centred(streams_of[8], (H * HD, D), (0.1 * TOKENS ** 0.5), 56.0, ((0, 4), (1, 8)), jnp.float32)
    output_average = centred(streams_of[9], (H * HD, D), (H * HD // 64) ** -0.5, 1.5, ((0, 4), (1, 8)), jnp.float32)
    gating_weight = centred(streams_of[10], (2, D, FF), D ** -0.5, 0.1875, ((1, 8), (2, 4)), jnp.float32)
    gating_moment = centred(streams_of[11], (2, D, FF), (0.25 * TOKENS ** 0.5), 128.0, ((1, 8), (2, 4)), jnp.float32)
    gating_average = centred(streams_of[12], (2, D, FF), D ** -0.5, 0.1875, ((1, 8), (2, 4)), jnp.float32)
    down_weight = centred(streams_of[13], (FF, D), FF ** -0.5, 0.078125, ((0, 4), (1, 8)), jnp.float32)
    down_moment = centred(streams_of[14], (FF, D), (0.5 * TOKENS ** 0.5), 256.0, ((0, 4), (1, 8)), jnp.float32)
    down_average = centred(streams_of[15], (FF, D), FF ** -0.5, 0.078125, ((0, 4), (1, 8)), jnp.float32)
    context_weight = centred(streams_of[16], (2, D, HD), D ** -0.5, 0.1875, ((1, 32),), jnp.float32)
    context_moment = centred(streams_of[17], (2, D, HD), (1.0 * TOKENS ** 0.5), 512.0, ((1, 32),), jnp.float32)
    context_average = centred(streams_of[18], (2, D, HD), D ** -0.5, 0.1875, ((1, 32),), jnp.float32)
    gains_weight = jnp.clip(1.0 + 0.1 * jax.random.normal(streams_of[19], (2, D), jnp.float32), 0.5, 1.5)
    gains_moment = centred(streams_of[20], (2, D), (0.3 * TOKENS ** 0.5), 160.0, ((1, 32),), jnp.float32)
    gains_average = jnp.clip(1.0 + 0.1 * jax.random.normal(streams_of[21], (2, D), jnp.float32), 0.5, 1.5)
    return {"tokens": tokens, "cotangent": cotangent, "lengths": lengths, "rates": rates, "query_weight": query_weight, "query_moment": query_moment, "query_average": query_average, "output_weight": output_weight, "output_moment": output_moment, "output_average": output_average, "gating_weight": gating_weight, "gating_moment": gating_moment, "gating_average": gating_average, "down_weight": down_weight, "down_moment": down_moment, "down_average": down_average, "context_weight": context_weight, "context_moment": context_moment, "context_average": context_average, "gains_weight": gains_weight, "gains_moment": gains_moment, "gains_average": gains_average}


@jax.custom_vjp
def low(v):
    return lax.optimization_barrier(v.astype(jnp.bfloat16)).astype(jnp.float32)

@jax.custom_vjp
def low_back(v):
    return v

def low_keep(v):
    return (low(v), None)

def low_pass(kept, grad):
    return (grad,)

def back_keep(v):
    return (v, None)

def back_low(kept, grad):
    return (low(grad),)
low.defvjp(low_keep, low_pass)
low_back.defvjp(back_keep, back_low)
EPSILON = 1e-06
MOMENTUM = 0.9
AVERAGING = 0.5
PRECISE = lax.Precision.HIGHEST

def rms_norm(tensor, gain_vec):
    return tensor * lax.rsqrt(lax.optimization_barrier(jnp.mean(tensor * tensor, axis=-1, keepdims=True)) + EPSILON) * gain_vec

def rotation(length, head_size):
    halfway = head_size // 2
    frequency = 1000000.0 ** (-(jnp.arange(halfway).astype(jnp.float32) * 2.0 / head_size))
    angles = jnp.arange(length).astype(jnp.float32)[:, None] * frequency[None, :]
    return (jnp.cos(angles), jnp.sin(angles))

def rotate(tensor, cosine, sine_tab):
    halfway = tensor.shape[-1] // 2
    former = tensor[..., :halfway]
    latter = tensor[..., halfway:]
    cos_rows = cosine[:, None, :]
    sin_rows = sine_tab[:, None, :]
    return jnp.concatenate([former * cos_rows - latter * sin_rows, latter * cos_rows + former * sin_rows], axis=-1)

def advance(gradient, moment, average, weight, step_rate):
    moment_new = MOMENTUM * moment + gradient
    weight_new = weight - step_rate * (gradient + MOMENTUM * moment_new)
    average_new = AVERAGING * average + (1.0 - AVERAGING) * weight_new
    return (gradient, moment_new, average_new, weight_new)

def reference(tokens, cotangent, lengths, rates, query_weight, query_moment, query_average, output_weight, output_moment, output_average, gating_weight, gating_moment, gating_average, down_weight, down_moment, down_average, context_weight, context_moment, context_average, gains_weight, gains_moment, gains_average):
    seq_count = lengths.shape[0]
    seq_rows = tokens.shape[0] // seq_count
    model_width = tokens.shape[1]
    places = jnp.arange(seq_rows).astype(jnp.int32)
    causal = places[None, :] <= places[:, None]
    cosine, sine_tab = rotation(seq_rows, HD)

    def forward(inputs, length, w_query, w_output, w_gating, w_down, w_context, gains):
        allowed = causal & (places[None, :] < length)
        normed = low(rms_norm(inputs, gains[0]))
        context_low = low(w_context)
        gating_low = low(w_gating)
        query = low_back(jnp.dot(normed, low(w_query), precision=PRECISE)).reshape(seq_rows, H, HD)
        keys_raw = low_back(jnp.dot(normed, context_low[0], precision=PRECISE))
        values = low(low_back(jnp.dot(normed, context_low[1], precision=PRECISE)))
        query = low(rotate(query, cosine, sine_tab))
        keys = low(rotate(keys_raw[:, None, :], cosine, sine_tab)[:, 0])

        def attend_head(head_query):
            scores = jnp.dot(head_query, keys.T, precision=PRECISE) * 0.0625
            scores = low_back(scores)
            scores = jnp.where(allowed, scores, -1e+30)
            highest = lax.optimization_barrier(jnp.max(scores, axis=-1, keepdims=True))
            weights = jnp.exp(scores - highest)
            probs = weights / lax.optimization_barrier(jnp.sum(weights, axis=-1, keepdims=True))
            return jnp.dot(low(probs), values, precision=PRECISE)
        mixed = lax.map(jax.checkpoint(attend_head), jnp.transpose(query, (1, 0, 2)))
        mixed = low(low_back(jnp.transpose(mixed, (1, 0, 2)).reshape(seq_rows, H * HD)))
        middle = inputs + low_back(jnp.dot(mixed, low(w_output), precision=PRECISE))
        normed_two = low(rms_norm(middle, gains[1]))
        gate_pre = low_back(jnp.dot(normed_two, gating_low[0], precision=PRECISE))
        up_pre = low_back(jnp.dot(normed_two, gating_low[1], precision=PRECISE))
        hidden = low(jax.nn.gelu(gate_pre, approximate=True) * up_pre)
        return middle + jnp.dot(hidden, low(w_down), precision=PRECISE)
    weights_all = (query_weight, output_weight, gating_weight, down_weight, context_weight, gains_weight)

    def step(totals, seq_item):
        inputs, grad_rows, length = seq_item
        valid = (places < length).astype(jnp.float32)[:, None]

        def closed(inputs_f, w_query, w_output, w_gating, w_down, w_context, gains):
            return forward(inputs_f, length, w_query, w_output, w_gating, w_down, w_context, gains)
        seq_out, pull = jax.vjp(closed, inputs.astype(jnp.float32), query_weight, output_weight, gating_weight, down_weight, context_weight, gains_weight)
        grads = pull(grad_rows.astype(jnp.float32) * valid)
        totals = tuple((running + piece_grad for running, piece_grad in zip(totals, grads[1:])))
        return (totals, (seq_out, grads[0]))
    zeros_all = tuple((jnp.zeros(param.shape, jnp.float32) for param in weights_all))
    totals, (outs_seq, grads_seq) = lax.scan(step, zeros_all, (tokens.reshape(seq_count, seq_rows, model_width), cotangent.reshape(seq_count, seq_rows, model_width), lengths))
    block_out = outs_seq.reshape(seq_count * seq_rows, model_width)
    tokens_grad = grads_seq.reshape(seq_count * seq_rows, model_width)
    query_grads, query_moments, query_averages, query_updated = advance(totals[0], query_moment, query_average, query_weight, rates[0])
    output_grads, output_moments, output_averages, output_updated = advance(totals[1], output_moment, output_average, output_weight, rates[1])
    gating_grads, gating_moments, gating_averages, gating_updated = advance(totals[2], gating_moment, gating_average, gating_weight, rates[2])
    down_grads, down_moments, down_averages, down_updated = advance(totals[3], down_moment, down_average, down_weight, rates[3])
    context_grads, context_moments, context_averages, context_updated = advance(totals[4], context_moment, context_average, context_weight, rates[4])
    gains_grads, gains_moments, gains_averages, gains_updated = advance(totals[5], gains_moment, gains_average, gains_weight, rates[5])
    return (block_out, tokens_grad, query_grads, query_moments, query_averages, query_updated, output_grads, output_moments, output_averages, output_updated, gating_grads, gating_moments, gating_averages, gating_updated, down_grads, down_moments, down_averages, down_updated, context_grads, context_moments, context_averages, context_updated, gains_grads, gains_moments, gains_averages, gains_updated)
```

```python
import jax
import jax.numpy as jnp
from jax import lax
from jax.sharding import PartitionSpec as P

HD = 256
LANES = 128
EPSILON = 1e-06
MOMENTUM = 0.9
AVERAGING = 0.5
BF = jnp.bfloat16
F32 = jnp.float32


def mm(a, b, dims):
    return lax.dot_general(a, b, (dims, ((), ())), preferred_element_type=F32)


def inverse_rms(tensor):
    return lax.rsqrt(jnp.mean(tensor * tensor, axis=-1, keepdims=True) + EPSILON)


def norm_back(grad_in, unit, inverse, gain_vec):
    scaled = grad_in * gain_vec
    return inverse * (scaled - unit * jnp.mean(scaled * unit, axis=-1, keepdims=True))


def rotation(length, head_size):
    halfway = head_size // 2
    frequency = 1000000.0 ** (-(jnp.arange(halfway).astype(F32) * 2.0 / head_size))
    angles = jnp.arange(length).astype(F32)[:, None] * frequency[None, :]
    return (jnp.cos(angles), jnp.sin(angles))


def rotate(tensor, cosine, sine_tab):
    halfway = tensor.shape[-1] // 2
    former = tensor[..., :halfway]
    latter = tensor[..., halfway:]
    return jnp.concatenate(
        [former * cosine - latter * sine_tab, latter * cosine + former * sine_tab], axis=-1
    )


def advance(gradient, moment, average, weight, step_rate):
    moment_new = MOMENTUM * moment + gradient
    weight_new = weight - step_rate * (gradient + MOMENTUM * moment_new)
    average_new = AVERAGING * average + (1.0 - AVERAGING) * weight_new
    return (gradient, moment_new, average_new, weight_new)


def swap(tensor, bit):
    count = lax.axis_size("dp")
    return lax.ppermute(tensor, "dp", [(i, i ^ bit) for i in range(count)])


def from_behind(tensor, step):
    count = lax.axis_size("mp")
    return lax.ppermute(tensor, "mp", [(i, (i + step) % count) for i in range(count)])


def from_ahead(tensor, step):
    count = lax.axis_size("mp")
    return lax.ppermute(tensor, "mp", [(i, (i - step) % count) for i in range(count)])


def bit_orders():
    bits = []
    while 2 ** len(bits) < lax.axis_size("dp"):
        bits.append(2 ** len(bits))
    outer = bits[1:]
    return (outer + bits[:1], outer[::-1] + bits[:1])


def spread(tensor, order):
    held = {0: tensor}
    for bit in order:
        held.update({k ^ bit: swap(piece, bit) for k, piece in list(held.items())})
    return held


def assemble(flows):
    me = lax.axis_index("dp")
    count = lax.axis_size("dp")
    share = flows[0][0].shape[0]
    width = sum(held[0].shape[1] for held in flows)
    whole = jnp.zeros((count * share, width), flows[0][0].dtype)
    column = 0
    for held in flows:
        for k in sorted(held):
            whole = lax.dynamic_update_slice(whole, held[k], ((me ^ k) * share, column))
        column += held[0].shape[1]
    return whole


def collect(tensor, order):
    me = lax.axis_index("dp")
    count = lax.axis_size("dp")
    depth = len(order)
    current = tensor.reshape((2,) * depth + (tensor.shape[0] // count, tensor.shape[1]))
    left = [2**j for j in reversed(range(depth))]
    for n, bit in enumerate(order):
        axis = left.index(bit)
        side = (me // bit) % 2
        keep = lax.dynamic_index_in_dim(current, side, axis, keepdims=False)
        send = lax.dynamic_index_in_dim(current, 1 - side, axis, keepdims=False)
        left.remove(bit)
        current = keep.astype(F32) + swap(send, bit).astype(F32)
        if n < depth - 1:
            current = current.astype(BF)
    return current


def split_three(tensor):
    high = lax.reduce_precision(tensor, 8, 7)
    rest = tensor - high
    middle = lax.reduce_precision(rest, 8, 7)
    return [high.astype(BF), middle.astype(BF), (rest - middle).astype(BF)]


def halves(tensor):
    cut = -(-tensor.shape[1] // (2 * LANES)) * LANES
    return (tensor[:, :cut], tensor[:, cut:])


def local(
    tokens,
    cotangent,
    lengths,
    rates,
    query_weight,
    query_moment,
    query_average,
    output_weight,
    output_moment,
    output_average,
    gating_weight,
    gating_moment,
    gating_average,
    down_weight,
    down_moment,
    down_average,
    context_weight,
    context_moment,
    context_average,
    gains_weight,
    gains_moment,
    gains_average,
):
    row_count, width = tokens.shape
    dp, mp = lax.axis_size("dp"), lax.axis_size("mp")
    place = lax.axis_index("mp")
    own_count = row_count // mp
    own_start = place * own_count
    share, piece = width // dp, width // (dp * mp)
    forth, back = bit_orders()
    forth_first, back_first = forth[-1:] + forth[:-1], back[-1:] + back[:-1]
    length = lengths[0]
    inputs = tokens.astype(F32)
    places = jnp.arange(row_count, dtype=jnp.int32)
    valid = (places < length).astype(F32)[:, None]

    def own_rows(tensor):
        return lax.dynamic_slice_in_dim(tensor, own_start, own_count, 0)

    def rows_at(tensor, step, count):
        return lax.dynamic_slice_in_dim(tensor, ((place - step) % mp) * count, count, 0)

    def gather_heads(tensor):
        return jnp.concatenate([tensor] + [from_behind(tensor, k) for k in range(1, mp)], axis=1)

    w_context_own = context_weight.astype(BF)
    gains_split = split_three(gains_weight)
    context_own = jnp.concatenate(
        [w_context_own[0], w_context_own[1]]
        + [part.T for part in gains_split]
        + [jnp.zeros((piece, LANES - 2 * len(gains_split)), BF)],
        axis=1,
    )
    context_parts = [context_own] + [from_behind(context_own, k) for k in range(1, mp)]
    ring = context_parts[::-1] * 2
    context_share = lax.dynamic_slice_in_dim(
        jnp.concatenate(ring, axis=0), (mp - 1 - place) * piece, share, 0
    )
    context_full = assemble([spread(context_share, back)])
    query_share = gather_heads(query_weight.astype(BF))
    w_query = assemble([spread(query_share, forth)])
    output_share = gather_heads(output_weight.T.astype(BF))
    output_a, output_b = halves(output_share)
    w_output = assemble([spread(output_a, forth), spread(output_b, back)])
    gating_low = gating_weight.astype(BF)
    down_a, down_b = halves(down_weight.T.astype(BF))
    w_gate = assemble([spread(gating_low[0], forth)])
    w_up = assemble([spread(gating_low[1], back)])
    w_down = assemble([spread(down_a, forth), spread(down_b, back)])

    w_context = context_full[:, : 2 * HD]
    gain_terms = context_full[:, 2 * HD : 2 * HD + 6].astype(F32).T
    gains = gain_terms[0:2] + gain_terms[2:4] + gain_terms[4:6]

    cosine, sine_tab = rotation(row_count, HD)
    cosine_own, sine_own = own_rows(cosine), own_rows(sine_tab)
    inverse = inverse_rms(inputs)
    normed = (inputs * inverse * gains[0]).astype(BF)
    normed_own = own_rows(normed)
    context_raw = mm(normed, w_context, ((1,), (0,)))
    keys = rotate(context_raw[:, :HD], cosine, sine_tab).astype(BF)
    values = context_raw[:, HD:].astype(BF)
    query_raw = mm(normed_own, w_query, ((1,), (0,)))
    heads = query_raw.shape[1] // HD
    query_heads = [
        rotate(query_raw[:, h * HD : (h + 1) * HD], cosine_own, sine_own).astype(BF)
        for h in range(heads)
    ]
    query = jnp.stack(query_heads)
    scores = jnp.einsum("hqd,kd->hqk", query, keys, preferred_element_type=F32) * 0.0625
    rows_here = own_start + jnp.arange(own_count, dtype=jnp.int32)
    allowed = (places[None, :] <= rows_here[:, None]) & (places[None, :] < length)
    scores = jnp.where(allowed[None], scores, -1e30)
    exped = jnp.exp(scores - jnp.max(scores, axis=-1, keepdims=True))
    probs = exped / jnp.sum(exped, axis=-1, keepdims=True)
    probs_low = probs.astype(BF)
    mixed_heads = jnp.einsum("hqk,kd->hqd", probs_low, values, preferred_element_type=F32)
    mixed = jnp.concatenate([mixed_heads[h].astype(BF) for h in range(heads)], axis=1)
    input_own = own_rows(inputs)
    middle = input_own + mm(mixed, w_output, ((1,), (1,)))
    inverse_two = inverse_rms(middle)
    unit_two = middle * inverse_two
    normed_two_own = (unit_two * gains[1]).astype(BF)

    normed_two = jnp.concatenate(
        [normed_two_own] + [from_behind(normed_two_own, k) for k in range(1, mp)], axis=0
    )
    grad_out = cotangent.astype(F32) * valid
    grad_low = grad_out.astype(BF)
    grad_rows = jnp.concatenate([rows_at(grad_low, k, own_count) for k in range(mp)], axis=0)
    gate_pre = mm(normed_two, w_gate, ((1,), (0,)))
    up_pre = mm(normed_two, w_up, ((1,), (0,)))
    grad_hidden = mm(grad_rows, w_down, ((1,), (0,)))

    def gated_unit(gate, up):
        return jax.nn.gelu(gate, approximate=True) * up

    hidden_full, unit_pull = jax.vjp(gated_unit, gate_pre, up_pre)
    hidden = hidden_full.astype(BF)
    grad_gate, grad_up = (part.astype(BF) for part in unit_pull(grad_hidden))
    normed_two_part = mm(grad_gate, w_gate, ((1,), (1,))) + mm(grad_up, w_up, ((1,), (1,)))

    def to_owners(part):
        total = part[:own_count]
        for k in range(1, mp):
            sent = from_ahead(part[k * own_count : (k + 1) * own_count].astype(BF), k)
            total = total + sent.astype(F32)
        return total

    grad_normed_two = to_owners(normed_two_part)
    feed_part = mm(hidden, w_down, ((1,), (1,)))
    block_out = middle + to_owners(feed_part)
    d_gate = mm(normed_two, grad_gate, ((0,), (0,))).astype(BF)
    d_up = mm(normed_two, grad_up, ((0,), (0,))).astype(BF)
    d_down = mm(grad_rows, hidden, ((0,), (0,))).astype(BF)

    grad_middle = own_rows(grad_out) + norm_back(grad_normed_two, unit_two, inverse_two, gains[1])
    middle_low = grad_middle.astype(BF)
    gain_two = jnp.sum(grad_normed_two * unit_two, axis=0)
    d_output = mm(middle_low, mixed, ((0,), (0,))).astype(BF)
    grad_mixed = mm(middle_low, w_output, ((1,), (0,))).astype(BF)
    grad_heads = jnp.stack([grad_mixed[:, h * HD : (h + 1) * HD] for h in range(heads)])
    grad_probs = jnp.einsum("hqd,kd->hqk", grad_heads, values, preferred_element_type=F32)
    inner = jnp.sum(probs * grad_probs, axis=-1, keepdims=True)
    grad_scores = (probs * (grad_probs - inner)).astype(BF)
    grad_query_rot = jnp.einsum("hqk,kd->hqd", grad_scores, keys, preferred_element_type=F32)
    grad_keys_rot = jnp.einsum("hqk,hqd->kd", grad_scores, query, preferred_element_type=F32)
    grad_values = jnp.einsum("hqk,hqd->kd", probs_low, grad_heads, preferred_element_type=F32)
    grad_query = jnp.concatenate(
        [
            rotate(grad_query_rot[h] * 0.0625, cosine_own, -sine_own).astype(BF)
            for h in range(heads)
        ],
        axis=1,
    )
    grad_keys = rotate(grad_keys_rot * 0.0625, cosine, -sine_tab)
    grad_context = jnp.concatenate([grad_keys.astype(BF), grad_values.astype(BF)], axis=1)

    grad_context_own = rows_at(grad_context, 0, own_count).astype(F32)
    for k in range(1, mp):
        sent = from_ahead(rows_at(grad_context, k, own_count), k)
        grad_context_own = grad_context_own + sent.astype(F32)
    grad_normed = mm(grad_query, w_query, ((1,), (1,))) + mm(
        grad_context_own.astype(BF), w_context, ((1,), (1,))
    )
    inverse_own = own_rows(inverse)
    tokens_grad = grad_middle + norm_back(
        grad_normed, input_own * inverse_own, inverse_own, gains[0]
    )

    d_query = mm(normed_own, grad_query, ((0,), (0,)))
    d_context = mm(normed, grad_context, ((0,), (0,)))
    gain_one = (
        jnp.sum(d_query * w_query.astype(F32), axis=1)
        + jnp.sum(d_context * w_context.astype(F32), axis=1)
    ) / gains[0]
    d_context = jnp.concatenate(
        [
            d_context.astype(BF),
            gain_one[:, None].astype(BF),
            gain_two[:, None].astype(BF),
            jnp.zeros((width, LANES - 2), BF),
        ],
        axis=1,
    )

    def join(parts):
        return jnp.concatenate(parts, axis=1)

    d_down_a, d_down_b = halves(d_down)
    d_output_a, d_output_b = halves(d_output)
    sum_gate = collect(d_gate, forth_first)
    sum_up = collect(d_up, back_first)
    sum_down = join([collect(d_down_a, forth_first), collect(d_down_b, back_first)]).T
    share_output = join([collect(d_output_a, forth_first), collect(d_output_b, back_first)])
    share_query = collect(d_query.astype(BF), forth_first)
    share_context = collect(d_context, back_first)

    def heads_to_owners(part):
        total = part[:, :HD]
        for k in range(1, mp):
            sent = from_ahead(part[:, k * HD : (k + 1) * HD].astype(BF), k)
            total = total + sent.astype(F32)
        return total

    sum_output = heads_to_owners(share_output).T
    sum_query = heads_to_owners(share_query)
    sum_context = rows_at(share_context, 0, piece)
    for k in range(1, mp):
        sent = from_ahead(rows_at(share_context, k, piece).astype(BF), k)
        sum_context = sum_context + sent.astype(F32)
    sum_gains = sum_context[:, 2 * HD : 2 * HD + 2].T
    sum_context = jnp.stack([sum_context[:, :HD], sum_context[:, HD : 2 * HD]])
    sum_gating = jnp.stack([sum_gate, sum_up])

    query_grads, query_moments, query_averages, query_updated = advance(
        sum_query, query_moment, query_average, query_weight, rates[0]
    )
    output_grads, output_moments, output_averages, output_updated = advance(
        sum_output, output_moment, output_average, output_weight, rates[1]
    )
    gating_grads, gating_moments, gating_averages, gating_updated = advance(
        sum_gating, gating_moment, gating_average, gating_weight, rates[2]
    )
    down_grads, down_moments, down_averages, down_updated = advance(
        sum_down, down_moment, down_average, down_weight, rates[3]
    )
    context_grads, context_moments, context_averages, context_updated = advance(
        sum_context, context_moment, context_average, context_weight, rates[4]
    )
    gains_grads, gains_moments, gains_averages, gains_updated = advance(
        sum_gains, gains_moment, gains_average, gains_weight, rates[5]
    )
    return (
        block_out,
        tokens_grad,
        query_grads,
        query_moments,
        query_averages,
        query_updated,
        output_grads,
        output_moments,
        output_averages,
        output_updated,
        gating_grads,
        gating_moments,
        gating_averages,
        gating_updated,
        down_grads,
        down_moments,
        down_averages,
        down_updated,
        context_grads,
        context_moments,
        context_averages,
        context_updated,
        gains_grads,
        gains_moments,
        gains_averages,
        gains_updated,
    )


def solution(mesh):
    return jax.shard_map(
        local,
        mesh=mesh,
        in_specs=(
            P("dp", None),
            P("dp", None),
            P("dp"),
            P(),
            P("dp", "mp"),
            P("dp", "mp"),
            P("dp", "mp"),
            P("mp", "dp"),
            P("mp", "dp"),
            P("mp", "dp"),
            P(None, "dp", "mp"),
            P(None, "dp", "mp"),
            P(None, "dp", "mp"),
            P("mp", "dp"),
            P("mp", "dp"),
            P("mp", "dp"),
            P(None, ("dp", "mp"), None),
            P(None, ("dp", "mp"), None),
            P(None, ("dp", "mp"), None),
            P(None, ("dp", "mp")),
            P(None, ("dp", "mp")),
            P(None, ("dp", "mp")),
        ),
        out_specs=(
            P(("dp", "mp"), None),
            P(("dp", "mp"), None),
            P("dp", "mp"),
            P("dp", "mp"),
            P("dp", "mp"),
            P("dp", "mp"),
            P("mp", "dp"),
            P("mp", "dp"),
            P("mp", "dp"),
            P("mp", "dp"),
            P(None, "dp", "mp"),
            P(None, "dp", "mp"),
            P(None, "dp", "mp"),
            P(None, "dp", "mp"),
            P("mp", "dp"),
            P("mp", "dp"),
            P("mp", "dp"),
            P("mp", "dp"),
            P(None, ("dp", "mp"), None),
            P(None, ("dp", "mp"), None),
            P(None, ("dp", "mp"), None),
            P(None, ("dp", "mp"), None),
            P(None, ("dp", "mp")),
            P(None, ("dp", "mp")),
            P(None, ("dp", "mp")),
            P(None, ("dp", "mp")),
        ),
        check_vma=False,
    )
```

```python
import jax
import jax.numpy as jnp
from jax import lax
from jax.experimental import pallas as pl
from jax.experimental.pallas import tpu as pltpu
from jax.sharding import PartitionSpec as P

HD = 256
LANES = 128
TILE = 256
VMEM_BYTES = 56 * 1024 * 1024
EPSILON = 1e-06
MOMENTUM = 0.9
AVERAGING = 0.5
BF = jnp.bfloat16
F32 = jnp.float32


def mm(a, b, dims):
    return lax.dot_general(a, b, (dims, ((), ())), preferred_element_type=F32)


def inverse_rms(tensor):
    return lax.rsqrt(jnp.mean(tensor * tensor, axis=-1, keepdims=True) + EPSILON)


def norm_back(grad_in, unit, inverse, gain_vec):
    scaled = grad_in * gain_vec
    return inverse * (scaled - unit * jnp.mean(scaled * unit, axis=-1, keepdims=True))


def rotation(length, head_size):
    halfway = head_size // 2
    frequency = 1000000.0 ** (-(jnp.arange(halfway).astype(F32) * 2.0 / head_size))
    angles = jnp.arange(length).astype(F32)[:, None] * frequency[None, :]
    return (jnp.cos(angles), jnp.sin(angles))


def rotate(tensor, cosine, sine_tab):
    halfway = tensor.shape[-1] // 2
    former = tensor[..., :halfway]
    latter = tensor[..., halfway:]
    return jnp.concatenate(
        [former * cosine - latter * sine_tab, latter * cosine + former * sine_tab], axis=-1
    )


def advance(gradient, moment, average, weight, step_rate):
    moment_new = MOMENTUM * moment + gradient
    weight_new = weight - step_rate * (gradient + MOMENTUM * moment_new)
    average_new = AVERAGING * average + (1.0 - AVERAGING) * weight_new
    return (gradient, moment_new, average_new, weight_new)


def swap(tensor, bit):
    count = lax.axis_size("dp")
    return lax.ppermute(tensor, "dp", [(i, i ^ bit) for i in range(count)])


def across_heads(tensor, bit):
    count = lax.axis_size("mp")
    return lax.ppermute(tensor, "mp", [(i, i ^ bit) for i in range(count)])


def bit_orders():
    bits = []
    while 2 ** len(bits) < lax.axis_size("dp"):
        bits.append(2 ** len(bits))
    outer = bits[1:]
    return (outer + bits[:1], outer[::-1] + bits[:1])


def split_three(tensor):
    high = lax.reduce_precision(tensor, 8, 7)
    rest = tensor - high
    middle = lax.reduce_precision(rest, 8, 7)
    return [high.astype(BF), middle.astype(BF), (rest - middle).astype(BF)]


def spread_on(pieces, order):
    held, offsets = jnp.concatenate(pieces, axis=0), [0, order[0]]
    for bit in order[1:-1]:
        held = jnp.concatenate([held, swap(held, bit)], axis=0)
        offsets = offsets + [k ^ bit for k in offsets]
    return [held, offsets]


def spread_out(group, order):
    held, offsets = group
    bit = order[-1]
    return [(held, offsets), (swap(held, bit), [k ^ bit for k in offsets])]


def spread_direct(tensor):
    offsets = list(range(0, lax.axis_size("dp"), 2))
    pieces = [tensor] + [swap(tensor, k) for k in offsets[1:]]
    held = jnp.concatenate(pieces, axis=0)
    return [(held, offsets), (swap(held, 1), [k + 1 for k in offsets])]


def spread_wide(pieces, second, order):
    offsets = [0, order[0]]
    for bit in order[1:-1]:
        sent = [swap(piece, bit) for piece in (second if len(pieces) == 2 else pieces)]
        pieces = pieces + sent
        offsets = offsets + [k ^ bit for k in offsets]
    return pieces, offsets


def spread_last(pieces, offsets, bit):
    pair = jnp.concatenate(pieces, axis=0)
    return [(pair, offsets), (swap(pair, bit), [k ^ bit for k in offsets])]


def round_up(number, unit):
    return -(-number // unit) * unit


def column_cuts(width):
    half = round_up(width // TILE, 2) // 2 * TILE
    first = round_up(half // TILE, 2) // 2 * TILE
    return half, [(0, first), (first, half), (half, width)]


def lay(groups):
    share = groups[0][0].shape[0] // len(groups[0][1])
    if share % 16 == 0:
        return groups
    me = lax.axis_index("dp")
    count = lax.axis_size("dp")
    whole = jnp.zeros((count * share, groups[0][0].shape[1]), groups[0][0].dtype)
    for array, offsets in groups:
        for n, k in enumerate(offsets):
            part = array[n * share : (n + 1) * share]
            whole = lax.dynamic_update_slice(whole, part, ((me ^ k) * share, 0))
    return [(whole, [])]


def arrays_of(groups):
    return [array for array, _ in groups]


def offsets_of(groups):
    return [offsets for _, offsets in groups]


def row_copies(me, shards, offsets, low, size, target, column, sem):
    copies = []
    columns, place = pl.ds(low, size), pl.ds(column, size)
    for shard, from_devices in zip(shards, offsets):
        if not from_devices:
            copies.append(
                pltpu.make_async_copy(shard.at[:, columns], target.at[:, place], sem)
            )
        for n, k in enumerate(from_devices):
            share = shard.shape[0] // len(from_devices)
            rows = pl.ds(pl.multiple_of((me ^ k) * share, 16), share)
            source = shard.at[pl.ds(n * share, share), columns]
            copies.append(pltpu.make_async_copy(source, target.at[rows, place], sem))
    return copies


def start_all(copies):
    for copy in copies:
        copy.start()


def wait_all(copies):
    for copy in copies:
        copy.wait()


def call(kernel, name, out_shape, operands, scratch):
    spaces = {
        "s": pl.BlockSpec(memory_space=pltpu.SMEM),
        "v": pl.BlockSpec(memory_space=pltpu.VMEM),
        "h": pl.BlockSpec(memory_space=pl.ANY),
    }
    return pl.pallas_call(
        kernel,
        out_shape=out_shape,
        in_specs=[spaces[space] for _, space in operands],
        out_specs=tuple(spaces["v"] for _ in out_shape),
        scratch_shapes=scratch,
        compiler_params=pltpu.CompilerParams(vmem_limit_bytes=VMEM_BYTES),
        cost_estimate=pl.CostEstimate(flops=1, transcendentals=0, bytes_accessed=1),
        name=name,
    )(*[array for array, _ in operands])


def shaped(rows, columns, kind=BF):
    return jax.ShapeDtypeStruct((rows, columns), kind)


def project(info, tokens, cosine, sine_tab, contexts):
    rows, width = tokens.shape
    block = min(rows, TILE)
    shards, offsets = arrays_of(contexts), offsets_of(contexts)
    wide = shards[0].shape[1]

    def kernel(info_ref, x_ref, cos_ref, sin_ref, *refs):
        shard_refs, refs = refs[: len(shards)], refs[len(shards) :]
        normed_ref, key_ref, value_ref, gain_ref, w_c, sems = refs
        copies = row_copies(info_ref[0], shard_refs, offsets, 0, wide, w_c, 0, sems.at[0])
        start_all(copies)
        wait_all(copies)
        terms = w_c[:, 2 * HD : 2 * HD + LANES].astype(F32).T
        gains = terms[0:2] + terms[2:4] + terms[4:6]
        gain_ref[...] = jnp.concatenate([gains] * 4, axis=0)
        for r in range(0, rows, block):
            span = pl.ds(r, block)
            x = x_ref[span, :].astype(F32)
            normed = (x * inverse_rms(x) * gains[0:1]).astype(BF)
            normed_ref[span, :] = normed
            raw = mm(normed, w_c[:, : 2 * HD], ((1,), (0,)))
            key_ref[span, :] = rotate(raw[:, :HD], cos_ref[span, :], sin_ref[span, :]).astype(BF)
            value_ref[span, :] = raw[:, HD:].astype(BF)

    return call(
        kernel,
        "project",
        (shaped(rows, width), *[shaped(rows, HD)] * 2, shaped(8, width, F32)),
        [(info, "s"), (tokens, "v"), (cosine, "v"), (sine_tab, "v")]
        + [(shard, "h") for shard in shards],
        [pltpu.VMEM((width, wide), BF), pltpu.SemaphoreType.DMA((1,))],
    )


def masked_scores(info_ref, query, keys):
    scores = mm(query, keys, ((1,), (1,))) * 0.0625
    at_row = info_ref[1] + lax.broadcasted_iota(jnp.int32, scores.shape, 0)
    at_key = lax.broadcasted_iota(jnp.int32, scores.shape, 1)
    allowed = (at_key <= at_row) & (at_key < info_ref[2])
    return jnp.where(allowed, scores, -1e30)


def attend(info, normed_own, keys, values, tokens_own, tables, gains, w_queries, w_outputs):
    own, width = tokens_own.shape
    q_shards, q_offsets = arrays_of(w_queries), offsets_of(w_queries)
    o_shards, o_offsets = arrays_of(w_outputs), offsets_of(w_outputs)
    across = q_shards[0].shape[1]

    def kernel(info_ref, own_ref, key_ref, value_ref, x_ref, cos_ref, sin_ref, gain_ref, *refs):
        q_refs, refs = refs[: len(q_shards)], refs[len(q_shards) :]
        o_refs, refs = refs[: len(o_shards)], refs[len(o_shards) :]
        query_ref, mixed_ref, middle_ref, normed_ref, log_ref, w_q, w_o, sems = refs
        copies = row_copies(info_ref[0], q_refs, q_offsets, 0, across, w_q, 0, sems.at[0])
        copies_o = row_copies(info_ref[0], o_refs, o_offsets, 0, across, w_o, 0, sems.at[1])
        start_all(copies)
        start_all(copies_o)
        wait_all(copies)
        keys, values = key_ref[...], value_ref[...]
        raw = mm(own_ref[...], w_q[...], ((1,), (0,)))
        for h in range(across // HD):
            columns = slice(h * HD, (h + 1) * HD)
            query = rotate(raw[:, columns], cos_ref[...], sin_ref[...]).astype(BF)
            query_ref[:, columns] = query
            scores = masked_scores(info_ref, query, keys)
            highest = jnp.max(scores, axis=-1, keepdims=True)
            exped = jnp.exp(scores - highest)
            total = jnp.sum(exped, axis=-1, keepdims=True)
            probs = (exped * (1.0 / total)).astype(BF)
            mixed_ref[:, columns] = mm(probs, values, ((1,), (0,))).astype(BF)
            log_ref[:, h : h + 1] = highest + jnp.log(total)
        wait_all(copies_o)
        middle = x_ref[...].astype(F32) + mm(mixed_ref[...], w_o[...], ((1,), (1,)))
        middle_ref[...] = middle
        normed_ref[...] = (middle * inverse_rms(middle) * gain_ref[1:2, :]).astype(BF)

    return call(
        kernel,
        "attend",
        (
            shaped(own, across),
            shaped(own, across),
            shaped(own, width, F32),
            shaped(own, width),
            shaped(own, LANES, F32),
        ),
        [(info, "s")]
        + [(array, "v") for array in (normed_own, keys, values, tokens_own, *tables, gains)]
        + [(shard, "h") for shard in q_shards + o_shards],
        [pltpu.VMEM((width, across), BF)] * 2 + [pltpu.SemaphoreType.DMA((2,))],
    )


def attend_back(
    info, parts, middle, grad_own, gains, queries, keys, values, log_sums, tables, w_outputs
):
    heads, n_parts = queries.shape[1] // HD, len(parts)
    own, width = middle.shape
    rows = keys.shape[0]
    output_shards, offsets = arrays_of(w_outputs), offsets_of(w_outputs)
    count = len(output_shards)

    def kernel(info_ref, *refs):
        part_refs, refs = refs[:n_parts], refs[n_parts:]
        middle_ref, grad_ref, gain_ref = refs[:3]
        query_ref, refs = refs[3], refs[4:]
        key_ref, value_ref, log_ref, cos_ref, sin_ref, cos_own, sin_own = refs[:7]
        shards, refs = refs[7 : 7 + count], refs[7 + count :]
        grad_middle_ref, low_ref, gain_two_ref, query_out, context_out, w_o, sem = refs
        copies = row_copies(info_ref[0], shards, offsets, 0, heads * HD, w_o, 0, sem.at[0])
        start_all(copies)
        grad_in = part_refs[0][...]
        for part_ref in part_refs[1:]:
            grad_in = grad_in + part_ref[...].astype(F32)
        middle = middle_ref[...]
        inverse = inverse_rms(middle)
        unit = middle * inverse
        gain_two = jnp.sum(grad_in * unit, axis=0, keepdims=True)
        gain_two_ref[...] = jnp.broadcast_to(gain_two, gain_two_ref.shape)
        grad_middle = grad_ref[...].astype(F32) + norm_back(
            grad_in, unit, inverse, gain_ref[1:2, :]
        )
        grad_middle_ref[...] = grad_middle
        low = grad_middle.astype(BF)
        low_ref[...] = low
        wait_all(copies)
        keys, values = key_ref[...], value_ref[...]
        grad_mixed = mm(low, w_o[...], ((1,), (0,))).astype(BF)
        grad_keys = grad_values = None
        for h in range(heads):
            query = query_ref[:, h * HD : (h + 1) * HD]
            scores = masked_scores(info_ref, query, keys)
            probs = jnp.exp(scores - log_ref[:, h : h + 1])
            grad_head = grad_mixed[:, h * HD : (h + 1) * HD]
            grad_probs = mm(grad_head, values, ((1,), (1,)))
            inner = jnp.sum(probs * grad_probs, axis=-1, keepdims=True)
            grad_scores = (probs * (grad_probs - inner)).astype(BF)
            turned = mm(grad_scores, keys, ((1,), (0,))) * 0.0625
            query_out[:, h * HD : (h + 1) * HD] = rotate(
                turned, cos_own[...], -sin_own[...]
            ).astype(BF)
            term_keys = mm(grad_scores, query, ((0,), (0,)))
            term_values = mm(probs.astype(BF), grad_head, ((0,), (0,)))
            grad_keys = term_keys if h == 0 else grad_keys + term_keys
            grad_values = term_values if h == 0 else grad_values + term_values
        context_out[:, :HD] = rotate(grad_keys * 0.0625, cos_ref[...], -sin_ref[...]).astype(BF)
        context_out[:, HD:] = grad_values.astype(BF)

    return call(
        kernel,
        "attend_back",
        (
            shaped(own, width, F32),
            shaped(own, width),
            shaped(8, width, F32),
            shaped(own, heads * HD),
            shaped(rows, 2 * HD),
        ),
        [(info, "s")]
        + [(part, "v") for part in parts]
        + [(middle, "v"), (grad_own, "v"), (gains, "v"), (queries, "v")]
        + [(array, "v") for array in (keys, values, log_sums, *tables)]
        + [(shard, "h") for shard in output_shards],
        [pltpu.VMEM((width, heads * HD), BF), pltpu.SemaphoreType.DMA((1,))],
    )


def store_sides(side, value, made, column, keep_ref, send_ref):
    blocks, share, _ = keep_ref.shape
    size = value.shape[1]
    for b in range(2 * blocks):
        made[b // 2, b % 2, :, :size] = value[b * share : (b + 1) * share].astype(BF)
    for b in range(blocks):
        keep_ref[b, :, column : column + size] = made[b, side, :, :size]
        send_ref[b, :, column : column + size] = made[b, 1 - side, :, :size]


def mixer_grads(
    info, normed, normed_own, grad_query, grad_context, low, mixed, gain_two, w_shards
):
    query_shards, context_shards = (arrays_of(groups) for groups in w_shards)
    offsets_q, offsets_c = (offsets_of(groups) for groups in w_shards)
    width = normed.shape[1]
    dp = lax.axis_size("dp")
    share = width // dp
    across = grad_query.shape[1]
    count = len(query_shards)
    first = jax.ShapeDtypeStruct((dp // 2, share, across + HD + LANES), BF)
    second = jax.ShapeDtypeStruct((dp // 2, share, across + HD), BF)

    def kernel(info_ref, *refs):
        normed_ref, own_ref, query_ref, context_ref, low_ref, mixed_ref, gain_ref = refs[:7]
        queries, contexts = refs[7 : 7 + count], refs[7 + count : 7 + 2 * count]
        keep_a, send_a, keep_b, send_b, w_q, w_c, made, sems = refs[7 + 2 * count :]
        side = info_ref[3]
        copies = row_copies(info_ref[0], queries, offsets_q, 0, across, w_q, 0, sems.at[0])
        copies_c = row_copies(info_ref[0], contexts, offsets_c, 0, 2 * HD, w_c, 0, sems.at[1])
        start_all(copies)
        start_all(copies_c)
        d_output = mm(low_ref[...], mixed_ref[...], ((0,), (0,)))
        halfway = across // HD // 2
        for h in range(across // HD):
            keep, send = (keep_a, send_a) if h < halfway else (keep_b, send_b)
            at = (2 * (h % halfway) + 1) * HD
            store_sides(side, d_output[:, h * HD : (h + 1) * HD], made, at, keep, send)
        d_query = mm(own_ref[...], query_ref[...], ((0,), (0,)))
        for h in range(across // HD):
            keep, send = (keep_a, send_a) if h < halfway else (keep_b, send_b)
            at = 2 * (h % halfway) * HD
            store_sides(side, d_query[:, h * HD : (h + 1) * HD], made, at, keep, send)
        d_context = mm(normed_ref[...], context_ref[...], ((0,), (0,)))
        store_sides(side, d_context[:, :HD], made, across, keep_a, send_a)
        store_sides(side, d_context[:, HD:], made, across, keep_b, send_b)
        wait_all(copies)
        wait_all(copies_c)
        gain_one = jnp.sum(d_query * w_q[...].astype(F32), axis=1, keepdims=True) + jnp.sum(
            d_context * w_c[...].astype(F32), axis=1, keepdims=True
        )
        second_gain = gain_ref[...].T
        lane = lax.broadcasted_iota(jnp.int32, (width, LANES), 1)
        both = jnp.where(lane == 0, gain_one, jnp.where(lane == 1, second_gain[:, 0:1], 0.0))
        store_sides(side, both, made, across + HD, keep_a, send_a)

    return call(
        kernel,
        "mixer_grads",
        (first, first, second, second),
        [(info, "s")]
        + [
            (array, "v")
            for array in (normed, normed_own, grad_query, grad_context, low, mixed, gain_two)
        ]
        + [(shard, "h") for shard in query_shards + context_shards],
        [
            pltpu.VMEM((width, across), BF),
            pltpu.VMEM((width, 2 * HD), BF),
            pltpu.VMEM((dp // 2, 2, share, across), BF),
            pltpu.SemaphoreType.DMA((2,)),
        ],
    )


def finish(info, grad_query, parts, grad_middle, tokens_own, gains, w_shards):
    query_shards, context_shards = (arrays_of(groups) for groups in w_shards)
    offsets_q, offsets_c = (offsets_of(groups) for groups in w_shards)
    own, width = grad_middle.shape
    across = grad_query.shape[1]
    count, n_parts = len(query_shards), len(parts)

    def kernel(info_ref, query_ref, *refs):
        part_refs, refs = refs[:n_parts], refs[n_parts:]
        middle_ref, x_ref, gain_ref = refs[:3]
        queries, contexts = refs[3 : 3 + count], refs[3 + count : 3 + 2 * count]
        out_ref, w_q, w_c, sems = refs[3 + 2 * count :]
        copies = row_copies(info_ref[0], queries, offsets_q, 0, across, w_q, 0, sems.at[0])
        copies_c = row_copies(info_ref[0], contexts, offsets_c, 0, 2 * HD, w_c, 0, sems.at[1])
        start_all(copies)
        start_all(copies_c)
        total = part_refs[0][...].astype(F32)
        for part_ref in part_refs[1:]:
            total = total + part_ref[...].astype(F32)
        x = x_ref[...].astype(F32)
        inverse = inverse_rms(x)
        wait_all(copies)
        wait_all(copies_c)
        grad_in = mm(query_ref[...], w_q[...], ((1,), (1,))) + mm(
            total.astype(BF), w_c[...], ((1,), (1,))
        )
        out_ref[...] = middle_ref[...] + norm_back(grad_in, x * inverse, inverse, gain_ref[0:1, :])

    return call(
        kernel,
        "finish",
        (shaped(own, width, F32),),
        [(info, "s"), (grad_query, "v")]
        + [(part, "v") for part in parts]
        + [(grad_middle, "v"), (tokens_own, "v"), (gains, "v")]
        + [(shard, "h") for shard in query_shards + context_shards],
        [
            pltpu.VMEM((width, across), BF),
            pltpu.VMEM((width, 2 * HD), BF),
            pltpu.SemaphoreType.DMA((2,)),
        ],
    )[0]


def feed_block(info, x, g, groups_a, groups_b, width, out_type):
    rows, depth = x.shape
    shards_a, shards_b = arrays_of(groups_a), arrays_of(groups_b)
    offsets, offsets_b = offsets_of(groups_a), offsets_of(groups_b)
    count = len(shards_a)
    half, cuts = column_cuts(width)

    def kernel(info_ref, x_ref, g_ref, *refs):
        first, second = refs[:count], refs[count : 2 * count]
        hid_ref, gate_ref, up_ref, feed_ref, back_ref = refs[2 * count : 2 * count + 5]
        w_gate, w_up, w_down, sems = refs[2 * count + 5 :]
        copies = []
        for n, (low, high) in enumerate(cuts):
            size = high - low
            source, at = (first, width + low) if high <= half else (second, width + low - half)
            group = []
            for shards, start, target in (
                (first, low, w_gate),
                (second, low, w_up),
                (source, at, w_down),
            ):
                own_offsets = offsets_b if shards is second else offsets
                group += row_copies(
                    info_ref[0], shards, own_offsets, start, size, target, low, sems.at[n]
                )
            copies.append(group)
            start_all(group)
        scale = 0.7978845608028654
        feed = back = None
        for n, (low, high) in enumerate(cuts):
            wait_all(copies[n])
            x, g = x_ref[...], g_ref[...]
            gate_w, up_w, down_w = w_gate[:, low:high], w_up[:, low:high], w_down[:, low:high]
            gate = mm(x, gate_w, ((1,), (0,)))
            up = mm(x, up_w, ((1,), (0,)))
            grad = mm(g, down_w, ((1,), (0,)))
            square = gate * gate
            tanh = jnp.tanh(scale * gate * (1.0 + 0.044715 * square))
            right = 0.5 * (1.0 + tanh)
            gelu = gate * right
            slope = right + gelu * (1.0 - tanh) * scale * (1.0 + 3 * 0.044715 * square)
            hidden = (gelu * up).astype(BF)
            grad_gate = (grad * up * slope).astype(BF)
            grad_up = (grad * gelu).astype(BF)
            hid_ref[:, low:high] = hidden
            gate_ref[:, low:high] = grad_gate
            up_ref[:, low:high] = grad_up
            feed_n = mm(hidden, down_w, ((1,), (1,)))
            back_n = mm(grad_gate, gate_w, ((1,), (1,))) + mm(grad_up, up_w, ((1,), (1,)))
            feed = feed_n if feed is None else feed + feed_n
            back = back_n if back is None else back + back_n
        feed_ref[...] = feed.astype(feed_ref.dtype)
        back_ref[...] = back.astype(back_ref.dtype)

    return call(
        kernel,
        "feed_block",
        (*[shaped(rows, width)] * 3, *[shaped(rows, depth, out_type)] * 2),
        [(info, "s"), (x, "v"), (g, "v")] + [(shard, "h") for shard in shards_a + shards_b],
        [pltpu.VMEM((depth, width), BF)] * 3 + [pltpu.SemaphoreType.DMA((3,))],
    )


def feed_grads(info, lefts, rights, low, high, firsts, whole):
    parts, dp = len(lefts), lax.axis_size("dp")
    depth, width = lefts[0].shape
    share = width // dp
    full = whole[0].shape[1]
    n_whole, n_part = full // TILE, (high - low) // TILE
    half = jax.ShapeDtypeStruct((dp // 2, share, full + high - low), BF)

    def kernel(info_ref, *refs):
        first_refs, whole_refs = refs[:parts], refs[parts : 2 * parts]
        left_refs, right_refs = refs[2 * parts : 3 * parts], refs[3 * parts : 4 * parts]
        keep_ref, send_ref, made = refs[4 * parts :]

        def one(rows, columns):
            total = None
            for row, column in zip(rows, columns):
                term = mm(row[...], column[...], ((0,), (0,)))
                total = term if total is None else total + term
            store_sides(info_ref[3], total, made, 0, keep_ref, send_ref)

        @pl.when(pl.program_id(0) < n_whole)
        def _():
            one(first_refs, whole_refs)

        @pl.when(pl.program_id(0) >= n_whole)
        def _():
            one(left_refs, right_refs)

    def whole_map(f, info_ref):
        return (0, jnp.minimum(f, n_whole - 1))

    def part_map(f, info_ref):
        return (0, low // TILE + jnp.maximum(f - n_whole, 0))

    fixed = pl.BlockSpec((depth, width), lambda f, info_ref: (0, 0))
    return pl.pallas_call(
        kernel,
        out_shape=(half, half),
        grid_spec=pltpu.PrefetchScalarGridSpec(
            num_scalar_prefetch=1,
            grid=(n_whole + n_part,),
            in_specs=[fixed] * parts
            + [pl.BlockSpec((depth, TILE), whole_map)] * parts
            + [fixed] * parts
            + [pl.BlockSpec((depth, TILE), part_map)] * parts,
            out_specs=[pl.BlockSpec((dp // 2, share, TILE), lambda f, info_ref: (0, 0, f))] * 2,
            scratch_shapes=[pltpu.VMEM((dp // 2, 2, share, TILE), BF)],
        ),
        compiler_params=pltpu.CompilerParams(vmem_limit_bytes=VMEM_BYTES),
        cost_estimate=pl.CostEstimate(flops=1, transcendentals=0, bytes_accessed=1),
        name="feed_grads",
    )(info, *firsts, *whole, *lefts, *rights)


class Halving:
    def __init__(self, keep, send, order):
        self.order = order
        self.left = [2**j for j in reversed(range(len(order)))]
        self.sent = swap(send, order[0])
        self.kept = keep
        self.left.remove(order[0])
        self.stage = 1

    def step(self):
        me = lax.axis_index("dp")
        total = (self.kept.astype(F32) + self.sent.astype(F32)).astype(BF)
        bit = self.order[self.stage]
        total = total.reshape((2,) * len(self.left) + total.shape[-2:])
        axis = self.left.index(bit)
        side = (me // bit) % 2
        self.kept = lax.dynamic_index_in_dim(total, side, axis, keepdims=False)
        self.sent = swap(lax.dynamic_index_in_dim(total, 1 - side, axis, keepdims=False), bit)
        self.left.remove(bit)
        self.stage += 1

    def done(self):
        while self.stage < len(self.order):
            self.step()
        return self.kept.astype(F32) + self.sent.astype(F32)


def after(values, *others):
    flat, tree = jax.tree.flatten((values, others))
    return jax.tree.unflatten(tree, lax.optimization_barrier(flat))


def local(
    tokens,
    cotangent,
    lengths,
    rates,
    query_weight,
    query_moment,
    query_average,
    output_weight,
    output_moment,
    output_average,
    gating_weight,
    gating_moment,
    gating_average,
    down_weight,
    down_moment,
    down_average,
    context_weight,
    context_moment,
    context_average,
    gains_weight,
    gains_moment,
    gains_average,
):
    row_count, width = tokens.shape
    dp, mp = lax.axis_size("dp"), lax.axis_size("mp")
    place = lax.axis_index("mp")
    own_count = row_count // mp
    own_start = place * own_count
    share, piece = width // dp, width // (dp * mp)
    forth, back = bit_orders()
    forth_first, back_first = forth[-1:] + forth[:-1], back[-1:] + back[:-1]
    length = lengths[0]
    places = jnp.arange(row_count, dtype=jnp.int32)
    me = lax.axis_index("dp")
    info = jnp.stack([me, own_start, length, me % 2]).astype(jnp.int32)

    def rows_at(tensor, step, count):
        return lax.dynamic_slice_in_dim(tensor, (place ^ step) * count, count, 0)

    gains_split = jnp.stack(split_three(gains_weight)).reshape(1, -1)
    message = jnp.concatenate(
        [
            query_weight.astype(BF),
            output_weight.T.astype(BF),
            context_weight.astype(BF).reshape(2 * piece, HD),
            jnp.pad(gains_split, ((0, 0), (0, HD - gains_split.shape[1]))),
        ],
        axis=0,
    )
    message = jnp.pad(message, ((0, -message.shape[0] % 16), (0, 0)))
    (gating_late, down_late), (message,) = after((gating_weight, down_weight), message)
    parts = [message] + [across_heads(message, k) for k in range(1, mp)]
    query_share = jnp.concatenate([part[:share] for part in parts], axis=1)
    output_share = jnp.concatenate([part[share : 2 * share] for part in parts], axis=1)
    rests = jnp.stack([part[2 * share :] for part in parts])
    rests = [lax.dynamic_index_in_dim(rests, place ^ k, 0, keepdims=False) for k in range(mp)]
    context_share = jnp.concatenate(
        [
            jnp.concatenate(
                [
                    rest[:piece],
                    rest[piece : 2 * piece],
                    jnp.pad(
                        rest[2 * piece, : 6 * piece].reshape(6, piece).T, ((0, 0), (0, LANES - 6))
                    ),
                ],
                axis=1,
            )
            for rest in rests
        ],
        axis=0,
    )

    units = gating_weight.shape[2]
    padded = round_up(units, TILE)
    half = column_cuts(padded)[0]

    def pad_units(tensor):
        return jnp.pad(tensor, ((0, 0), (0, padded - units)))

    gating_low = gating_late.astype(BF)
    down_low = pad_units(down_late.T.astype(BF))
    feed_a = jnp.concatenate([pad_units(gating_low[0]), down_low[:, :half]], axis=1)
    feed_b = jnp.concatenate([pad_units(gating_low[1]), down_low[:, half:]], axis=1)
    contexts = spread_direct(context_share)
    first_a, first_b = swap(feed_a, forth[0]), swap(feed_b, back[0])
    held_q, held_o = [query_share, swap(query_share, forth[0])], [output_share, swap(output_share, back[0])]

    cosine, sine_tab = rotation(row_count, HD)
    tokens_own = rows_at(tokens, 0, own_count)
    tables_own = (rows_at(cosine, 0, own_count), rows_at(sine_tab, 0, own_count))
    (cotangent_too, second_a, second_b), (context_held,) = after(
        (cotangent, feed_a, feed_b), contexts[0][0]
    )
    contexts = [(context_held, contexts[0][1])] + contexts[1:]
    grad_low = jnp.where((places < length)[:, None], cotangent_too, jnp.zeros_like(cotangent))
    grad_blocks = [rows_at(grad_low, k, own_count) for k in range(mp)]
    normed_one, (grad_blocks, tokens_own, tables_own, first_a, first_b) = after(
        contexts[1][0], grad_blocks, tokens_own, tables_own, first_a, first_b
    )
    contexts = [contexts[0], (normed_one, contexts[1][1])]
    contexts = lay(contexts)
    normed, keys, values, gains = project(info, tokens, cosine, sine_tab, contexts)
    normed_own = rows_at(normed, 0, own_count)
    (held_q, held_o), (gains,) = after((held_q, held_o), gains)
    w_queries = spread_on(held_q, forth)
    w_outputs = spread_on(held_o, back)
    (sent_a, sent_b), (w_queries[0], w_outputs[0]) = after(
        (first_a, first_b), w_queries[0], w_outputs[0]
    )
    w_queries, w_outputs = spread_out(w_queries, forth), spread_out(w_outputs, back)
    w_queries, w_outputs = lay(w_queries), lay(w_outputs)
    pieces_a, offsets_a = spread_wide([feed_a, first_a], [second_a, sent_a], forth)
    pieces_b, offsets_b = spread_wide([feed_b, first_b], [second_b, sent_b], back)
    shards_a = spread_last(pieces_a[:2], offsets_a[:2], forth[-1])
    shards_b = spread_last(pieces_b[:2], offsets_b[:2], back[-1])
    normed_own, (shards_a, shards_b) = after(
        normed_own, arrays_of(shards_a), arrays_of(shards_b)
    )
    shards_a = list(zip(shards_a, [offsets_a[:2], [k ^ 1 for k in offsets_a[:2]]]))
    shards_b = list(zip(shards_b, [offsets_b[:2], [k ^ 1 for k in offsets_b[:2]]]))
    queries, mixed, middle, normed_two_own, log_sums = attend(
        info, normed_own, keys, values, tokens_own, tables_own, gains, w_queries, w_outputs
    )

    (pieces_a[2:], pieces_b[2:]), (normed_two_own,) = after(
        (pieces_a[2:], pieces_b[2:]), normed_two_own
    )
    for n in range(2, len(pieces_a), 2):
        shards_a = shards_a + spread_last(pieces_a[n : n + 2], offsets_a[n : n + 2], forth[-1])
        shards_b = shards_b + spread_last(pieces_b[n : n + 2], offsets_b[n : n + 2], back[-1])
    shards_a, shards_b = lay(shards_a), lay(shards_b)
    blocks = [normed_two_own] + [across_heads(normed_two_own, k) for k in range(1, mp)]
    made = []
    for k in range(mp):
        if k > 0:
            blocks[k], (made[k - 1],) = after(blocks[k], made[k - 1])
        made.append(
            feed_block(
                info, blocks[k], grad_blocks[k], shards_a, shards_b, padded, F32 if k == 0 else BF
            )
        )
    hidden, grad_gate, grad_up, feed_parts, back_parts = (
        [made[k][n] for k in range(mp)] for n in range(5)
    )
    back_parts = back_parts[:1] + [across_heads(back_parts[k], k) for k in range(1, mp)]
    def halve(parts):
        rows, bit = parts[0].shape[0], mp // len(parts)
        sent = across_heads(jnp.concatenate(parts[1::2], axis=0), bit)
        return parts[0::2], [sent[k * rows : (k + 1) * rows] for k in range(len(parts) // 2)]

    def summed(kept, sent):
        return [a.astype(F32) + b.astype(F32) for a, b in zip(kept, sent)]

    def to_owner(parts):
        while len(parts) > 1:
            parts = summed(*halve([part.astype(BF) for part in parts]))
        return parts[0]

    keep_b, send_b = feed_grads(info, grad_blocks, hidden, half, padded, blocks, grad_up)
    send_b, (back_parts[:-1],) = after(send_b, back_parts[:-1])
    flow_b = Halving(keep_b, send_b, back_first)
    flow_b.step()
    grad_gate, (flow_b.kept,) = after(grad_gate, flow_b.kept)
    keep_a, send_a = feed_grads(info, grad_blocks, hidden, 0, half, blocks, grad_gate)
    send_a, (back_parts[-1],) = after(send_a, back_parts[-1])
    flow_a = Halving(keep_a, send_a, forth_first)
    flow_a.step()
    feed_parts, (back_parts,) = after(feed_parts, back_parts)
    feed_kept, feed_sent = halve([part.astype(BF) for part in feed_parts])
    back_parts, (flow_a.kept,) = after(back_parts, flow_a.kept)

    grad_middle, middle_low, gain_two, grad_query, grad_context = attend_back(
        info,
        back_parts,
        middle,
        grad_blocks[0],
        gains,
        queries,
        keys,
        values,
        log_sums,
        (cosine, sine_tab, *tables_own),
        w_outputs,
    )

    context_kept, context_sent = halve([rows_at(grad_context, k, own_count) for k in range(mp)])
    grad_query, (flow_b.sent,) = after(grad_query, flow_b.sent)
    w_shards = (w_queries, contexts)
    keep_a, send_a, keep_b, send_b = mixer_grads(
        info, normed, normed_own, grad_query, grad_context, middle_low, mixed, gain_two, w_shards
    )
    (send_a, send_b), (flow_a.sent,) = after((send_a, send_b), flow_a.sent)
    context_sent, (keep_a,) = after(context_sent, keep_a)
    context_own = to_owner(summed(context_kept, context_sent))
    mixer_a, mixer_b = Halving(keep_a, send_a, forth_first), Halving(keep_b, send_b, back_first)
    flow_a.step()
    flow_b.step()
    (mixer_a.sent, mixer_b.sent), (flow_a.kept, flow_b.kept) = after(
        (mixer_a.sent, mixer_b.sent), flow_a.kept, flow_b.kept
    )
    mixer_a.step()
    mixer_b.step()
    context_own, (mixer_a.kept, mixer_b.kept) = after(context_own, mixer_a.kept, mixer_b.kept)
    tokens_grad = finish(info, grad_query, [context_own], grad_middle, tokens_own, gains, w_shards)
    feed_sent, (mixer_a.sent, mixer_b.sent) = after(feed_sent, mixer_a.sent, mixer_b.sent)
    block_out = middle + to_owner(summed(feed_kept, feed_sent))

    feed_one, feed_two = flow_a.done(), flow_b.done()
    mixer_one, mixer_two = mixer_a.done(), mixer_b.done()
    across, halfway = grad_query.shape[1], mp // 2
    shares = [
        (mixer_one if k < halfway else mixer_two)[
            :, (k % halfway) * 2 * HD : (k % halfway + 1) * 2 * HD
        ]
        for k in range(mp)
    ]
    share_context = jnp.concatenate([mixer_one[:, across:], mixer_two[:, across:]], axis=1)
    wide = share_context.shape[1]
    total, sum_context = shares[0], rows_at(share_context, 0, piece)
    for k in range(1, mp):
        total = total + across_heads(shares[k].astype(BF), k).astype(F32)
        sent = across_heads(rows_at(share_context, k, piece).astype(BF), k)
        sum_context = sum_context + sent.astype(F32)
    sum_query, sum_output = total[:, :HD], total[:, HD:].T
    sum_gains = jnp.stack([sum_context[:, HD] / gains_weight[0], sum_context[:, HD + 1]])
    sum_context = jnp.stack([sum_context[:, :HD], sum_context[:, wide - HD :]])
    sum_gating = jnp.stack([feed_one[:, :units], feed_two[:, :units]])
    sum_down = jnp.concatenate([feed_one[:, padded:], feed_two[:, padded:]], axis=1)[:, :units].T

    query_grads, query_moments, query_averages, query_updated = advance(
        sum_query, query_moment, query_average, query_weight, rates[0]
    )
    output_grads, output_moments, output_averages, output_updated = advance(
        sum_output, output_moment, output_average, output_weight, rates[1]
    )
    gating_grads, gating_moments, gating_averages, gating_updated = advance(
        sum_gating, gating_moment, gating_average, gating_weight, rates[2]
    )
    down_grads, down_moments, down_averages, down_updated = advance(
        sum_down, down_moment, down_average, down_weight, rates[3]
    )
    context_grads, context_moments, context_averages, context_updated = advance(
        sum_context, context_moment, context_average, context_weight, rates[4]
    )
    gains_grads, gains_moments, gains_averages, gains_updated = advance(
        sum_gains, gains_moment, gains_average, gains_weight, rates[5]
    )
    return (
        block_out,
        tokens_grad,
        query_grads,
        query_moments,
        query_averages,
        query_updated,
        output_grads,
        output_moments,
        output_averages,
        output_updated,
        gating_grads,
        gating_moments,
        gating_averages,
        gating_updated,
        down_grads,
        down_moments,
        down_averages,
        down_updated,
        context_grads,
        context_moments,
        context_averages,
        context_updated,
        gains_grads,
        gains_moments,
        gains_averages,
        gains_updated,
    )


def solution(mesh):
    return jax.shard_map(
        local,
        mesh=mesh,
        in_specs=(
            P("dp", None),
            P("dp", None),
            P("dp"),
            P(),
            P("dp", "mp"),
            P("dp", "mp"),
            P("dp", "mp"),
            P("mp", "dp"),
            P("mp", "dp"),
            P("mp", "dp"),
            P(None, "dp", "mp"),
            P(None, "dp", "mp"),
            P(None, "dp", "mp"),
            P("mp", "dp"),
            P("mp", "dp"),
            P("mp", "dp"),
            P(None, ("dp", "mp"), None),
            P(None, ("dp", "mp"), None),
            P(None, ("dp", "mp"), None),
            P(None, ("dp", "mp")),
            P(None, ("dp", "mp")),
            P(None, ("dp", "mp")),
        ),
        out_specs=(
            P(("dp", "mp"), None),
            P(("dp", "mp"), None),
            P("dp", "mp"),
            P("dp", "mp"),
            P("dp", "mp"),
            P("dp", "mp"),
            P("mp", "dp"),
            P("mp", "dp"),
            P("mp", "dp"),
            P("mp", "dp"),
            P(None, "dp", "mp"),
            P(None, "dp", "mp"),
            P(None, "dp", "mp"),
            P(None, "dp", "mp"),
            P("mp", "dp"),
            P("mp", "dp"),
            P("mp", "dp"),
            P("mp", "dp"),
            P(None, ("dp", "mp"), None),
            P(None, ("dp", "mp"), None),
            P(None, ("dp", "mp"), None),
            P(None, ("dp", "mp"), None),
            P(None, ("dp", "mp")),
            P(None, ("dp", "mp")),
            P(None, ("dp", "mp")),
            P(None, ("dp", "mp")),
        ),
        check_vma=False,
    )
```

```python
import jax
import jax.numpy as jnp
from jax import lax
from jax.experimental import pallas as pl
from jax.experimental.pallas import tpu as pltpu
from jax.sharding import PartitionSpec as P

HD = 256
LANES = 128
TILE = 256
VMEM_BYTES = 56 * 1024 * 1024
EPSILON = 1e-06
MOMENTUM = 0.9
AVERAGING = 0.5
BF = jnp.bfloat16
F32 = jnp.float32


def mm(a, b, dims):
    return lax.dot_general(a, b, (dims, ((), ())), preferred_element_type=F32)


def inverse_rms(tensor):
    return lax.rsqrt(jnp.mean(tensor * tensor, axis=-1, keepdims=True) + EPSILON)


def norm_back(grad_in, unit, inverse, gain_vec):
    scaled = grad_in * gain_vec
    return inverse * (scaled - unit * jnp.mean(scaled * unit, axis=-1, keepdims=True))


def rotation(length, head_size):
    halfway = head_size // 2
    frequency = 1000000.0 ** (-(jnp.arange(halfway).astype(F32) * 2.0 / head_size))
    angles = jnp.arange(length).astype(F32)[:, None] * frequency[None, :]
    return (jnp.cos(angles), jnp.sin(angles))


def rotate(tensor, cosine, sine_tab):
    halfway = tensor.shape[-1] // 2
    former = tensor[..., :halfway]
    latter = tensor[..., halfway:]
    return jnp.concatenate(
        [former * cosine - latter * sine_tab, latter * cosine + former * sine_tab], axis=-1
    )


def advance(gradient, moment, average, weight, step_rate):
    moment_new = MOMENTUM * moment + gradient
    weight_new = weight - step_rate * (gradient + MOMENTUM * moment_new)
    average_new = AVERAGING * average + (1.0 - AVERAGING) * weight_new
    return (gradient, moment_new, average_new, weight_new)


def swap(tensor, bit):
    count = lax.axis_size("dp")
    return lax.ppermute(tensor, "dp", [(i, i ^ bit) for i in range(count)])


def across_heads(tensor, bit):
    count = lax.axis_size("mp")
    return lax.ppermute(tensor, "mp", [(i, i ^ bit) for i in range(count)])


def bit_orders():
    bits = []
    while 2 ** len(bits) < lax.axis_size("dp"):
        bits.append(2 ** len(bits))
    outer = bits[1:]
    return (outer + bits[:1], outer[::-1] + bits[:1])


def split_three(tensor):
    high = lax.reduce_precision(tensor, 8, 7)
    rest = tensor - high
    middle = lax.reduce_precision(rest, 8, 7)
    return [high.astype(BF), middle.astype(BF), (rest - middle).astype(BF)]


def spread_on(pieces, order):
    held, offsets = jnp.concatenate(pieces, axis=0), [0, order[0]]
    for bit in order[1:-1]:
        held = jnp.concatenate([held, swap(held, bit)], axis=0)
        offsets = offsets + [k ^ bit for k in offsets]
    return [held, offsets]


def spread_out(group, order):
    held, offsets = group
    bit = order[-1]
    return [(held, offsets), (swap(held, bit), [k ^ bit for k in offsets])]


def spread_at_once(tensor):
    count = lax.axis_size("dp")
    groups = [list(range(side, count, 2)) for side in (0, 1)]
    copies = jnp.broadcast_to(tensor[None], (count // 2, *tensor.shape))
    held = lax.all_to_all(copies, "dp", 0, 0, axis_index_groups=groups, tiled=True)
    held = held.reshape(count // 2 * tensor.shape[0], tensor.shape[1])
    return [
        (held, [(j, 0) for j in range(count // 2)]),
        (swap(held, 1), [(j, 1) for j in range(count // 2)]),
    ]


def spread_wide(pieces, own_sent, first_sent, order):
    offsets = [0, order[0], order[1], order[0] ^ order[1]]
    pieces = pieces + [own_sent, swap(first_sent, order[1])]
    for bit in order[2:-1]:
        pieces = pieces + [swap(piece, bit) for piece in pieces]
        offsets = offsets + [k ^ bit for k in offsets]
    return pieces, offsets


def spread_last(pieces, offsets, bit):
    pair = jnp.concatenate(pieces, axis=0)
    return [(pair, offsets), (swap(pair, bit), [k ^ bit for k in offsets])]


def round_up(number, unit):
    return -(-number // unit) * unit


def column_cuts(width):
    half = round_up(width // TILE, 2) // 2 * TILE
    first = round_up(half // TILE, 2) // 2 * TILE
    return half, [(0, first), (first, half), (half, width)]


def device_of(me, offset):
    if isinstance(offset, tuple):
        return 2 * offset[0] + ((me & 1) ^ offset[1])
    return me ^ offset


def lay(groups):
    share = groups[0][0].shape[0] // len(groups[0][1])
    if share % 16 == 0:
        return groups
    me = lax.axis_index("dp")
    count = lax.axis_size("dp")
    whole = jnp.zeros((count * share, groups[0][0].shape[1]), groups[0][0].dtype)
    for array, offsets in groups:
        for n, k in enumerate(offsets):
            part = array[n * share : (n + 1) * share]
            whole = lax.dynamic_update_slice(whole, part, (device_of(me, k) * share, 0))
    return [(whole, [])]


def arrays_of(groups):
    return [array for array, _ in groups]


def offsets_of(groups):
    return [offsets for _, offsets in groups]


def row_copies(me, shards, offsets, low, size, target, column, sem):
    copies = []
    columns, place = pl.ds(low, size), pl.ds(column, size)
    for shard, from_devices in zip(shards, offsets):
        if not from_devices:
            copies.append(
                pltpu.make_async_copy(shard.at[:, columns], target.at[:, place], sem)
            )
        for n, k in enumerate(from_devices):
            share = shard.shape[0] // len(from_devices)
            rows = pl.ds(pl.multiple_of(device_of(me, k) * share, 16), share)
            source = shard.at[pl.ds(n * share, share), columns]
            copies.append(pltpu.make_async_copy(source, target.at[rows, place], sem))
    return copies


def start_all(copies):
    for copy in copies:
        copy.start()


def wait_all(copies):
    for copy in copies:
        copy.wait()


def call(kernel, name, out_shape, operands, scratch):
    spaces = {
        "s": pl.BlockSpec(memory_space=pltpu.SMEM),
        "v": pl.BlockSpec(memory_space=pltpu.VMEM),
        "h": pl.BlockSpec(memory_space=pltpu.HBM),
    }
    return pl.pallas_call(
        kernel,
        out_shape=out_shape,
        in_specs=[spaces[space] for _, space in operands],
        out_specs=tuple(spaces["v"] for _ in out_shape),
        scratch_shapes=scratch,
        compiler_params=pltpu.CompilerParams(vmem_limit_bytes=VMEM_BYTES),
        cost_estimate=pl.CostEstimate(flops=1, transcendentals=0, bytes_accessed=1),
        name=name,
    )(*[array for array, _ in operands])


def shaped(rows, columns, kind=BF):
    return jax.ShapeDtypeStruct((rows, columns), kind)


def project(info, tokens, cosine, sine_tab, contexts):
    rows, width = tokens.shape
    own = rows // lax.axis_size("mp")
    block = min(rows, TILE)
    shards, offsets = arrays_of(contexts), offsets_of(contexts)
    wide = shards[0].shape[1]

    def kernel(info_ref, x_ref, cos_ref, sin_ref, *refs):
        shard_refs, refs = refs[: len(shards)], refs[len(shards) :]
        normed_ref, own_ref, key_ref, value_ref, gain_ref, w_c, sems = refs
        copies = row_copies(info_ref[0], shard_refs, offsets, 0, wide, w_c, 0, sems.at[0])
        start_all(copies)
        wait_all(copies)
        terms = w_c[:, 2 * HD : 2 * HD + LANES].astype(F32).T
        gains = terms[0:2] + terms[2:4] + terms[4:6]
        gain_ref[...] = jnp.concatenate([gains] * 4, axis=0)
        for r in range(0, rows, block):
            span = pl.ds(r, block)
            x = x_ref[span, :].astype(F32)
            normed = (x * inverse_rms(x) * gains[0:1]).astype(BF)
            normed_ref[span, :] = normed
            raw = mm(normed, w_c[:, : 2 * HD], ((1,), (0,)))
            key_ref[span, :] = rotate(raw[:, :HD], cos_ref[span, :], sin_ref[span, :]).astype(BF)
            value_ref[span, :] = raw[:, HD:].astype(BF)
        own_ref[...] = normed_ref[pl.ds(pl.multiple_of(info_ref[1], own), own), :]

    return call(
        kernel,
        "project",
        (
            shaped(rows, width),
            shaped(own, width),
            *[shaped(rows, HD)] * 2,
            shaped(8, width, F32),
        ),
        [(info, "s"), (tokens, "v"), (cosine, "v"), (sine_tab, "v")]
        + [(shard, "h") for shard in shards],
        [pltpu.VMEM((width, wide), BF), pltpu.SemaphoreType.DMA((1,))],
    )


def masked_scores(info_ref, query, keys):
    scores = mm(query, keys, ((1,), (1,))) * 0.0625
    at_row = info_ref[1] + lax.broadcasted_iota(jnp.int32, scores.shape, 0)
    at_key = lax.broadcasted_iota(jnp.int32, scores.shape, 1)
    allowed = (at_key <= at_row) & (at_key < info_ref[2])
    return jnp.where(allowed, scores, -1e30)


def attend(info, normed_own, keys, values, tokens_own, tables, gains, w_queries, w_outputs):
    own, width = tokens_own.shape
    q_shards, q_offsets = arrays_of(w_queries), offsets_of(w_queries)
    o_shards, o_offsets = arrays_of(w_outputs), offsets_of(w_outputs)
    across = q_shards[0].shape[1]

    def kernel(info_ref, own_ref, key_ref, value_ref, x_ref, cos_ref, sin_ref, gain_ref, *refs):
        q_refs, refs = refs[: len(q_shards)], refs[len(q_shards) :]
        o_refs, refs = refs[: len(o_shards)], refs[len(o_shards) :]
        query_ref, mixed_ref, middle_ref, normed_ref, log_ref, w_q, w_o, sems = refs
        copies = row_copies(info_ref[0], q_refs, q_offsets, 0, across, w_q, 0, sems.at[0])
        copies_o = row_copies(info_ref[0], o_refs, o_offsets, 0, across, w_o, 0, sems.at[1])
        start_all(copies)
        start_all(copies_o)
        wait_all(copies)
        keys, values = key_ref[...], value_ref[...]
        raw = mm(own_ref[...], w_q[...], ((1,), (0,)))
        for h in range(across // HD):
            columns = slice(h * HD, (h + 1) * HD)
            query = rotate(raw[:, columns], cos_ref[...], sin_ref[...]).astype(BF)
            query_ref[:, columns] = query
            scores = masked_scores(info_ref, query, keys)
            highest = jnp.max(scores, axis=-1, keepdims=True)
            exped = jnp.exp(scores - highest)
            total = jnp.sum(exped, axis=-1, keepdims=True)
            probs = (exped * (1.0 / total)).astype(BF)
            mixed_ref[:, columns] = mm(probs, values, ((1,), (0,))).astype(BF)
            log_ref[:, h : h + 1] = highest + jnp.log(total)
        wait_all(copies_o)
        middle = x_ref[...].astype(F32) + mm(mixed_ref[...], w_o[...], ((1,), (1,)))
        middle_ref[...] = middle
        normed_ref[...] = (middle * inverse_rms(middle) * gain_ref[1:2, :]).astype(BF)

    return call(
        kernel,
        "attend",
        (
            shaped(own, across),
            shaped(own, across),
            shaped(own, width, F32),
            shaped(own, width),
            shaped(own, LANES, F32),
        ),
        [(info, "s")]
        + [(array, "v") for array in (normed_own, keys, values, tokens_own, *tables, gains)]
        + [(shard, "h") for shard in q_shards + o_shards],
        [pltpu.VMEM((width, across), BF)] * 2 + [pltpu.SemaphoreType.DMA((2,))],
    )


def attend_back(
    info, parts, middle, grad_own, gains, queries, keys, values, log_sums, tables, w_outputs
):
    heads, n_parts = queries.shape[1] // HD, len(parts)
    own, width = middle.shape
    rows = keys.shape[0]
    output_shards, offsets = arrays_of(w_outputs), offsets_of(w_outputs)
    count = len(output_shards)

    def kernel(info_ref, *refs):
        part_refs, refs = refs[:n_parts], refs[n_parts:]
        middle_ref, grad_ref, gain_ref = refs[:3]
        query_ref, refs = refs[3], refs[4:]
        key_ref, value_ref, log_ref, cos_ref, sin_ref, cos_own, sin_own = refs[:7]
        shards, refs = refs[7 : 7 + count], refs[7 + count :]
        grad_middle_ref, low_ref, gain_two_ref, query_out, context_out, w_o, sem = refs
        copies = row_copies(info_ref[0], shards, offsets, 0, heads * HD, w_o, 0, sem.at[0])
        start_all(copies)
        grad_in = part_refs[0][...]
        for part_ref in part_refs[1:]:
            grad_in = grad_in + part_ref[...].astype(F32)
        middle = middle_ref[...]
        inverse = inverse_rms(middle)
        unit = middle * inverse
        gain_two = jnp.sum(grad_in * unit, axis=0, keepdims=True)
        gain_two_ref[...] = jnp.broadcast_to(gain_two, gain_two_ref.shape)
        grad_middle = grad_ref[...].astype(F32) + norm_back(
            grad_in, unit, inverse, gain_ref[1:2, :]
        )
        grad_middle_ref[...] = grad_middle
        low = grad_middle.astype(BF)
        low_ref[...] = low
        wait_all(copies)
        keys, values = key_ref[...], value_ref[...]
        grad_mixed = mm(low, w_o[...], ((1,), (0,))).astype(BF)
        grad_keys = grad_values = None
        for h in range(heads):
            query = query_ref[:, h * HD : (h + 1) * HD]
            scores = masked_scores(info_ref, query, keys)
            probs = jnp.exp(scores - log_ref[:, h : h + 1])
            grad_head = grad_mixed[:, h * HD : (h + 1) * HD]
            grad_probs = mm(grad_head, values, ((1,), (1,)))
            inner = jnp.sum(probs * grad_probs, axis=-1, keepdims=True)
            grad_scores = (probs * (grad_probs - inner)).astype(BF)
            turned = mm(grad_scores, keys, ((1,), (0,))) * 0.0625
            query_out[:, h * HD : (h + 1) * HD] = rotate(
                turned, cos_own[...], -sin_own[...]
            ).astype(BF)
            term_keys = mm(grad_scores, query, ((0,), (0,)))
            term_values = mm(probs.astype(BF), grad_head, ((0,), (0,)))
            grad_keys = term_keys if h == 0 else grad_keys + term_keys
            grad_values = term_values if h == 0 else grad_values + term_values
        context_out[:, :HD] = rotate(grad_keys * 0.0625, cos_ref[...], -sin_ref[...]).astype(BF)
        context_out[:, HD:] = grad_values.astype(BF)

    return call(
        kernel,
        "attend_back",
        (
            shaped(own, width, F32),
            shaped(own, width),
            shaped(8, width, F32),
            shaped(own, heads * HD),
            shaped(rows, 2 * HD),
        ),
        [(info, "s")]
        + [(part, "v") for part in parts]
        + [(middle, "v"), (grad_own, "v"), (gains, "v"), (queries, "v")]
        + [(array, "v") for array in (keys, values, log_sums, *tables)]
        + [(shard, "h") for shard in output_shards],
        [pltpu.VMEM((width, heads * HD), BF), pltpu.SemaphoreType.DMA((1,))],
    )


def store_sides(side, value, made, column, keep_ref, send_ref):
    blocks, share, _ = keep_ref.shape
    size = value.shape[1]
    for b in range(2 * blocks):
        made[b // 2, b % 2, :, :size] = value[b * share : (b + 1) * share].astype(BF)
    for b in range(blocks):
        keep_ref[b, :, column : column + size] = made[b, side, :, :size]
        send_ref[b, :, column : column + size] = made[b, 1 - side, :, :size]


def mixer_grads(
    info, normed, normed_own, grad_query, grad_context, low, mixed, gain_two, w_shards
):
    query_shards, context_shards = (arrays_of(groups) for groups in w_shards)
    offsets_q, offsets_c = (offsets_of(groups) for groups in w_shards)
    width = normed.shape[1]
    dp = lax.axis_size("dp")
    share = width // dp
    across = grad_query.shape[1]
    count = len(query_shards)
    first = jax.ShapeDtypeStruct((dp // 2, share, across + HD + LANES), BF)
    second = jax.ShapeDtypeStruct((dp // 2, share, across + HD), BF)

    def kernel(info_ref, *refs):
        normed_ref, own_ref, query_ref, context_ref, low_ref, mixed_ref, gain_ref = refs[:7]
        queries, contexts = refs[7 : 7 + count], refs[7 + count : 7 + 2 * count]
        keep_a, send_a, keep_b, send_b, w_q, w_c, made, sems = refs[7 + 2 * count :]
        side = info_ref[3]
        copies = row_copies(info_ref[0], queries, offsets_q, 0, across, w_q, 0, sems.at[0])
        copies_c = row_copies(info_ref[0], contexts, offsets_c, 0, 2 * HD, w_c, 0, sems.at[1])
        start_all(copies)
        start_all(copies_c)
        d_output = mm(low_ref[...], mixed_ref[...], ((0,), (0,)))
        halfway = across // HD // 2
        for h in range(across // HD):
            keep, send = (keep_a, send_a) if h < halfway else (keep_b, send_b)
            at = (2 * (h % halfway) + 1) * HD
            store_sides(side, d_output[:, h * HD : (h + 1) * HD], made, at, keep, send)
        d_query = mm(own_ref[...], query_ref[...], ((0,), (0,)))
        for h in range(across // HD):
            keep, send = (keep_a, send_a) if h < halfway else (keep_b, send_b)
            at = 2 * (h % halfway) * HD
            store_sides(side, d_query[:, h * HD : (h + 1) * HD], made, at, keep, send)
        d_context = mm(normed_ref[...], context_ref[...], ((0,), (0,)))
        store_sides(side, d_context[:, :HD], made, across, keep_a, send_a)
        store_sides(side, d_context[:, HD:], made, across, keep_b, send_b)
        wait_all(copies)
        wait_all(copies_c)
        gain_one = jnp.sum(d_query * w_q[...].astype(F32), axis=1, keepdims=True) + jnp.sum(
            d_context * w_c[...].astype(F32), axis=1, keepdims=True
        )
        second_gain = gain_ref[...].T
        lane = lax.broadcasted_iota(jnp.int32, (width, LANES), 1)
        both = jnp.where(lane == 0, gain_one, jnp.where(lane == 1, second_gain[:, 0:1], 0.0))
        store_sides(side, both, made, across + HD, keep_a, send_a)

    return call(
        kernel,
        "mixer_grads",
        (first, first, second, second),
        [(info, "s")]
        + [
            (array, "v")
            for array in (normed, normed_own, grad_query, grad_context, low, mixed, gain_two)
        ]
        + [(shard, "h") for shard in query_shards + context_shards],
        [
            pltpu.VMEM((width, across), BF),
            pltpu.VMEM((width, 2 * HD), BF),
            pltpu.VMEM((dp // 2, 2, share, across), BF),
            pltpu.SemaphoreType.DMA((2,)),
        ],
    )


def finish(info, grad_query, parts, grad_middle, tokens_own, gains, w_shards):
    query_shards, context_shards = (arrays_of(groups) for groups in w_shards)
    offsets_q, offsets_c = (offsets_of(groups) for groups in w_shards)
    own, width = grad_middle.shape
    across = grad_query.shape[1]
    count, n_parts = len(query_shards), len(parts)

    def kernel(info_ref, query_ref, *refs):
        part_refs, refs = refs[:n_parts], refs[n_parts:]
        middle_ref, x_ref, gain_ref = refs[:3]
        queries, contexts = refs[3 : 3 + count], refs[3 + count : 3 + 2 * count]
        out_ref, w_q, w_c, sems = refs[3 + 2 * count :]
        copies = row_copies(info_ref[0], queries, offsets_q, 0, across, w_q, 0, sems.at[0])
        copies_c = row_copies(info_ref[0], contexts, offsets_c, 0, 2 * HD, w_c, 0, sems.at[1])
        start_all(copies)
        start_all(copies_c)
        total = part_refs[0][...].astype(F32)
        for part_ref in part_refs[1:]:
            total = total + part_ref[...].astype(F32)
        x = x_ref[...].astype(F32)
        inverse = inverse_rms(x)
        wait_all(copies)
        wait_all(copies_c)
        grad_in = mm(query_ref[...], w_q[...], ((1,), (1,))) + mm(
            total.astype(BF), w_c[...], ((1,), (1,))
        )
        out_ref[...] = middle_ref[...] + norm_back(grad_in, x * inverse, inverse, gain_ref[0:1, :])

    return call(
        kernel,
        "finish",
        (shaped(own, width, F32),),
        [(info, "s"), (grad_query, "v")]
        + [(part, "v") for part in parts]
        + [(grad_middle, "v"), (tokens_own, "v"), (gains, "v")]
        + [(shard, "h") for shard in query_shards + context_shards],
        [
            pltpu.VMEM((width, across), BF),
            pltpu.VMEM((width, 2 * HD), BF),
            pltpu.SemaphoreType.DMA((2,)),
        ],
    )[0]


def feed_block(info, x, g, groups_a, groups_b, width, out_type):
    rows, depth = x.shape
    shards_a, shards_b = arrays_of(groups_a), arrays_of(groups_b)
    offsets, offsets_b = offsets_of(groups_a), offsets_of(groups_b)
    count = len(shards_a)
    half, cuts = column_cuts(width)

    def kernel(info_ref, x_ref, g_ref, *refs):
        first, second = refs[:count], refs[count : 2 * count]
        hid_ref, gate_ref, up_ref, feed_ref, back_ref = refs[2 * count : 2 * count + 5]
        w_gate, w_up, w_down, sems = refs[2 * count + 5 :]
        copies = []
        for n, (low, high) in enumerate(cuts):
            size = high - low
            source, at = (first, width + low) if high <= half else (second, width + low - half)
            group = []
            for shards, start, target in (
                (first, low, w_gate),
                (second, low, w_up),
                (source, at, w_down),
            ):
                own_offsets = offsets_b if shards is second else offsets
                group += row_copies(
                    info_ref[0], shards, own_offsets, start, size, target, low, sems.at[n]
                )
            copies.append(group)
            start_all(group)
        scale = 0.7978845608028654
        feed = back = None
        for n, (low, high) in enumerate(cuts):
            wait_all(copies[n])
            x, g = x_ref[...], g_ref[...]
            gate_w, up_w, down_w = w_gate[:, low:high], w_up[:, low:high], w_down[:, low:high]
            gate = mm(x, gate_w, ((1,), (0,)))
            up = mm(x, up_w, ((1,), (0,)))
            grad = mm(g, down_w, ((1,), (0,)))
            square = gate * gate
            tanh = jnp.tanh(scale * gate * (1.0 + 0.044715 * square))
            right = 0.5 * (1.0 + tanh)
            gelu = gate * right
            slope = right + gelu * (1.0 - tanh) * scale * (1.0 + 3 * 0.044715 * square)
            hidden = (gelu * up).astype(BF)
            grad_gate = (grad * up * slope).astype(BF)
            grad_up = (grad * gelu).astype(BF)
            hid_ref[:, low:high] = hidden
            gate_ref[:, low:high] = grad_gate
            up_ref[:, low:high] = grad_up
            feed_n = mm(hidden, down_w, ((1,), (1,)))
            back_n = mm(grad_gate, gate_w, ((1,), (1,))) + mm(grad_up, up_w, ((1,), (1,)))
            feed = feed_n if feed is None else feed + feed_n
            back = back_n if back is None else back + back_n
        feed_ref[...] = feed.astype(feed_ref.dtype)
        back_ref[...] = back.astype(back_ref.dtype)

    return call(
        kernel,
        "feed_block",
        (*[shaped(rows, width)] * 3, *[shaped(rows, depth, out_type)] * 2),
        [(info, "s"), (x, "v"), (g, "v")] + [(shard, "h") for shard in shards_a + shards_b],
        [pltpu.VMEM((depth, width), BF)] * 3 + [pltpu.SemaphoreType.DMA((3,))],
    )


def feed_grads(info, lefts, rights, low, high, firsts, whole):
    parts, dp = len(lefts), lax.axis_size("dp")
    depth, width = lefts[0].shape
    share = width // dp
    full = whole[0].shape[1]
    n_whole, n_part = full // TILE, (high - low) // TILE
    half = jax.ShapeDtypeStruct((dp // 2, share, full + high - low), BF)

    def kernel(info_ref, *refs):
        first_refs, whole_refs = refs[:parts], refs[parts : 2 * parts]
        left_refs, right_refs = refs[2 * parts : 3 * parts], refs[3 * parts : 4 * parts]
        keep_ref, send_ref, made = refs[4 * parts :]

        def one(rows, columns):
            total = None
            for row, column in zip(rows, columns):
                term = mm(row[...], column[...], ((0,), (0,)))
                total = term if total is None else total + term
            store_sides(info_ref[3], total, made, 0, keep_ref, send_ref)

        @pl.when(pl.program_id(0) < n_whole)
        def _():
            one(first_refs, whole_refs)

        @pl.when(pl.program_id(0) >= n_whole)
        def _():
            one(left_refs, right_refs)

    def whole_map(f, info_ref):
        return (0, jnp.minimum(f, n_whole - 1))

    def part_map(f, info_ref):
        return (0, low // TILE + jnp.maximum(f - n_whole, 0))

    fixed = pl.BlockSpec((depth, width), lambda f, info_ref: (0, 0))
    return pl.pallas_call(
        kernel,
        out_shape=(half, half),
        grid_spec=pltpu.PrefetchScalarGridSpec(
            num_scalar_prefetch=1,
            grid=(n_whole + n_part,),
            in_specs=[fixed] * parts
            + [pl.BlockSpec((depth, TILE), whole_map)] * parts
            + [fixed] * parts
            + [pl.BlockSpec((depth, TILE), part_map)] * parts,
            out_specs=[pl.BlockSpec((dp // 2, share, TILE), lambda f, info_ref: (0, 0, f))] * 2,
            scratch_shapes=[pltpu.VMEM((dp // 2, 2, share, TILE), BF)],
        ),
        compiler_params=pltpu.CompilerParams(vmem_limit_bytes=VMEM_BYTES),
        cost_estimate=pl.CostEstimate(flops=1, transcendentals=0, bytes_accessed=1),
        name="feed_grads",
    )(info, *firsts, *whole, *lefts, *rights)


class Halving:
    def __init__(self, keep, send, order):
        self.order = order
        self.left = [2**j for j in reversed(range(len(order)))]
        self.sent = swap(send, order[0])
        self.kept = keep
        self.left.remove(order[0])
        self.stage = 1

    def step(self):
        me = lax.axis_index("dp")
        total = (self.kept.astype(F32) + self.sent.astype(F32)).astype(BF)
        bit = self.order[self.stage]
        total = total.reshape((2,) * len(self.left) + total.shape[-2:])
        axis = self.left.index(bit)
        side = (me // bit) % 2
        self.kept = lax.dynamic_index_in_dim(total, side, axis, keepdims=False)
        self.sent = swap(lax.dynamic_index_in_dim(total, 1 - side, axis, keepdims=False), bit)
        self.left.remove(bit)
        self.stage += 1

    def done(self):
        while self.stage < len(self.order):
            self.step()
        return self.kept.astype(F32) + self.sent.astype(F32)


def after(values, *others):
    flat, tree = jax.tree.flatten((values, others))
    return jax.tree.unflatten(tree, lax.optimization_barrier(flat))


def local(
    tokens,
    cotangent,
    lengths,
    rates,
    query_weight,
    query_moment,
    query_average,
    output_weight,
    output_moment,
    output_average,
    gating_weight,
    gating_moment,
    gating_average,
    down_weight,
    down_moment,
    down_average,
    context_weight,
    context_moment,
    context_average,
    gains_weight,
    gains_moment,
    gains_average,
):
    row_count, width = tokens.shape
    dp, mp = lax.axis_size("dp"), lax.axis_size("mp")
    place = lax.axis_index("mp")
    own_count = row_count // mp
    own_start = place * own_count
    share, piece = width // dp, width // (dp * mp)
    forth, back = bit_orders()
    forth_first, back_first = forth[-1:] + forth[:-1], back[-1:] + back[:-1]
    length = lengths[0]
    places = jnp.arange(row_count, dtype=jnp.int32)
    me = lax.axis_index("dp")
    info = jnp.stack([me, own_start, length, me % 2]).astype(jnp.int32)

    def rows_at(tensor, step, count):
        return lax.dynamic_slice_in_dim(tensor, (place ^ step) * count, count, 0)

    gains_split = jnp.stack(split_three(gains_weight)).reshape(1, -1)
    message = jnp.concatenate(
        [
            query_weight.astype(BF),
            output_weight.T.astype(BF),
            context_weight.astype(BF).reshape(2 * piece, HD),
            jnp.pad(gains_split, ((0, 0), (0, HD - gains_split.shape[1]))),
        ],
        axis=0,
    )
    message = jnp.pad(message, ((0, -message.shape[0] % 16), (0, 0)))
    copies = jnp.broadcast_to(message[None], (mp, *message.shape))
    line = lax.all_to_all(copies, "mp", 0, 0, tiled=True)
    parts = [lax.dynamic_index_in_dim(line, place ^ k, 0, keepdims=False) for k in range(mp)]
    query_share = jnp.concatenate([part[:share] for part in parts], axis=1)
    output_share = jnp.concatenate([part[share : 2 * share] for part in parts], axis=1)
    rests = [line[k, 2 * share :] for k in range(mp)]
    context_share = jnp.concatenate(
        [
            jnp.concatenate(
                [
                    rest[:piece],
                    rest[piece : 2 * piece],
                    jnp.pad(
                        rest[2 * piece, : 6 * piece].reshape(6, piece).T, ((0, 0), (0, LANES - 6))
                    ),
                ],
                axis=1,
            )
            for rest in rests
        ],
        axis=0,
    )

    units = gating_weight.shape[2]
    padded = round_up(units, TILE)
    half = column_cuts(padded)[0]

    def pad_units(tensor):
        return jnp.pad(tensor, ((0, 0), (0, padded - units)))

    gating_low = gating_weight.astype(BF)
    down_low = pad_units(down_weight.T.astype(BF))
    feed_a = jnp.concatenate([pad_units(gating_low[0]), down_low[:, :half]], axis=1)
    feed_b = jnp.concatenate([pad_units(gating_low[1]), down_low[:, half:]], axis=1)
    contexts = spread_at_once(context_share)
    first_a, first_b = swap(feed_a, forth[0]), swap(feed_b, back[0])
    held_q, held_o = [query_share, swap(query_share, forth[0])], [output_share, swap(output_share, back[0])]

    cosine, sine_tab = rotation(row_count, HD)
    tokens_own = rows_at(tokens, 0, own_count)
    tables_own = (rows_at(cosine, 0, own_count), rows_at(sine_tab, 0, own_count))
    own_a, own_b = swap(feed_a, forth[1]), swap(feed_b, back[1])
    context_near, (first_a, first_b, own_a, own_b, tokens_own, tables_own) = after(
        contexts[1][0], first_a, first_b, own_a, own_b, tokens_own, tables_own
    )
    contexts = [contexts[0], (context_near, contexts[1][1])]
    contexts = lay(contexts)
    normed, normed_own, keys, values, gains = project(info, tokens, cosine, sine_tab, contexts)
    (held_q, held_o, cotangent_too), (gains,) = after((held_q, held_o, cotangent), gains)
    grad_low = jnp.where((places < length)[:, None], cotangent_too, jnp.zeros_like(cotangent))
    grad_blocks = [rows_at(grad_low, k, own_count) for k in range(mp)]
    w_queries = spread_on(held_q, forth)
    w_outputs = spread_on(held_o, back)
    (sent_a, sent_b), (w_queries[0], w_outputs[0]) = after(
        (first_a, first_b), w_queries[0], w_outputs[0]
    )
    w_queries, w_outputs = spread_out(w_queries, forth), spread_out(w_outputs, back)
    w_queries, w_outputs = lay(w_queries), lay(w_outputs)
    pieces_a, offsets_a = spread_wide([feed_a, first_a], own_a, sent_a, forth)
    pieces_b, offsets_b = spread_wide([feed_b, first_b], own_b, sent_b, back)
    shards_a = spread_last(pieces_a[:2], offsets_a[:2], forth[-1])
    shards_b = spread_last(pieces_b[:2], offsets_b[:2], back[-1])
    normed_own, (shards_a, shards_b, grad_blocks) = after(
        normed_own, arrays_of(shards_a), arrays_of(shards_b), grad_blocks
    )
    shards_a = list(zip(shards_a, [offsets_a[:2], [k ^ 1 for k in offsets_a[:2]]]))
    shards_b = list(zip(shards_b, [offsets_b[:2], [k ^ 1 for k in offsets_b[:2]]]))
    queries, mixed, middle, normed_two_own, log_sums = attend(
        info, normed_own, keys, values, tokens_own, tables_own, gains, w_queries, w_outputs
    )

    (pieces_a[2:], pieces_b[2:]), (normed_two_own,) = after(
        (pieces_a[2:], pieces_b[2:]), normed_two_own
    )
    for n in range(2, len(pieces_a), 2):
        shards_a = shards_a + spread_last(pieces_a[n : n + 2], offsets_a[n : n + 2], forth[-1])
        shards_b = shards_b + spread_last(pieces_b[n : n + 2], offsets_b[n : n + 2], back[-1])
    shards_a, shards_b = lay(shards_a), lay(shards_b)
    blocks = [normed_two_own] + [across_heads(normed_two_own, k) for k in range(1, mp)]
    made = []
    for k in range(mp):
        if k > 0:
            blocks[k], (made[k - 1],) = after(blocks[k], made[k - 1])
        made.append(
            feed_block(
                info, blocks[k], grad_blocks[k], shards_a, shards_b, padded, F32 if k == 0 else BF
            )
        )
    hidden, grad_gate, grad_up, feed_parts, back_parts = (
        [made[k][n] for k in range(mp)] for n in range(5)
    )
    back_parts = back_parts[:1] + [across_heads(back_parts[k], k) for k in range(1, mp)]
    keep_b, send_b = feed_grads(info, grad_blocks, hidden, half, padded, blocks, grad_up)
    grad_gate, (keep_b,) = after(grad_gate, keep_b)
    keep_a, send_a = feed_grads(info, grad_blocks, hidden, 0, half, blocks, grad_gate)
    (send_a, send_b), (back_parts,) = after((send_a, send_b), back_parts)
    flow_a, flow_b = Halving(keep_a, send_a, forth_first), Halving(keep_b, send_b, back_first)
    flow_a.step()
    flow_b.step()
    feed_parts, (back_parts,) = after(feed_parts, back_parts)
    feed_line = jnp.stack([part.astype(BF) for part in feed_parts])
    feed_line = jnp.stack(
        [lax.dynamic_index_in_dim(feed_line, place ^ k, 0, keepdims=False) for k in range(mp)]
    )
    feed_line = lax.all_to_all(feed_line, "mp", 0, 0, tiled=True)
    back_parts, (flow_a.kept, flow_b.kept) = after(back_parts, flow_a.kept, flow_b.kept)

    grad_middle, middle_low, gain_two, grad_query, grad_context = attend_back(
        info,
        back_parts,
        middle,
        grad_blocks[0],
        gains,
        queries,
        keys,
        values,
        log_sums,
        (cosine, sine_tab, *tables_own),
        w_outputs,
    )

    context_line, (feed_line,) = after(grad_context, feed_line)
    context_line = context_line.reshape(mp, own_count, 2 * HD)
    context_line = lax.all_to_all(context_line, "mp", 0, 0, tiled=True)
    w_shards = (w_queries, contexts)
    keep_a, send_a, keep_b, send_b = mixer_grads(
        info, normed, normed_own, grad_query, grad_context, middle_low, mixed, gain_two, w_shards
    )
    (send_a, send_b), (flow_a.sent, flow_b.sent) = after((send_a, send_b), flow_a.sent, flow_b.sent)
    mixer_a, mixer_b = Halving(keep_a, send_a, forth_first), Halving(keep_b, send_b, back_first)
    flow_a.step()
    flow_b.step()
    (mixer_a.sent, mixer_b.sent), (flow_a.kept, flow_b.kept) = after(
        (mixer_a.sent, mixer_b.sent), flow_a.kept, flow_b.kept
    )
    mixer_a.step()
    mixer_b.step()
    (flow_a.sent, flow_b.sent), (mixer_a.kept, mixer_b.kept) = after(
        (flow_a.sent, flow_b.sent), mixer_a.kept, mixer_b.kept
    )
    feed_one, feed_two = flow_a.done(), flow_b.done()
    mixer_a.step()
    mixer_b.step()
    (context_line, feed_line), (mixer_a.kept, mixer_b.kept) = after(
        (context_line, feed_line), mixer_a.kept, mixer_b.kept
    )
    context_own = jnp.sum(context_line.astype(F32), axis=0)
    tokens_grad = finish(info, grad_query, [context_own], grad_middle, tokens_own, gains, w_shards)
    block_out = middle + jnp.sum(feed_line.astype(F32), axis=0)

    mixer_one, mixer_two = mixer_a.done(), mixer_b.done()
    across, halfway = grad_query.shape[1], mp // 2
    shares = [
        (mixer_one if k < halfway else mixer_two)[
            :, (k % halfway) * 2 * HD : (k % halfway + 1) * 2 * HD
        ]
        for k in range(mp)
    ]
    share_context = jnp.concatenate([mixer_one[:, across:], mixer_two[:, across:]], axis=1)
    wide = share_context.shape[1]
    total, sum_context = shares[0], rows_at(share_context, 0, piece)
    for k in range(1, mp):
        total = total + across_heads(shares[k].astype(BF), k).astype(F32)
        sent = across_heads(rows_at(share_context, k, piece).astype(BF), k)
        sum_context = sum_context + sent.astype(F32)
    sum_query, sum_output = total[:, :HD], total[:, HD:].T
    sum_gains = jnp.stack([sum_context[:, HD] / gains_weight[0], sum_context[:, HD + 1]])
    sum_context = jnp.stack([sum_context[:, :HD], sum_context[:, wide - HD :]])
    sum_gating = jnp.stack([feed_one[:, :units], feed_two[:, :units]])
    sum_down = jnp.concatenate([feed_one[:, padded:], feed_two[:, padded:]], axis=1)[:, :units].T

    query_grads, query_moments, query_averages, query_updated = advance(
        sum_query, query_moment, query_average, query_weight, rates[0]
    )
    output_grads, output_moments, output_averages, output_updated = advance(
        sum_output, output_moment, output_average, output_weight, rates[1]
    )
    gating_grads, gating_moments, gating_averages, gating_updated = advance(
        sum_gating, gating_moment, gating_average, gating_weight, rates[2]
    )
    down_grads, down_moments, down_averages, down_updated = advance(
        sum_down, down_moment, down_average, down_weight, rates[3]
    )
    context_grads, context_moments, context_averages, context_updated = advance(
        sum_context, context_moment, context_average, context_weight, rates[4]
    )
    gains_grads, gains_moments, gains_averages, gains_updated = advance(
        sum_gains, gains_moment, gains_average, gains_weight, rates[5]
    )
    return (
        block_out,
        tokens_grad,
        query_grads,
        query_moments,
        query_averages,
        query_updated,
        output_grads,
        output_moments,
        output_averages,
        output_updated,
        gating_grads,
        gating_moments,
        gating_averages,
        gating_updated,
        down_grads,
        down_moments,
        down_averages,
        down_updated,
        context_grads,
        context_moments,
        context_averages,
        context_updated,
        gains_grads,
        gains_moments,
        gains_averages,
        gains_updated,
    )


def solution(mesh):
    return jax.shard_map(
        local,
        mesh=mesh,
        in_specs=(
            P("dp", None),
            P("dp", None),
            P("dp"),
            P(),
            P("dp", "mp"),
            P("dp", "mp"),
            P("dp", "mp"),
            P("mp", "dp"),
            P("mp", "dp"),
            P("mp", "dp"),
            P(None, "dp", "mp"),
            P(None, "dp", "mp"),
            P(None, "dp", "mp"),
            P("mp", "dp"),
            P("mp", "dp"),
            P("mp", "dp"),
            P(None, ("dp", "mp"), None),
            P(None, ("dp", "mp"), None),
            P(None, ("dp", "mp"), None),
            P(None, ("dp", "mp")),
            P(None, ("dp", "mp")),
            P(None, ("dp", "mp")),
        ),
        out_specs=(
            P(("dp", "mp"), None),
            P(("dp", "mp"), None),
            P("dp", "mp"),
            P("dp", "mp"),
            P("dp", "mp"),
            P("dp", "mp"),
            P("mp", "dp"),
            P("mp", "dp"),
            P("mp", "dp"),
            P("mp", "dp"),
            P(None, "dp", "mp"),
            P(None, "dp", "mp"),
            P(None, "dp", "mp"),
            P(None, "dp", "mp"),
            P("mp", "dp"),
            P("mp", "dp"),
            P("mp", "dp"),
            P("mp", "dp"),
            P(None, ("dp", "mp"), None),
            P(None, ("dp", "mp"), None),
            P(None, ("dp", "mp"), None),
            P(None, ("dp", "mp"), None),
            P(None, ("dp", "mp")),
            P(None, ("dp", "mp")),
            P(None, ("dp", "mp")),
            P(None, ("dp", "mp")),
        ),
        check_vma=False,
    )
```

```python
import jax
import jax.numpy as jnp
from jax import lax
from jax.experimental import pallas as pl
from jax.experimental.pallas import tpu as pltpu
from jax.sharding import PartitionSpec as P

HD = 256
LANES = 128
TILE = 256
VMEM_BYTES = 56 * 1024 * 1024
EPSILON = 1e-06
MOMENTUM = 0.9
AVERAGING = 0.5
BF = jnp.bfloat16
F32 = jnp.float32


def mm(a, b, dims):
    return lax.dot_general(a, b, (dims, ((), ())), preferred_element_type=F32)


def inverse_rms(tensor):
    return lax.rsqrt(jnp.mean(tensor * tensor, axis=-1, keepdims=True) + EPSILON)


def norm_back(grad_in, unit, inverse, gain_vec):
    scaled = grad_in * gain_vec
    return inverse * (scaled - unit * jnp.mean(scaled * unit, axis=-1, keepdims=True))


def rotation(length, head_size):
    halfway = head_size // 2
    frequency = 1000000.0 ** (-(jnp.arange(halfway).astype(F32) * 2.0 / head_size))
    angles = jnp.arange(length).astype(F32)[:, None] * frequency[None, :]
    return (jnp.cos(angles), jnp.sin(angles))


def rotate(tensor, cosine, sine_tab):
    halfway = tensor.shape[-1] // 2
    former = tensor[..., :halfway]
    latter = tensor[..., halfway:]
    return jnp.concatenate(
        [former * cosine - latter * sine_tab, latter * cosine + former * sine_tab], axis=-1
    )


def advance(gradient, moment, average, weight, step_rate):
    moment_new = MOMENTUM * moment + gradient
    weight_new = weight - step_rate * (gradient + MOMENTUM * moment_new)
    average_new = AVERAGING * average + (1.0 - AVERAGING) * weight_new
    return (gradient, moment_new, average_new, weight_new)


def swap(tensor, bit):
    count = lax.axis_size("dp")
    return lax.ppermute(tensor, "dp", [(i, i ^ bit) for i in range(count)])


def across_heads(tensor, bit):
    count = lax.axis_size("mp")
    return lax.ppermute(tensor, "mp", [(i, i ^ bit) for i in range(count)])


def bit_orders():
    bits = []
    while 2 ** len(bits) < lax.axis_size("dp"):
        bits.append(2 ** len(bits))
    outer = bits[1:]
    return (outer + bits[:1], outer[::-1] + bits[:1])


def split_three(tensor):
    high = lax.reduce_precision(tensor, 8, 7)
    rest = tensor - high
    middle = lax.reduce_precision(rest, 8, 7)
    return [high.astype(BF), middle.astype(BF), (rest - middle).astype(BF)]


def spread_on(pieces, order):
    held, offsets = jnp.concatenate(pieces, axis=0), [0, order[0]]
    for bit in order[1:-1]:
        held = jnp.concatenate([held, swap(held, bit)], axis=0)
        offsets = offsets + [k ^ bit for k in offsets]
    return [held, offsets]


def spread_out(group, order):
    held, offsets = group
    bit = order[-1]
    return [(held, offsets), (swap(held, bit), [k ^ bit for k in offsets])]


def spread_at_once(tensor, early):
    count = lax.axis_size("dp")
    groups = [list(range(side, count, 2)) for side in (0, 1)]
    copies = jnp.broadcast_to(tensor[None], (count // 2, *tensor.shape))
    held = lax.all_to_all(copies, "dp", 0, 0, axis_index_groups=groups, tiled=True)
    held = held.reshape(count // 2 * tensor.shape[0], tensor.shape[1])
    held, early = after(held, *early)
    return early, [
        (held, [(j, 0) for j in range(count // 2)]),
        (swap(held, 1), [(j, 1) for j in range(count // 2)]),
    ]


def spread_wide(pieces, own_sent, first_sent, order):
    offsets = [0, order[0], order[1], order[0] ^ order[1]]
    pieces = pieces + [own_sent, swap(first_sent, order[1])]
    for bit in order[2:-1]:
        pieces = pieces + [swap(piece, bit) for piece in pieces]
        offsets = offsets + [k ^ bit for k in offsets]
    return pieces, offsets


def spread_last(pieces, offsets, bit):
    pair = jnp.concatenate(pieces, axis=0)
    return [(pair, offsets), (swap(pair, bit), [k ^ bit for k in offsets])]


def round_up(number, unit):
    return -(-number // unit) * unit


def column_cuts(width):
    half = round_up(width // TILE, 2) // 2 * TILE
    first = round_up(half // TILE, 2) // 2 * TILE
    return half, [(0, first), (first, half), (half, width)]


def device_of(me, offset):
    if isinstance(offset, tuple):
        return 2 * offset[0] + ((me & 1) ^ offset[1])
    return me ^ offset


def lay(groups):
    share = groups[0][0].shape[0] // len(groups[0][1])
    if share % 16 == 0:
        return groups
    me = lax.axis_index("dp")
    count = lax.axis_size("dp")
    whole = jnp.zeros((count * share, groups[0][0].shape[1]), groups[0][0].dtype)
    for array, offsets in groups:
        for n, k in enumerate(offsets):
            part = array[n * share : (n + 1) * share]
            whole = lax.dynamic_update_slice(whole, part, (device_of(me, k) * share, 0))
    return [(whole, [])]


def arrays_of(groups):
    return [array for array, _ in groups]


def offsets_of(groups):
    return [offsets for _, offsets in groups]


def row_copies(me, shards, offsets, low, size, target, column, sem):
    copies = []
    columns, place = pl.ds(low, size), pl.ds(column, size)
    for shard, from_devices in zip(shards, offsets):
        if not from_devices:
            copies.append(
                pltpu.make_async_copy(shard.at[:, columns], target.at[:, place], sem)
            )
        for n, k in enumerate(from_devices):
            share = shard.shape[0] // len(from_devices)
            rows = pl.ds(pl.multiple_of(device_of(me, k) * share, 16), share)
            source = shard.at[pl.ds(n * share, share), columns]
            copies.append(pltpu.make_async_copy(source, target.at[rows, place], sem))
    return copies


def start_all(copies):
    for copy in copies:
        copy.start()


def wait_all(copies):
    for copy in copies:
        copy.wait()


def call(kernel, name, out_shape, operands, scratch):
    spaces = {
        "s": pl.BlockSpec(memory_space=pltpu.SMEM),
        "v": pl.BlockSpec(memory_space=pltpu.VMEM),
        "h": pl.BlockSpec(memory_space=pltpu.HBM),
    }
    return pl.pallas_call(
        kernel,
        out_shape=out_shape,
        in_specs=[spaces[space] for _, space in operands],
        out_specs=tuple(spaces["v"] for _ in out_shape),
        scratch_shapes=scratch,
        compiler_params=pltpu.CompilerParams(vmem_limit_bytes=VMEM_BYTES),
        cost_estimate=pl.CostEstimate(flops=1, transcendentals=0, bytes_accessed=1),
        name=name,
    )(*[array for array, _ in operands])


def shaped(rows, columns, kind=BF):
    return jax.ShapeDtypeStruct((rows, columns), kind)


def project(info, tokens, cosine, sine_tab, contexts):
    rows, width = tokens.shape
    own = rows // lax.axis_size("mp")
    block = min(rows, TILE)
    shards, offsets = arrays_of(contexts), offsets_of(contexts)
    wide = shards[0].shape[1]

    def kernel(info_ref, x_ref, cos_ref, sin_ref, *refs):
        shard_refs, refs = refs[: len(shards)], refs[len(shards) :]
        normed_ref, own_ref, key_ref, value_ref, gain_ref, w_c, sems = refs
        copies = row_copies(info_ref[0], shard_refs, offsets, 0, wide, w_c, 0, sems.at[0])
        start_all(copies)
        wait_all(copies)
        terms = w_c[:, 2 * HD : 2 * HD + LANES].astype(F32).T
        gains = terms[0:2] + terms[2:4] + terms[4:6]
        gain_ref[...] = jnp.concatenate([gains] * 4, axis=0)
        for r in range(0, rows, block):
            span = pl.ds(r, block)
            x = x_ref[span, :].astype(F32)
            normed = (x * inverse_rms(x) * gains[0:1]).astype(BF)
            normed_ref[span, :] = normed
            raw = mm(normed, w_c[:, : 2 * HD], ((1,), (0,)))
            key_ref[span, :] = rotate(raw[:, :HD], cos_ref[span, :], sin_ref[span, :]).astype(BF)
            value_ref[span, :] = raw[:, HD:].astype(BF)
        own_ref[...] = normed_ref[pl.ds(pl.multiple_of(info_ref[1], own), own), :]

    return call(
        kernel,
        "project",
        (
            shaped(rows, width),
            shaped(own, width),
            *[shaped(rows, HD)] * 2,
            shaped(8, width, F32),
        ),
        [(info, "s"), (tokens, "v"), (cosine, "v"), (sine_tab, "v")]
        + [(shard, "h") for shard in shards],
        [pltpu.VMEM((width, wide), BF), pltpu.SemaphoreType.DMA((1,))],
    )


def masked_scores(info_ref, query, keys):
    scores = mm(query, keys, ((1,), (1,))) * 0.0625
    at_row = info_ref[1] + lax.broadcasted_iota(jnp.int32, scores.shape, 0)
    at_key = lax.broadcasted_iota(jnp.int32, scores.shape, 1)
    allowed = (at_key <= at_row) & (at_key < info_ref[2])
    return jnp.where(allowed, scores, -1e30)


def attend(info, normed_own, keys, values, tokens_own, tables, gains, w_queries, w_outputs):
    own, width = tokens_own.shape
    q_shards, q_offsets = arrays_of(w_queries), offsets_of(w_queries)
    o_shards, o_offsets = arrays_of(w_outputs), offsets_of(w_outputs)
    across = q_shards[0].shape[1]

    def kernel(info_ref, own_ref, key_ref, value_ref, x_ref, cos_ref, sin_ref, gain_ref, *refs):
        q_refs, refs = refs[: len(q_shards)], refs[len(q_shards) :]
        o_refs, refs = refs[: len(o_shards)], refs[len(o_shards) :]
        query_ref, mixed_ref, middle_ref, normed_ref, log_ref, w_q, w_o, sems = refs
        copies = row_copies(info_ref[0], q_refs, q_offsets, 0, across, w_q, 0, sems.at[0])
        copies_o = row_copies(info_ref[0], o_refs, o_offsets, 0, across, w_o, 0, sems.at[1])
        start_all(copies)
        start_all(copies_o)
        wait_all(copies)
        keys, values = key_ref[...], value_ref[...]
        raw = mm(own_ref[...], w_q[...], ((1,), (0,)))
        for h in range(across // HD):
            columns = slice(h * HD, (h + 1) * HD)
            query = rotate(raw[:, columns], cos_ref[...], sin_ref[...]).astype(BF)
            query_ref[:, columns] = query
            scores = masked_scores(info_ref, query, keys)
            highest = jnp.max(scores, axis=-1, keepdims=True)
            exped = jnp.exp(scores - highest)
            total = jnp.sum(exped, axis=-1, keepdims=True)
            probs = (exped * (1.0 / total)).astype(BF)
            mixed_ref[:, columns] = mm(probs, values, ((1,), (0,))).astype(BF)
            log_ref[:, h : h + 1] = highest + jnp.log(total)
        wait_all(copies_o)
        middle = x_ref[...].astype(F32) + mm(mixed_ref[...], w_o[...], ((1,), (1,)))
        middle_ref[...] = middle
        normed_ref[...] = (middle * inverse_rms(middle) * gain_ref[1:2, :]).astype(BF)

    return call(
        kernel,
        "attend",
        (
            shaped(own, across),
            shaped(own, across),
            shaped(own, width, F32),
            shaped(own, width),
            shaped(own, LANES, F32),
        ),
        [(info, "s")]
        + [(array, "v") for array in (normed_own, keys, values, tokens_own, *tables, gains)]
        + [(shard, "h") for shard in q_shards + o_shards],
        [pltpu.VMEM((width, across), BF)] * 2 + [pltpu.SemaphoreType.DMA((2,))],
    )


def attend_back(
    info, parts, middle, grad_own, gains, queries, keys, values, log_sums, tables, w_outputs
):
    heads, n_parts = queries.shape[1] // HD, len(parts)
    own, width = middle.shape
    rows = keys.shape[0]
    output_shards, offsets = arrays_of(w_outputs), offsets_of(w_outputs)
    count = len(output_shards)

    def kernel(info_ref, *refs):
        part_refs, refs = refs[:n_parts], refs[n_parts:]
        middle_ref, grad_ref, gain_ref = refs[:3]
        query_ref, refs = refs[3], refs[4:]
        key_ref, value_ref, log_ref, cos_ref, sin_ref, cos_own, sin_own = refs[:7]
        shards, refs = refs[7 : 7 + count], refs[7 + count :]
        grad_middle_ref, low_ref, gain_two_ref, query_out, context_out, w_o, sem = refs
        copies = row_copies(info_ref[0], shards, offsets, 0, heads * HD, w_o, 0, sem.at[0])
        start_all(copies)
        grad_in = part_refs[0][...]
        for part_ref in part_refs[1:]:
            grad_in = grad_in + part_ref[...].astype(F32)
        middle = middle_ref[...]
        inverse = inverse_rms(middle)
        unit = middle * inverse
        gain_two = jnp.sum(grad_in * unit, axis=0, keepdims=True)
        gain_two_ref[...] = jnp.broadcast_to(gain_two, gain_two_ref.shape)
        grad_middle = grad_ref[...].astype(F32) + norm_back(
            grad_in, unit, inverse, gain_ref[1:2, :]
        )
        grad_middle_ref[...] = grad_middle
        low = grad_middle.astype(BF)
        low_ref[...] = low
        wait_all(copies)
        keys, values = key_ref[...], value_ref[...]
        grad_mixed = mm(low, w_o[...], ((1,), (0,))).astype(BF)
        grad_keys = grad_values = None
        for h in range(heads):
            query = query_ref[:, h * HD : (h + 1) * HD]
            scores = masked_scores(info_ref, query, keys)
            probs = jnp.exp(scores - log_ref[:, h : h + 1])
            grad_head = grad_mixed[:, h * HD : (h + 1) * HD]
            grad_probs = mm(grad_head, values, ((1,), (1,)))
            inner = jnp.sum(probs * grad_probs, axis=-1, keepdims=True)
            grad_scores = (probs * (grad_probs - inner)).astype(BF)
            turned = mm(grad_scores, keys, ((1,), (0,))) * 0.0625
            query_out[:, h * HD : (h + 1) * HD] = rotate(
                turned, cos_own[...], -sin_own[...]
            ).astype(BF)
            term_keys = mm(grad_scores, query, ((0,), (0,)))
            term_values = mm(probs.astype(BF), grad_head, ((0,), (0,)))
            grad_keys = term_keys if h == 0 else grad_keys + term_keys
            grad_values = term_values if h == 0 else grad_values + term_values
        context_out[:, :HD] = rotate(grad_keys * 0.0625, cos_ref[...], -sin_ref[...]).astype(BF)
        context_out[:, HD:] = grad_values.astype(BF)

    return call(
        kernel,
        "attend_back",
        (
            shaped(own, width, F32),
            shaped(own, width),
            shaped(8, width, F32),
            shaped(own, heads * HD),
            shaped(rows, 2 * HD),
        ),
        [(info, "s")]
        + [(part, "v") for part in parts]
        + [(middle, "v"), (grad_own, "v"), (gains, "v"), (queries, "v")]
        + [(array, "v") for array in (keys, values, log_sums, *tables)]
        + [(shard, "h") for shard in output_shards],
        [pltpu.VMEM((width, heads * HD), BF), pltpu.SemaphoreType.DMA((1,))],
    )


def store_sides(side, value, made, column, keep_ref, send_ref):
    blocks, share, _ = keep_ref.shape
    size = value.shape[1]
    for b in range(2 * blocks):
        made[b // 2, b % 2, :, :size] = value[b * share : (b + 1) * share].astype(BF)
    for b in range(blocks):
        keep_ref[b, :, column : column + size] = made[b, side, :, :size]
        send_ref[b, :, column : column + size] = made[b, 1 - side, :, :size]


def mixer_grads(
    info, normed, normed_own, grad_query, grad_context, low, mixed, gain_two, w_shards
):
    query_shards, context_shards = (arrays_of(groups) for groups in w_shards)
    offsets_q, offsets_c = (offsets_of(groups) for groups in w_shards)
    width = normed.shape[1]
    dp = lax.axis_size("dp")
    share = width // dp
    across = grad_query.shape[1]
    count = len(query_shards)
    first = jax.ShapeDtypeStruct((dp // 2, share, across + HD + LANES), BF)
    second = jax.ShapeDtypeStruct((dp // 2, share, across + HD), BF)

    def kernel(info_ref, *refs):
        normed_ref, own_ref, query_ref, context_ref, low_ref, mixed_ref, gain_ref = refs[:7]
        queries, contexts = refs[7 : 7 + count], refs[7 + count : 7 + 2 * count]
        keep_a, send_a, keep_b, send_b, w_q, w_c, made, sems = refs[7 + 2 * count :]
        side = info_ref[3]
        copies = row_copies(info_ref[0], queries, offsets_q, 0, across, w_q, 0, sems.at[0])
        copies_c = row_copies(info_ref[0], contexts, offsets_c, 0, 2 * HD, w_c, 0, sems.at[1])
        start_all(copies)
        start_all(copies_c)
        d_output = mm(low_ref[...], mixed_ref[...], ((0,), (0,)))
        halfway = across // HD // 2
        for h in range(across // HD):
            keep, send = (keep_a, send_a) if h < halfway else (keep_b, send_b)
            at = (2 * (h % halfway) + 1) * HD
            store_sides(side, d_output[:, h * HD : (h + 1) * HD], made, at, keep, send)
        d_query = mm(own_ref[...], query_ref[...], ((0,), (0,)))
        for h in range(across // HD):
            keep, send = (keep_a, send_a) if h < halfway else (keep_b, send_b)
            at = 2 * (h % halfway) * HD
            store_sides(side, d_query[:, h * HD : (h + 1) * HD], made, at, keep, send)
        d_context = mm(normed_ref[...], context_ref[...], ((0,), (0,)))
        store_sides(side, d_context[:, :HD], made, across, keep_a, send_a)
        store_sides(side, d_context[:, HD:], made, across, keep_b, send_b)
        wait_all(copies)
        wait_all(copies_c)
        gain_one = jnp.sum(d_query * w_q[...].astype(F32), axis=1, keepdims=True) + jnp.sum(
            d_context * w_c[...].astype(F32), axis=1, keepdims=True
        )
        second_gain = gain_ref[...].T
        lane = lax.broadcasted_iota(jnp.int32, (width, LANES), 1)
        both = jnp.where(lane == 0, gain_one, jnp.where(lane == 1, second_gain[:, 0:1], 0.0))
        store_sides(side, both, made, across + HD, keep_a, send_a)

    return call(
        kernel,
        "mixer_grads",
        (first, first, second, second),
        [(info, "s")]
        + [
            (array, "v")
            for array in (normed, normed_own, grad_query, grad_context, low, mixed, gain_two)
        ]
        + [(shard, "h") for shard in query_shards + context_shards],
        [
            pltpu.VMEM((width, across), BF),
            pltpu.VMEM((width, 2 * HD), BF),
            pltpu.VMEM((dp // 2, 2, share, across), BF),
            pltpu.SemaphoreType.DMA((2,)),
        ],
    )


def finish(info, grad_query, parts, grad_middle, tokens_own, gains, w_shards):
    query_shards, context_shards = (arrays_of(groups) for groups in w_shards)
    offsets_q, offsets_c = (offsets_of(groups) for groups in w_shards)
    own, width = grad_middle.shape
    across = grad_query.shape[1]
    count, n_parts = len(query_shards), len(parts)

    def kernel(info_ref, query_ref, *refs):
        part_refs, refs = refs[:n_parts], refs[n_parts:]
        middle_ref, x_ref, gain_ref = refs[:3]
        queries, contexts = refs[3 : 3 + count], refs[3 + count : 3 + 2 * count]
        out_ref, w_q, w_c, sems = refs[3 + 2 * count :]
        copies = row_copies(info_ref[0], queries, offsets_q, 0, across, w_q, 0, sems.at[0])
        copies_c = row_copies(info_ref[0], contexts, offsets_c, 0, 2 * HD, w_c, 0, sems.at[1])
        start_all(copies)
        start_all(copies_c)
        total = part_refs[0][...].astype(F32)
        for part_ref in part_refs[1:]:
            total = total + part_ref[...].astype(F32)
        x = x_ref[...].astype(F32)
        inverse = inverse_rms(x)
        wait_all(copies)
        wait_all(copies_c)
        grad_in = mm(query_ref[...], w_q[...], ((1,), (1,))) + mm(
            total.astype(BF), w_c[...], ((1,), (1,))
        )
        out_ref[...] = middle_ref[...] + norm_back(grad_in, x * inverse, inverse, gain_ref[0:1, :])

    return call(
        kernel,
        "finish",
        (shaped(own, width, F32),),
        [(info, "s"), (grad_query, "v")]
        + [(part, "v") for part in parts]
        + [(grad_middle, "v"), (tokens_own, "v"), (gains, "v")]
        + [(shard, "h") for shard in query_shards + context_shards],
        [
            pltpu.VMEM((width, across), BF),
            pltpu.VMEM((width, 2 * HD), BF),
            pltpu.SemaphoreType.DMA((2,)),
        ],
    )[0]


def feed_block(info, x, g, groups_a, groups_b, width, out_type):
    rows, depth = x.shape
    shards_a, shards_b = arrays_of(groups_a), arrays_of(groups_b)
    offsets, offsets_b = offsets_of(groups_a), offsets_of(groups_b)
    count = len(shards_a)
    half, cuts = column_cuts(width)

    def kernel(info_ref, x_ref, g_ref, *refs):
        first, second = refs[:count], refs[count : 2 * count]
        hid_ref, gate_ref, up_ref, feed_ref, back_ref = refs[2 * count : 2 * count + 5]
        w_gate, w_up, w_down, sems = refs[2 * count + 5 :]
        copies = []
        for n, (low, high) in enumerate(cuts):
            size = high - low
            source, at = (first, width + low) if high <= half else (second, width + low - half)
            group = []
            for shards, start, target in (
                (first, low, w_gate),
                (second, low, w_up),
                (source, at, w_down),
            ):
                own_offsets = offsets_b if shards is second else offsets
                group += row_copies(
                    info_ref[0], shards, own_offsets, start, size, target, low, sems.at[n]
                )
            copies.append(group)
            start_all(group)
        scale = 0.7978845608028654
        feed = back = None
        for n, (low, high) in enumerate(cuts):
            wait_all(copies[n])
            x, g = x_ref[...], g_ref[...]
            gate_w, up_w, down_w = w_gate[:, low:high], w_up[:, low:high], w_down[:, low:high]
            gate = mm(x, gate_w, ((1,), (0,)))
            up = mm(x, up_w, ((1,), (0,)))
            grad = mm(g, down_w, ((1,), (0,)))
            square = gate * gate
            tanh = jnp.tanh(scale * gate * (1.0 + 0.044715 * square))
            right = 0.5 * (1.0 + tanh)
            gelu = gate * right
            slope = right + gelu * (1.0 - tanh) * scale * (1.0 + 3 * 0.044715 * square)
            hidden = (gelu * up).astype(BF)
            grad_gate = (grad * up * slope).astype(BF)
            grad_up = (grad * gelu).astype(BF)
            hid_ref[:, low:high] = hidden
            gate_ref[:, low:high] = grad_gate
            up_ref[:, low:high] = grad_up
            feed_n = mm(hidden, down_w, ((1,), (1,)))
            back_n = mm(grad_gate, gate_w, ((1,), (1,))) + mm(grad_up, up_w, ((1,), (1,)))
            feed = feed_n if feed is None else feed + feed_n
            back = back_n if back is None else back + back_n
        feed_ref[...] = feed.astype(feed_ref.dtype)
        back_ref[...] = back.astype(back_ref.dtype)

    return call(
        kernel,
        "feed_block",
        (*[shaped(rows, width)] * 3, *[shaped(rows, depth, out_type)] * 2),
        [(info, "s"), (x, "v"), (g, "v")] + [(shard, "h") for shard in shards_a + shards_b],
        [pltpu.VMEM((depth, width), BF)] * 3 + [pltpu.SemaphoreType.DMA((3,))],
    )


def feed_grads(info, lefts, rights, low, high, firsts, whole):
    parts, dp = len(lefts), lax.axis_size("dp")
    depth, width = lefts[0].shape
    share = width // dp
    full = whole[0].shape[1]
    n_whole, n_part = full // TILE, (high - low) // TILE
    half = jax.ShapeDtypeStruct((dp // 2, share, full + high - low), BF)

    def kernel(info_ref, *refs):
        first_refs, whole_refs = refs[:parts], refs[parts : 2 * parts]
        left_refs, right_refs = refs[2 * parts : 3 * parts], refs[3 * parts : 4 * parts]
        keep_ref, send_ref, made = refs[4 * parts :]

        def one(rows, columns):
            total = None
            for row, column in zip(rows, columns):
                term = mm(row[...], column[...], ((0,), (0,)))
                total = term if total is None else total + term
            store_sides(info_ref[3], total, made, 0, keep_ref, send_ref)

        @pl.when(pl.program_id(0) < n_whole)
        def _():
            one(first_refs, whole_refs)

        @pl.when(pl.program_id(0) >= n_whole)
        def _():
            one(left_refs, right_refs)

    def whole_map(f, info_ref):
        return (0, jnp.minimum(f, n_whole - 1))

    def part_map(f, info_ref):
        return (0, low // TILE + jnp.maximum(f - n_whole, 0))

    fixed = pl.BlockSpec((depth, width), lambda f, info_ref: (0, 0))
    return pl.pallas_call(
        kernel,
        out_shape=(half, half),
        grid_spec=pltpu.PrefetchScalarGridSpec(
            num_scalar_prefetch=1,
            grid=(n_whole + n_part,),
            in_specs=[fixed] * parts
            + [pl.BlockSpec((depth, TILE), whole_map)] * parts
            + [fixed] * parts
            + [pl.BlockSpec((depth, TILE), part_map)] * parts,
            out_specs=[pl.BlockSpec((dp // 2, share, TILE), lambda f, info_ref: (0, 0, f))] * 2,
            scratch_shapes=[pltpu.VMEM((dp // 2, 2, share, TILE), BF)],
        ),
        compiler_params=pltpu.CompilerParams(vmem_limit_bytes=VMEM_BYTES),
        cost_estimate=pl.CostEstimate(flops=1, transcendentals=0, bytes_accessed=1),
        name="feed_grads",
    )(info, *firsts, *whole, *lefts, *rights)


class Halving:
    def __init__(self, keep, send, order):
        self.order = order
        self.left = [2**j for j in reversed(range(len(order)))]
        self.sent = swap(send, order[0])
        self.kept = keep
        self.left.remove(order[0])
        self.stage = 1

    def halve(self):
        me = lax.axis_index("dp")
        total = (self.kept.astype(F32) + self.sent.astype(F32)).astype(BF)
        bit = self.order[self.stage]
        total = total.reshape((2,) * len(self.left) + total.shape[-2:])
        axis = self.left.index(bit)
        side = (me // bit) % 2
        self.kept = lax.dynamic_index_in_dim(total, side, axis, keepdims=False)
        self.ready = lax.dynamic_index_in_dim(total, 1 - side, axis, keepdims=False)
        self.left.remove(bit)

    def send(self):
        self.sent = swap(self.ready, self.order[self.stage])
        self.stage += 1

    def step(self):
        self.halve()
        self.send()

    def done(self):
        while self.stage < len(self.order):
            self.step()
        return self.kept.astype(F32) + self.sent.astype(F32)


def step_both(first, second):
    first.halve()
    second.halve()
    first.kept, (second.kept, first.ready, second.ready) = after(
        first.kept, second.kept, first.ready, second.ready
    )
    first.send()
    second.send()


def after(values, *others):
    flat, tree = jax.tree.flatten((values, others))
    return jax.tree.unflatten(tree, lax.optimization_barrier(flat))


def local(
    tokens,
    cotangent,
    lengths,
    rates,
    query_weight,
    query_moment,
    query_average,
    output_weight,
    output_moment,
    output_average,
    gating_weight,
    gating_moment,
    gating_average,
    down_weight,
    down_moment,
    down_average,
    context_weight,
    context_moment,
    context_average,
    gains_weight,
    gains_moment,
    gains_average,
):
    row_count, width = tokens.shape
    dp, mp = lax.axis_size("dp"), lax.axis_size("mp")
    place = lax.axis_index("mp")
    own_count = row_count // mp
    own_start = place * own_count
    share, piece = width // dp, width // (dp * mp)
    forth, back = bit_orders()
    forth_first, back_first = forth[-1:] + forth[:-1], back[-1:] + back[:-1]
    length = lengths[0]
    places = jnp.arange(row_count, dtype=jnp.int32)
    me = lax.axis_index("dp")
    info = jnp.stack([me, own_start, length, me % 2]).astype(jnp.int32)

    def rows_at(tensor, step, count):
        return lax.dynamic_slice_in_dim(tensor, (place ^ step) * count, count, 0)

    gains_split = jnp.stack(split_three(gains_weight)).reshape(1, -1)
    message = jnp.concatenate(
        [
            query_weight.astype(BF),
            output_weight.T.astype(BF),
            context_weight.astype(BF).reshape(2 * piece, HD),
            jnp.pad(gains_split, ((0, 0), (0, HD - gains_split.shape[1]))),
        ],
        axis=0,
    )
    message = jnp.pad(message, ((0, -message.shape[0] % 16), (0, 0)))
    copies = jnp.broadcast_to(message[None], (mp, *message.shape))
    line = lax.all_to_all(copies, "mp", 0, 0, tiled=True)
    parts = [lax.dynamic_index_in_dim(line, place ^ k, 0, keepdims=False) for k in range(mp)]
    query_share = jnp.concatenate([part[:share] for part in parts], axis=1)
    output_share = jnp.concatenate([part[share : 2 * share] for part in parts], axis=1)
    rests = [line[k, 2 * share :] for k in range(mp)]
    context_share = jnp.concatenate(
        [
            jnp.concatenate(
                [
                    rest[:piece],
                    rest[piece : 2 * piece],
                    jnp.pad(
                        rest[2 * piece, : 6 * piece].reshape(6, piece).T, ((0, 0), (0, LANES - 6))
                    ),
                ],
                axis=1,
            )
            for rest in rests
        ],
        axis=0,
    )

    units = gating_weight.shape[2]
    padded = round_up(units, TILE)
    half = column_cuts(padded)[0]

    def pad_units(tensor):
        return jnp.pad(tensor, ((0, 0), (0, padded - units)))

    gating_low = gating_weight.astype(BF)
    down_low = pad_units(down_weight.T.astype(BF))
    feed_a = jnp.concatenate([pad_units(gating_low[0]), down_low[:, :half]], axis=1)
    feed_b = jnp.concatenate([pad_units(gating_low[1]), down_low[:, half:]], axis=1)
    first_a, first_b = swap(feed_a, forth[0]), swap(feed_b, back[0])
    own_a, own_b = swap(feed_a, forth[1]), swap(feed_b, back[1])
    early, contexts = spread_at_once(context_share, (first_a, first_b, own_a, own_b))
    first_a, first_b, own_a, own_b = early
    held_q, held_o = [query_share, swap(query_share, forth[0])], [output_share, swap(output_share, back[0])]

    cosine, sine_tab = rotation(row_count, HD)
    tokens_own = rows_at(tokens, 0, own_count)
    tables_own = (rows_at(cosine, 0, own_count), rows_at(sine_tab, 0, own_count))
    context_near, (tokens_own, tables_own) = after(contexts[1][0], tokens_own, tables_own)
    contexts = [contexts[0], (context_near, contexts[1][1])]
    contexts = lay(contexts)
    normed, normed_own, keys, values, gains = project(info, tokens, cosine, sine_tab, contexts)
    (held_q, held_o, cotangent_too), (gains,) = after((held_q, held_o, cotangent), gains)
    grad_low = jnp.where((places < length)[:, None], cotangent_too, jnp.zeros_like(cotangent))
    grad_blocks = [rows_at(grad_low, k, own_count) for k in range(mp)]
    w_queries = spread_on(held_q, forth)
    w_outputs = spread_on(held_o, back)
    w_queries[0], (grad_blocks,) = after(w_queries[0], grad_blocks)
    (sent_a, sent_b), (w_queries[0], w_outputs[0]) = after(
        (first_a, first_b), w_queries[0], w_outputs[0]
    )
    w_queries, w_outputs = spread_out(w_queries, forth), spread_out(w_outputs, back)
    w_queries, w_outputs = lay(w_queries), lay(w_outputs)
    pieces_a, offsets_a = spread_wide([feed_a, first_a], own_a, sent_a, forth)
    pieces_b, offsets_b = spread_wide([feed_b, first_b], own_b, sent_b, back)
    shards_a = spread_last(pieces_a[:2], offsets_a[:2], forth[-1])
    shards_b = spread_last(pieces_b[:2], offsets_b[:2], back[-1])
    normed_own, (shards_a, shards_b, grad_blocks) = after(
        normed_own, arrays_of(shards_a), arrays_of(shards_b), grad_blocks
    )
    shards_a = list(zip(shards_a, [offsets_a[:2], [k ^ 1 for k in offsets_a[:2]]]))
    shards_b = list(zip(shards_b, [offsets_b[:2], [k ^ 1 for k in offsets_b[:2]]]))
    queries, mixed, middle, normed_two_own, log_sums = attend(
        info, normed_own, keys, values, tokens_own, tables_own, gains, w_queries, w_outputs
    )

    (pieces_a[2:], pieces_b[2:]), (normed_two_own,) = after(
        (pieces_a[2:], pieces_b[2:]), normed_two_own
    )
    for n in range(2, len(pieces_a), 2):
        shards_a = shards_a + spread_last(pieces_a[n : n + 2], offsets_a[n : n + 2], forth[-1])
        shards_b = shards_b + spread_last(pieces_b[n : n + 2], offsets_b[n : n + 2], back[-1])
    shards_a, shards_b = lay(shards_a), lay(shards_b)
    blocks = [normed_two_own] + [across_heads(normed_two_own, k) for k in range(1, mp)]
    made = []
    for k in range(mp):
        if k > 0:
            blocks[k], (made[k - 1],) = after(blocks[k], made[k - 1])
        made.append(
            feed_block(
                info, blocks[k], grad_blocks[k], shards_a, shards_b, padded, F32 if k == 0 else BF
            )
        )
    hidden, grad_gate, grad_up, feed_parts, back_parts = (
        [made[k][n] for k in range(mp)] for n in range(5)
    )
    back_parts = back_parts[:1] + [across_heads(back_parts[k], k) for k in range(1, mp)]
    grad_up, (back_parts[1],) = after(grad_up, back_parts[1])
    keep_b, send_b = feed_grads(info, grad_blocks, hidden, half, padded, blocks, grad_up)
    grad_gate, (keep_b, back_parts[2:-1]) = after(grad_gate, keep_b, back_parts[2:-1])
    keep_a, send_a = feed_grads(info, grad_blocks, hidden, 0, half, blocks, grad_gate)
    held = (back_parts, feed_parts, keep_a, keep_b, normed, normed_own, mixed, middle, queries)
    held += (keys, values, log_sums, gains, cosine, sine_tab, tables_own, tokens_own, grad_blocks)
    held += (arrays_of(w_queries), arrays_of(contexts), arrays_of(w_outputs))
    (send_a, send_b), held = after((send_a, send_b), *held)
    back_parts, feed_parts, keep_a, keep_b, normed, normed_own, mixed, middle, queries = held[:9]
    keys, values, log_sums, gains, cosine, sine_tab, tables_own, tokens_own, grad_blocks = held[9:18]
    w_queries = list(zip(held[18], offsets_of(w_queries)))
    contexts = list(zip(held[19], offsets_of(contexts)))
    w_outputs = list(zip(held[20], offsets_of(w_outputs)))
    flow_a, flow_b = Halving(keep_a, send_a, forth_first), Halving(keep_b, send_b, back_first)
    flow_a.sent, (flow_b.sent, flow_a.kept, flow_b.kept) = after(
        flow_a.sent, flow_b.sent, flow_a.kept, flow_b.kept
    )
    step_both(flow_a, flow_b)
    feed_parts, (back_parts,) = after(feed_parts, back_parts)
    feed_line = jnp.stack([part.astype(BF) for part in feed_parts])
    feed_line = jnp.stack(
        [lax.dynamic_index_in_dim(feed_line, place ^ k, 0, keepdims=False) for k in range(mp)]
    )
    feed_line = lax.all_to_all(feed_line, "mp", 0, 0, tiled=True)
    back_parts, (flow_a.kept, flow_b.kept) = after(back_parts, flow_a.kept, flow_b.kept)

    grad_middle, middle_low, gain_two, grad_query, grad_context = attend_back(
        info,
        back_parts,
        middle,
        grad_blocks[0],
        gains,
        queries,
        keys,
        values,
        log_sums,
        (cosine, sine_tab, *tables_own),
        w_outputs,
    )

    w_shards = (w_queries, contexts)
    keep_a, send_a, keep_b, send_b = mixer_grads(
        info, normed, normed_own, grad_query, grad_context, middle_low, mixed, gain_two, w_shards
    )
    (send_a, send_b), (flow_a.sent, flow_b.sent) = after((send_a, send_b), flow_a.sent, flow_b.sent)
    step_both(flow_a, flow_b)
    mixer_a, mixer_b = Halving(keep_a, send_a, forth_first), Halving(keep_b, send_b, back_first)
    mixer_a.sent, (mixer_b.sent, flow_a.kept, flow_b.kept) = after(
        mixer_a.sent, mixer_b.sent, flow_a.kept, flow_b.kept
    )
    step_both(mixer_a, mixer_b)
    mixer_a.sent, (mixer_b.sent, mixer_a.kept, mixer_b.kept, flow_a.sent, flow_b.sent) = after(
        mixer_a.sent, mixer_b.sent, mixer_a.kept, mixer_b.kept, flow_a.sent, flow_b.sent
    )
    step_both(mixer_a, mixer_b)
    (flow_a.sent, flow_b.sent), (mixer_a.sent, mixer_b.sent) = after(
        (flow_a.sent, flow_b.sent), mixer_a.sent, mixer_b.sent
    )
    context_line, (feed_line,) = after(grad_context, feed_line)
    context_line = context_line.reshape(mp, own_count, 2 * HD)
    context_line = lax.all_to_all(context_line, "mp", 0, 0, tiled=True)
    feed_one, feed_two = flow_a.done(), flow_b.done()
    mixer_one, mixer_two = mixer_a.done(), mixer_b.done()
    across, halfway = grad_query.shape[1], mp // 2
    shares = [
        (mixer_one if k < halfway else mixer_two)[
            :, (k % halfway) * 2 * HD : (k % halfway + 1) * 2 * HD
        ]
        for k in range(mp)
    ]
    share_context = jnp.concatenate([mixer_one[:, across:], mixer_two[:, across:]], axis=1)
    wide = share_context.shape[1]
    total = shares[0]
    for k in range(1, mp):
        total = total + across_heads(shares[k].astype(BF), k).astype(F32)
    sum_context = rows_at(share_context, 0, piece)
    for k in range(1, mp):
        sent = across_heads(rows_at(share_context, k, piece).astype(BF), k)
        sum_context = sum_context + sent.astype(F32)
    context_own = jnp.sum(context_line.astype(F32), axis=0)
    tokens_grad = finish(info, grad_query, [context_own], grad_middle, tokens_own, gains, w_shards)
    block_out = middle + jnp.sum(feed_line.astype(F32), axis=0)

    total, (tokens_grad,) = after(total, tokens_grad)
    sum_query, sum_output = total[:, :HD], total[:, HD:].T
    sum_gains = jnp.stack([sum_context[:, HD] / gains_weight[0], sum_context[:, HD + 1]])
    sum_context = jnp.stack([sum_context[:, :HD], sum_context[:, wide - HD :]])
    sum_gating = jnp.stack([feed_one[:, :units], feed_two[:, :units]])
    sum_down = jnp.concatenate([feed_one[:, padded:], feed_two[:, padded:]], axis=1)[:, :units].T

    query_grads, query_moments, query_averages, query_updated = advance(
        sum_query, query_moment, query_average, query_weight, rates[0]
    )
    output_grads, output_moments, output_averages, output_updated = advance(
        sum_output, output_moment, output_average, output_weight, rates[1]
    )
    gating_grads, gating_moments, gating_averages, gating_updated = advance(
        sum_gating, gating_moment, gating_average, gating_weight, rates[2]
    )
    down_grads, down_moments, down_averages, down_updated = advance(
        sum_down, down_moment, down_average, down_weight, rates[3]
    )
    context_grads, context_moments, context_averages, context_updated = advance(
        sum_context, context_moment, context_average, context_weight, rates[4]
    )
    gains_grads, gains_moments, gains_averages, gains_updated = advance(
        sum_gains, gains_moment, gains_average, gains_weight, rates[5]
    )
    return (
        block_out,
        tokens_grad,
        query_grads,
        query_moments,
        query_averages,
        query_updated,
        output_grads,
        output_moments,
        output_averages,
        output_updated,
        gating_grads,
        gating_moments,
        gating_averages,
        gating_updated,
        down_grads,
        down_moments,
        down_averages,
        down_updated,
        context_grads,
        context_moments,
        context_averages,
        context_updated,
        gains_grads,
        gains_moments,
        gains_averages,
        gains_updated,
    )


def solution(mesh):
    return jax.shard_map(
        local,
        mesh=mesh,
        in_specs=(
            P("dp", None),
            P("dp", None),
            P("dp"),
            P(),
            P("dp", "mp"),
            P("dp", "mp"),
            P("dp", "mp"),
            P("mp", "dp"),
            P("mp", "dp"),
            P("mp", "dp"),
            P(None, "dp", "mp"),
            P(None, "dp", "mp"),
            P(None, "dp", "mp"),
            P("mp", "dp"),
            P("mp", "dp"),
            P("mp", "dp"),
            P(None, ("dp", "mp"), None),
            P(None, ("dp", "mp"), None),
            P(None, ("dp", "mp"), None),
            P(None, ("dp", "mp")),
            P(None, ("dp", "mp")),
            P(None, ("dp", "mp")),
        ),
        out_specs=(
            P(("dp", "mp"), None),
            P(("dp", "mp"), None),
            P("dp", "mp"),
            P("dp", "mp"),
            P("dp", "mp"),
            P("dp", "mp"),
            P("mp", "dp"),
            P("mp", "dp"),
            P("mp", "dp"),
            P("mp", "dp"),
            P(None, "dp", "mp"),
            P(None, "dp", "mp"),
            P(None, "dp", "mp"),
            P(None, "dp", "mp"),
            P("mp", "dp"),
            P("mp", "dp"),
            P("mp", "dp"),
            P("mp", "dp"),
            P(None, ("dp", "mp"), None),
            P(None, ("dp", "mp"), None),
            P(None, ("dp", "mp"), None),
            P(None, ("dp", "mp"), None),
            P(None, ("dp", "mp")),
            P(None, ("dp", "mp")),
            P(None, ("dp", "mp")),
            P(None, ("dp", "mp")),
        ),
        check_vma=False,
    )
```

```python
import jax
import jax.numpy as jnp
from jax import lax
from jax.experimental import pallas as pl
from jax.experimental.pallas import tpu as pltpu
from jax.sharding import PartitionSpec as P

HD = 256
LANES = 128
TILE = 256
VMEM_BYTES = 56 * 1024 * 1024
EPSILON = 1e-06
MOMENTUM = 0.9
AVERAGING = 0.5
BF = jnp.bfloat16
F32 = jnp.float32


def mm(a, b, dims):
    return lax.dot_general(a, b, (dims, ((), ())), preferred_element_type=F32)


def inverse_rms(tensor):
    return lax.rsqrt(jnp.mean(tensor * tensor, axis=-1, keepdims=True) + EPSILON)


def norm_back(grad_in, unit, inverse, gain_vec):
    scaled = grad_in * gain_vec
    return inverse * (scaled - unit * jnp.mean(scaled * unit, axis=-1, keepdims=True))


def rotation(length, head_size):
    halfway = head_size // 2
    frequency = 1000000.0 ** (-(jnp.arange(halfway).astype(F32) * 2.0 / head_size))
    angles = jnp.arange(length).astype(F32)[:, None] * frequency[None, :]
    return (jnp.cos(angles), jnp.sin(angles))


def rotate(tensor, cosine, sine_tab):
    halfway = tensor.shape[-1] // 2
    former = tensor[..., :halfway]
    latter = tensor[..., halfway:]
    return jnp.concatenate(
        [former * cosine - latter * sine_tab, latter * cosine + former * sine_tab], axis=-1
    )


def advance(gradient, moment, average, weight, step_rate):
    moment_new = MOMENTUM * moment + gradient
    weight_new = weight - step_rate * (gradient + MOMENTUM * moment_new)
    average_new = AVERAGING * average + (1.0 - AVERAGING) * weight_new
    return (gradient, moment_new, average_new, weight_new)


def swap(tensor, bit):
    count = lax.axis_size("dp")
    return lax.ppermute(tensor, "dp", [(i, i ^ bit) for i in range(count)])


def across_heads(tensor, bit):
    count = lax.axis_size("mp")
    return lax.ppermute(tensor, "mp", [(i, i ^ bit) for i in range(count)])


def bit_orders():
    bits = []
    while 2 ** len(bits) < lax.axis_size("dp"):
        bits.append(2 ** len(bits))
    outer = bits[1:]
    return (outer + bits[:1], outer[::-1] + bits[:1])


def split_three(tensor):
    high = lax.reduce_precision(tensor, 8, 7)
    rest = tensor - high
    middle = lax.reduce_precision(rest, 8, 7)
    return [high.astype(BF), middle.astype(BF), (rest - middle).astype(BF)]


def spread_on(pieces, order):
    held, offsets = jnp.concatenate(pieces, axis=0), [0, order[0]]
    for bit in order[1:-1]:
        held = jnp.concatenate([held, swap(held, bit)], axis=0)
        offsets = offsets + [k ^ bit for k in offsets]
    return [held, offsets]


def spread_out(group, order):
    held, offsets = group
    bit = order[-1]
    return [(held, offsets), (swap(held, bit), [k ^ bit for k in offsets])]


def spread_at_once(tensor, early):
    count = lax.axis_size("dp")
    groups = [list(range(side, count, 2)) for side in (0, 1)]
    copies = jnp.broadcast_to(tensor[None], (count // 2, *tensor.shape))
    held = lax.all_to_all(copies, "dp", 0, 0, axis_index_groups=groups, tiled=True)
    held = held.reshape(count // 2 * tensor.shape[0], tensor.shape[1])
    held, early = after(held, *early)
    return early, [
        (held, [(j, 0) for j in range(count // 2)]),
        (swap(held, 1), [(j, 1) for j in range(count // 2)]),
    ]


def spread_wide(pieces, own_sent, first_sent, order):
    offsets = [0, order[0], order[1], order[0] ^ order[1]]
    pieces = pieces + [own_sent, swap(first_sent, order[1])]
    for bit in order[2:-1]:
        pieces = pieces + [swap(piece, bit) for piece in pieces]
        offsets = offsets + [k ^ bit for k in offsets]
    return pieces, offsets


def spread_last(pieces, offsets, bit):
    pair = jnp.concatenate(pieces, axis=0)
    return [(pair, offsets), (swap(pair, bit), [k ^ bit for k in offsets])]


def round_up(number, unit):
    return -(-number // unit) * unit


def column_cuts(width):
    half = round_up(width // TILE, 2) // 2 * TILE
    first = TILE
    return half, [(0, first), (first, half), (half, width)]


def device_of(me, offset):
    if isinstance(offset, tuple):
        return 2 * offset[0] + ((me & 1) ^ offset[1])
    return me ^ offset


def lay(groups):
    share = groups[0][0].shape[0] // len(groups[0][1])
    if share % 16 == 0:
        return groups
    me = lax.axis_index("dp")
    count = lax.axis_size("dp")
    whole = jnp.zeros((count * share, groups[0][0].shape[1]), groups[0][0].dtype)
    for array, offsets in groups:
        for n, k in enumerate(offsets):
            part = array[n * share : (n + 1) * share]
            whole = lax.dynamic_update_slice(whole, part, (device_of(me, k) * share, 0))
    return [(whole, [])]


def arrays_of(groups):
    return [array for array, _ in groups]


def offsets_of(groups):
    return [offsets for _, offsets in groups]


def row_copies(me, shards, offsets, low, size, target, column, sem):
    copies = []
    columns, place = pl.ds(low, size), pl.ds(column, size)
    for shard, from_devices in zip(shards, offsets):
        if not from_devices:
            copies.append(
                pltpu.make_async_copy(shard.at[:, columns], target.at[:, place], sem)
            )
        for n, k in enumerate(from_devices):
            share = shard.shape[0] // len(from_devices)
            rows = pl.ds(pl.multiple_of(device_of(me, k) * share, 16), share)
            source = shard.at[pl.ds(n * share, share), columns]
            copies.append(pltpu.make_async_copy(source, target.at[rows, place], sem))
    return copies


def start_all(copies):
    for copy in copies:
        copy.start()


def wait_all(copies):
    for copy in copies:
        copy.wait()


def call(kernel, name, out_shape, operands, scratch):
    spaces = {
        "s": pl.BlockSpec(memory_space=pltpu.SMEM),
        "v": pl.BlockSpec(memory_space=pltpu.VMEM),
        "h": pl.BlockSpec(memory_space=pltpu.HBM),
    }
    return pl.pallas_call(
        kernel,
        out_shape=out_shape,
        in_specs=[spaces[space] for _, space in operands],
        out_specs=tuple(spaces["v"] for _ in out_shape),
        scratch_shapes=scratch,
        compiler_params=pltpu.CompilerParams(vmem_limit_bytes=VMEM_BYTES),
        cost_estimate=pl.CostEstimate(flops=1, transcendentals=0, bytes_accessed=1),
        name=name,
    )(*[array for array, _ in operands])


def shaped(rows, columns, kind=BF):
    return jax.ShapeDtypeStruct((rows, columns), kind)


def project(info, tokens, cosine, sine_tab, contexts):
    rows, width = tokens.shape
    own = rows // lax.axis_size("mp")
    block = min(rows, TILE)
    shards, offsets = arrays_of(contexts), offsets_of(contexts)
    wide = shards[0].shape[1]

    def kernel(info_ref, x_ref, cos_ref, sin_ref, *refs):
        shard_refs, refs = refs[: len(shards)], refs[len(shards) :]
        normed_ref, own_ref, key_ref, value_ref, gain_ref, w_c, sems = refs
        copies = row_copies(info_ref[0], shard_refs, offsets, 0, wide, w_c, 0, sems.at[0])
        start_all(copies)
        wait_all(copies)
        terms = w_c[:, 2 * HD : 2 * HD + LANES].astype(F32).T
        gains = terms[0:2] + terms[2:4] + terms[4:6]
        gain_ref[...] = jnp.concatenate([gains] * 4, axis=0)
        for r in range(0, rows, block):
            span = pl.ds(r, block)
            x = x_ref[span, :].astype(F32)
            normed = (x * inverse_rms(x) * gains[0:1]).astype(BF)
            normed_ref[span, :] = normed
            raw = mm(normed, w_c[:, : 2 * HD], ((1,), (0,)))
            key_ref[span, :] = rotate(raw[:, :HD], cos_ref[span, :], sin_ref[span, :]).astype(BF)
            value_ref[span, :] = raw[:, HD:].astype(BF)
        own_ref[...] = normed_ref[pl.ds(pl.multiple_of(info_ref[1], own), own), :]

    return call(
        kernel,
        "project",
        (
            shaped(rows, width),
            shaped(own, width),
            *[shaped(rows, HD)] * 2,
            shaped(8, width, F32),
        ),
        [(info, "s"), (tokens, "v"), (cosine, "v"), (sine_tab, "v")]
        + [(shard, "h") for shard in shards],
        [pltpu.VMEM((width, wide), BF), pltpu.SemaphoreType.DMA((1,))],
    )


def masked_scores(info_ref, query, keys):
    scores = mm(query, keys, ((1,), (1,))) * 0.0625
    at_row = info_ref[1] + lax.broadcasted_iota(jnp.int32, scores.shape, 0)
    at_key = lax.broadcasted_iota(jnp.int32, scores.shape, 1)
    allowed = (at_key <= at_row) & (at_key < info_ref[2])
    return jnp.where(allowed, scores, -1e30)


def attend(info, normed_own, keys, values, tokens_own, tables, gains, w_queries, w_outputs):
    own, width = tokens_own.shape
    q_shards, q_offsets = arrays_of(w_queries), offsets_of(w_queries)
    o_shards, o_offsets = arrays_of(w_outputs), offsets_of(w_outputs)
    across = q_shards[0].shape[1]

    def kernel(info_ref, own_ref, key_ref, value_ref, x_ref, cos_ref, sin_ref, gain_ref, *refs):
        q_refs, refs = refs[: len(q_shards)], refs[len(q_shards) :]
        o_refs, refs = refs[: len(o_shards)], refs[len(o_shards) :]
        query_ref, mixed_ref, middle_ref, normed_ref, log_ref, w_q, w_o, sems = refs
        copies = row_copies(info_ref[0], q_refs, q_offsets, 0, across, w_q, 0, sems.at[0])
        copies_o = row_copies(info_ref[0], o_refs, o_offsets, 0, across, w_o, 0, sems.at[1])
        start_all(copies)
        start_all(copies_o)
        wait_all(copies)
        keys, values = key_ref[...], value_ref[...]
        raw = mm(own_ref[...], w_q[...], ((1,), (0,)))
        for h in range(across // HD):
            columns = slice(h * HD, (h + 1) * HD)
            query = rotate(raw[:, columns], cos_ref[...], sin_ref[...]).astype(BF)
            query_ref[:, columns] = query
            scores = masked_scores(info_ref, query, keys)
            highest = jnp.max(scores, axis=-1, keepdims=True)
            exped = jnp.exp(scores - highest)
            total = jnp.sum(exped, axis=-1, keepdims=True)
            probs = (exped * (1.0 / total)).astype(BF)
            mixed_ref[:, columns] = mm(probs, values, ((1,), (0,))).astype(BF)
            log_ref[:, h : h + 1] = highest + jnp.log(total)
        wait_all(copies_o)
        middle = x_ref[...].astype(F32) + mm(mixed_ref[...], w_o[...], ((1,), (1,)))
        middle_ref[...] = middle
        normed_ref[...] = (middle * inverse_rms(middle) * gain_ref[1:2, :]).astype(BF)

    return call(
        kernel,
        "attend",
        (
            shaped(own, across),
            shaped(own, across),
            shaped(own, width, F32),
            shaped(own, width),
            shaped(own, LANES, F32),
        ),
        [(info, "s")]
        + [(array, "v") for array in (normed_own, keys, values, tokens_own, *tables, gains)]
        + [(shard, "h") for shard in q_shards + o_shards],
        [pltpu.VMEM((width, across), BF)] * 2 + [pltpu.SemaphoreType.DMA((2,))],
    )


def attend_back(
    info, parts, middle, grad_own, gains, queries, keys, values, log_sums, tables, w_outputs
):
    heads, n_parts = queries.shape[1] // HD, len(parts)
    own, width = middle.shape
    rows = keys.shape[0]
    output_shards, offsets = arrays_of(w_outputs), offsets_of(w_outputs)
    count = len(output_shards)

    def kernel(info_ref, *refs):
        part_refs, refs = refs[:n_parts], refs[n_parts:]
        middle_ref, grad_ref, gain_ref = refs[:3]
        query_ref, refs = refs[3], refs[4:]
        key_ref, value_ref, log_ref, cos_ref, sin_ref, cos_own, sin_own = refs[:7]
        shards, refs = refs[7 : 7 + count], refs[7 + count :]
        grad_middle_ref, low_ref, gain_two_ref, query_out, context_out, w_o, sem = refs
        copies = row_copies(info_ref[0], shards, offsets, 0, heads * HD, w_o, 0, sem.at[0])
        start_all(copies)
        grad_in = part_refs[0][...]
        for part_ref in part_refs[1:]:
            grad_in = grad_in + part_ref[...].astype(F32)
        middle = middle_ref[...]
        inverse = inverse_rms(middle)
        unit = middle * inverse
        gain_two = jnp.sum(grad_in * unit, axis=0, keepdims=True)
        gain_two_ref[...] = jnp.broadcast_to(gain_two, gain_two_ref.shape)
        grad_middle = grad_ref[...].astype(F32) + norm_back(
            grad_in, unit, inverse, gain_ref[1:2, :]
        )
        grad_middle_ref[...] = grad_middle
        low = grad_middle.astype(BF)
        low_ref[...] = low
        wait_all(copies)
        keys, values = key_ref[...], value_ref[...]
        grad_mixed = mm(low, w_o[...], ((1,), (0,))).astype(BF)
        grad_keys = grad_values = None
        for h in range(heads):
            query = query_ref[:, h * HD : (h + 1) * HD]
            scores = masked_scores(info_ref, query, keys)
            probs = jnp.exp(scores - log_ref[:, h : h + 1])
            grad_head = grad_mixed[:, h * HD : (h + 1) * HD]
            grad_probs = mm(grad_head, values, ((1,), (1,)))
            inner = jnp.sum(probs * grad_probs, axis=-1, keepdims=True)
            grad_scores = (probs * (grad_probs - inner)).astype(BF)
            turned = mm(grad_scores, keys, ((1,), (0,))) * 0.0625
            query_out[:, h * HD : (h + 1) * HD] = rotate(
                turned, cos_own[...], -sin_own[...]
            ).astype(BF)
            term_keys = mm(grad_scores, query, ((0,), (0,)))
            term_values = mm(probs.astype(BF), grad_head, ((0,), (0,)))
            grad_keys = term_keys if h == 0 else grad_keys + term_keys
            grad_values = term_values if h == 0 else grad_values + term_values
        context_out[:, :HD] = rotate(grad_keys * 0.0625, cos_ref[...], -sin_ref[...]).astype(BF)
        context_out[:, HD:] = grad_values.astype(BF)

    return call(
        kernel,
        "attend_back",
        (
            shaped(own, width, F32),
            shaped(own, width),
            shaped(8, width, F32),
            shaped(own, heads * HD),
            shaped(rows, 2 * HD),
        ),
        [(info, "s")]
        + [(part, "v") for part in parts]
        + [(middle, "v"), (grad_own, "v"), (gains, "v"), (queries, "v")]
        + [(array, "v") for array in (keys, values, log_sums, *tables)]
        + [(shard, "h") for shard in output_shards],
        [pltpu.VMEM((width, heads * HD), BF), pltpu.SemaphoreType.DMA((1,))],
    )


def store_sides(side, value, made, column, keep_ref, send_ref):
    blocks, share, _ = keep_ref.shape
    size = value.shape[1]
    for b in range(2 * blocks):
        made[b // 2, b % 2, :, :size] = value[b * share : (b + 1) * share].astype(BF)
    for b in range(blocks):
        keep_ref[b, :, column : column + size] = made[b, side, :, :size]
        send_ref[b, :, column : column + size] = made[b, 1 - side, :, :size]


def mixer_grads(
    info, normed, normed_own, grad_query, grad_context, low, mixed, gain_two, w_shards
):
    query_shards, context_shards = (arrays_of(groups) for groups in w_shards)
    offsets_q, offsets_c = (offsets_of(groups) for groups in w_shards)
    width = normed.shape[1]
    dp = lax.axis_size("dp")
    share = width // dp
    across = grad_query.shape[1]
    count = len(query_shards)
    first = jax.ShapeDtypeStruct((dp // 2, share, across + HD + LANES), BF)
    second = jax.ShapeDtypeStruct((dp // 2, share, across + HD), BF)

    def kernel(info_ref, *refs):
        normed_ref, own_ref, query_ref, context_ref, low_ref, mixed_ref, gain_ref = refs[:7]
        queries, contexts = refs[7 : 7 + count], refs[7 + count : 7 + 2 * count]
        keep_a, send_a, keep_b, send_b, w_q, w_c, made, sems = refs[7 + 2 * count :]
        side = info_ref[3]
        copies = row_copies(info_ref[0], queries, offsets_q, 0, across, w_q, 0, sems.at[0])
        copies_c = row_copies(info_ref[0], contexts, offsets_c, 0, 2 * HD, w_c, 0, sems.at[1])
        start_all(copies)
        start_all(copies_c)
        d_output = mm(low_ref[...], mixed_ref[...], ((0,), (0,)))
        halfway = across // HD // 2
        for h in range(across // HD):
            keep, send = (keep_a, send_a) if h < halfway else (keep_b, send_b)
            at = (2 * (h % halfway) + 1) * HD
            store_sides(side, d_output[:, h * HD : (h + 1) * HD], made, at, keep, send)
        d_query = mm(own_ref[...], query_ref[...], ((0,), (0,)))
        for h in range(across // HD):
            keep, send = (keep_a, send_a) if h < halfway else (keep_b, send_b)
            at = 2 * (h % halfway) * HD
            store_sides(side, d_query[:, h * HD : (h + 1) * HD], made, at, keep, send)
        d_context = mm(normed_ref[...], context_ref[...], ((0,), (0,)))
        store_sides(side, d_context[:, :HD], made, across, keep_a, send_a)
        store_sides(side, d_context[:, HD:], made, across, keep_b, send_b)
        wait_all(copies)
        wait_all(copies_c)
        gain_one = jnp.sum(d_query * w_q[...].astype(F32), axis=1, keepdims=True) + jnp.sum(
            d_context * w_c[...].astype(F32), axis=1, keepdims=True
        )
        second_gain = gain_ref[...].T
        lane = lax.broadcasted_iota(jnp.int32, (width, LANES), 1)
        both = jnp.where(lane == 0, gain_one, jnp.where(lane == 1, second_gain[:, 0:1], 0.0))
        store_sides(side, both, made, across + HD, keep_a, send_a)

    return call(
        kernel,
        "mixer_grads",
        (first, first, second, second),
        [(info, "s")]
        + [
            (array, "v")
            for array in (normed, normed_own, grad_query, grad_context, low, mixed, gain_two)
        ]
        + [(shard, "h") for shard in query_shards + context_shards],
        [
            pltpu.VMEM((width, across), BF),
            pltpu.VMEM((width, 2 * HD), BF),
            pltpu.VMEM((dp // 2, 2, share, across), BF),
            pltpu.SemaphoreType.DMA((2,)),
        ],
    )


def finish(info, grad_query, parts, grad_middle, tokens_own, gains, w_shards):
    query_shards, context_shards = (arrays_of(groups) for groups in w_shards)
    offsets_q, offsets_c = (offsets_of(groups) for groups in w_shards)
    own, width = grad_middle.shape
    across = grad_query.shape[1]
    count, n_parts = len(query_shards), len(parts)

    def kernel(info_ref, query_ref, *refs):
        part_refs, refs = refs[:n_parts], refs[n_parts:]
        middle_ref, x_ref, gain_ref = refs[:3]
        queries, contexts = refs[3 : 3 + count], refs[3 + count : 3 + 2 * count]
        out_ref, w_q, w_c, sems = refs[3 + 2 * count :]
        copies = row_copies(info_ref[0], queries, offsets_q, 0, across, w_q, 0, sems.at[0])
        copies_c = row_copies(info_ref[0], contexts, offsets_c, 0, 2 * HD, w_c, 0, sems.at[1])
        start_all(copies)
        start_all(copies_c)
        total = part_refs[0][...].astype(F32)
        for part_ref in part_refs[1:]:
            total = total + part_ref[...].astype(F32)
        x = x_ref[...].astype(F32)
        inverse = inverse_rms(x)
        wait_all(copies)
        wait_all(copies_c)
        grad_in = mm(query_ref[...], w_q[...], ((1,), (1,))) + mm(
            total.astype(BF), w_c[...], ((1,), (1,))
        )
        out_ref[...] = middle_ref[...] + norm_back(grad_in, x * inverse, inverse, gain_ref[0:1, :])

    return call(
        kernel,
        "finish",
        (shaped(own, width, F32),),
        [(info, "s"), (grad_query, "v")]
        + [(part, "v") for part in parts]
        + [(grad_middle, "v"), (tokens_own, "v"), (gains, "v")]
        + [(shard, "h") for shard in query_shards + context_shards],
        [
            pltpu.VMEM((width, across), BF),
            pltpu.VMEM((width, 2 * HD), BF),
            pltpu.SemaphoreType.DMA((2,)),
        ],
    )[0]


def feed_block(info, x, g, groups_a, groups_b, width, out_type):
    rows, depth = x.shape
    shards_a, shards_b = arrays_of(groups_a), arrays_of(groups_b)
    offsets, offsets_b = offsets_of(groups_a), offsets_of(groups_b)
    count = len(shards_a)
    half, cuts = column_cuts(width)

    def kernel(info_ref, x_ref, g_ref, *refs):
        first, second = refs[:count], refs[count : 2 * count]
        hid_ref, gate_ref, up_ref, feed_ref, back_ref = refs[2 * count : 2 * count + 5]
        w_gate, w_up, w_down, sems = refs[2 * count + 5 :]
        copies = []
        for n, (low, high) in enumerate(cuts):
            size = high - low
            source, at = (first, width + low) if high <= half else (second, width + low - half)
            group = []
            for shards, start, target in (
                (first, low, w_gate),
                (second, low, w_up),
                (source, at, w_down),
            ):
                own_offsets = offsets_b if shards is second else offsets
                group += row_copies(
                    info_ref[0], shards, own_offsets, start, size, target, low, sems.at[n]
                )
            copies.append(group)
            start_all(group)
        scale = 0.7978845608028654
        feed = back = None
        for n, (low, high) in enumerate(cuts):
            wait_all(copies[n])
            x, g = x_ref[...], g_ref[...]
            gate_w, up_w, down_w = w_gate[:, low:high], w_up[:, low:high], w_down[:, low:high]
            gate = mm(x, gate_w, ((1,), (0,)))
            up = mm(x, up_w, ((1,), (0,)))
            grad = mm(g, down_w, ((1,), (0,)))
            square = gate * gate
            tanh = jnp.tanh(scale * gate * (1.0 + 0.044715 * square))
            right = 0.5 * (1.0 + tanh)
            gelu = gate * right
            slope = right + gelu * (1.0 - tanh) * scale * (1.0 + 3 * 0.044715 * square)
            hidden = (gelu * up).astype(BF)
            grad_gate = (grad * up * slope).astype(BF)
            grad_up = (grad * gelu).astype(BF)
            hid_ref[:, low:high] = hidden
            gate_ref[:, low:high] = grad_gate
            up_ref[:, low:high] = grad_up
            feed_n = mm(hidden, down_w, ((1,), (1,)))
            back_n = mm(grad_gate, gate_w, ((1,), (1,))) + mm(grad_up, up_w, ((1,), (1,)))
            feed = feed_n if feed is None else feed + feed_n
            back = back_n if back is None else back + back_n
        feed_ref[...] = feed.astype(feed_ref.dtype)
        back_ref[...] = back.astype(back_ref.dtype)

    return call(
        kernel,
        "feed_block",
        (*[shaped(rows, width)] * 3, *[shaped(rows, depth, out_type)] * 2),
        [(info, "s"), (x, "v"), (g, "v")] + [(shard, "h") for shard in shards_a + shards_b],
        [pltpu.VMEM((depth, width), BF)] * 3 + [pltpu.SemaphoreType.DMA((3,))],
    )


def feed_grads(info, lefts, rights, low, high, firsts, whole):
    parts, dp = len(lefts), lax.axis_size("dp")
    depth, width = lefts[0].shape
    share = width // dp
    full = whole[0].shape[1]
    n_whole, n_part = full // TILE, (high - low) // TILE
    half = jax.ShapeDtypeStruct((dp // 2, share, full + high - low), BF)

    def kernel(info_ref, *refs):
        first_refs, whole_refs = refs[:parts], refs[parts : 2 * parts]
        left_refs, right_refs = refs[2 * parts : 3 * parts], refs[3 * parts : 4 * parts]
        keep_ref, send_ref, made = refs[4 * parts :]

        def one(rows, columns):
            total = None
            for row, column in zip(rows, columns):
                term = mm(row[...], column[...], ((0,), (0,)))
                total = term if total is None else total + term
            store_sides(info_ref[3], total, made, 0, keep_ref, send_ref)

        @pl.when(pl.program_id(0) < n_whole)
        def _():
            one(first_refs, whole_refs)

        @pl.when(pl.program_id(0) >= n_whole)
        def _():
            one(left_refs, right_refs)

    def whole_map(f, info_ref):
        return (0, jnp.minimum(f, n_whole - 1))

    def part_map(f, info_ref):
        return (0, low // TILE + jnp.maximum(f - n_whole, 0))

    fixed = pl.BlockSpec((depth, width), lambda f, info_ref: (0, 0))
    return pl.pallas_call(
        kernel,
        out_shape=(half, half),
        grid_spec=pltpu.PrefetchScalarGridSpec(
            num_scalar_prefetch=1,
            grid=(n_whole + n_part,),
            in_specs=[fixed] * parts
            + [pl.BlockSpec((depth, TILE), whole_map)] * parts
            + [fixed] * parts
            + [pl.BlockSpec((depth, TILE), part_map)] * parts,
            out_specs=[pl.BlockSpec((dp // 2, share, TILE), lambda f, info_ref: (0, 0, f))] * 2,
            scratch_shapes=[pltpu.VMEM((dp // 2, 2, share, TILE), BF)],
        ),
        compiler_params=pltpu.CompilerParams(vmem_limit_bytes=VMEM_BYTES),
        cost_estimate=pl.CostEstimate(flops=1, transcendentals=0, bytes_accessed=1),
        name="feed_grads",
    )(info, *firsts, *whole, *lefts, *rights)


class Halving:
    def __init__(self, keep, send, order):
        self.order = order
        self.left = [2**j for j in reversed(range(len(order)))]
        self.sent = swap(send, order[0])
        self.kept = keep
        self.left.remove(order[0])
        self.stage = 1

    def halve(self):
        me = lax.axis_index("dp")
        total = (self.kept.astype(F32) + self.sent.astype(F32)).astype(BF)
        bit = self.order[self.stage]
        total = total.reshape((2,) * len(self.left) + total.shape[-2:])
        axis = self.left.index(bit)
        side = (me // bit) % 2
        self.kept = lax.dynamic_index_in_dim(total, side, axis, keepdims=False)
        self.ready = lax.dynamic_index_in_dim(total, 1 - side, axis, keepdims=False)
        self.left.remove(bit)

    def send(self):
        self.sent = swap(self.ready, self.order[self.stage])
        self.stage += 1

    def step(self):
        self.halve()
        self.send()

    def done(self):
        while self.stage < len(self.order):
            self.step()
        return self.kept.astype(F32) + self.sent.astype(F32)


def step_both(first, second):
    first.halve()
    second.halve()
    first.kept, (second.kept, first.ready, second.ready) = after(
        first.kept, second.kept, first.ready, second.ready
    )
    first.send()
    second.send()


def after(values, *others):
    flat, tree = jax.tree.flatten((values, others))
    return jax.tree.unflatten(tree, lax.optimization_barrier(flat))


def local(
    tokens,
    cotangent,
    lengths,
    rates,
    query_weight,
    query_moment,
    query_average,
    output_weight,
    output_moment,
    output_average,
    gating_weight,
    gating_moment,
    gating_average,
    down_weight,
    down_moment,
    down_average,
    context_weight,
    context_moment,
    context_average,
    gains_weight,
    gains_moment,
    gains_average,
):
    row_count, width = tokens.shape
    dp, mp = lax.axis_size("dp"), lax.axis_size("mp")
    place = lax.axis_index("mp")
    own_count = row_count // mp
    own_start = place * own_count
    share, piece = width // dp, width // (dp * mp)
    forth, back = bit_orders()
    forth_first, back_first = forth[-1:] + forth[:-1], back[-1:] + back[:-1]
    length = lengths[0]
    places = jnp.arange(row_count, dtype=jnp.int32)
    me = lax.axis_index("dp")
    info = jnp.stack([me, own_start, length, me % 2]).astype(jnp.int32)

    def rows_at(tensor, step, count):
        return lax.dynamic_slice_in_dim(tensor, (place ^ step) * count, count, 0)

    gains_split = jnp.stack(split_three(gains_weight)).reshape(1, -1)
    message = jnp.concatenate(
        [
            query_weight.astype(BF),
            output_weight.T.astype(BF),
            context_weight.astype(BF).reshape(2 * piece, HD),
            jnp.pad(gains_split, ((0, 0), (0, HD - gains_split.shape[1]))),
        ],
        axis=0,
    )
    message = jnp.pad(message, ((0, -message.shape[0] % 16), (0, 0)))
    copies = jnp.broadcast_to(message[None], (mp, *message.shape))
    line = lax.all_to_all(copies, "mp", 0, 0, tiled=True)
    parts = [lax.dynamic_index_in_dim(line, place ^ k, 0, keepdims=False) for k in range(mp)]
    query_share = jnp.concatenate([part[:share] for part in parts], axis=1)
    output_share = jnp.concatenate([part[share : 2 * share] for part in parts], axis=1)
    rests = [line[k, 2 * share :] for k in range(mp)]
    context_share = jnp.concatenate(
        [
            jnp.concatenate(
                [
                    rest[:piece],
                    rest[piece : 2 * piece],
                    jnp.pad(
                        rest[2 * piece, : 6 * piece].reshape(6, piece).T, ((0, 0), (0, LANES - 6))
                    ),
                ],
                axis=1,
            )
            for rest in rests
        ],
        axis=0,
    )

    units = gating_weight.shape[2]
    padded = round_up(units, TILE)
    half = column_cuts(padded)[0]

    def pad_units(tensor):
        return jnp.pad(tensor, ((0, 0), (0, padded - units)))

    gating_low = gating_weight.astype(BF)
    down_low = pad_units(down_weight.T.astype(BF))
    feed_a = jnp.concatenate([pad_units(gating_low[0]), down_low[:, :half]], axis=1)
    feed_b = jnp.concatenate([pad_units(gating_low[1]), down_low[:, half:]], axis=1)
    first_a, first_b = swap(feed_a, forth[0]), swap(feed_b, back[0])
    own_a, own_b = swap(feed_a, forth[1]), swap(feed_b, back[1])
    early, contexts = spread_at_once(context_share, (first_a, first_b, own_a, own_b))
    first_a, first_b, own_a, own_b = early
    held_q, held_o = [query_share, swap(query_share, forth[0])], [output_share, swap(output_share, back[0])]

    cosine, sine_tab = rotation(row_count, HD)
    tokens_own = rows_at(tokens, 0, own_count)
    tables_own = (rows_at(cosine, 0, own_count), rows_at(sine_tab, 0, own_count))
    context_near, (tokens_own, tables_own) = after(contexts[1][0], tokens_own, tables_own)
    contexts = [contexts[0], (context_near, contexts[1][1])]
    contexts = lay(contexts)
    normed, normed_own, keys, values, gains = project(info, tokens, cosine, sine_tab, contexts)
    (held_q, held_o, cotangent_too), (gains,) = after((held_q, held_o, cotangent), gains)
    grad_low = jnp.where((places < length)[:, None], cotangent_too, jnp.zeros_like(cotangent))
    grad_blocks = [rows_at(grad_low, k, own_count) for k in range(mp)]
    w_queries = spread_on(held_q, forth)
    w_outputs = spread_on(held_o, back)
    w_queries[0], (grad_blocks,) = after(w_queries[0], grad_blocks)
    (sent_a, sent_b), (w_queries[0], w_outputs[0]) = after(
        (first_a, first_b), w_queries[0], w_outputs[0]
    )
    w_queries, w_outputs = spread_out(w_queries, forth), spread_out(w_outputs, back)
    w_queries, w_outputs = lay(w_queries), lay(w_outputs)
    pieces_a, offsets_a = spread_wide([feed_a, first_a], own_a, sent_a, forth)
    pieces_b, offsets_b = spread_wide([feed_b, first_b], own_b, sent_b, back)
    shards_a = spread_last(pieces_a[:2], offsets_a[:2], forth[-1])
    shards_b = spread_last(pieces_b[:2], offsets_b[:2], back[-1])
    normed_own, (shards_a, shards_b, grad_blocks) = after(
        normed_own, arrays_of(shards_a), arrays_of(shards_b), grad_blocks
    )
    shards_a = list(zip(shards_a, [offsets_a[:2], [k ^ 1 for k in offsets_a[:2]]]))
    shards_b = list(zip(shards_b, [offsets_b[:2], [k ^ 1 for k in offsets_b[:2]]]))
    queries, mixed, middle, normed_two_own, log_sums = attend(
        info, normed_own, keys, values, tokens_own, tables_own, gains, w_queries, w_outputs
    )

    (pieces_a[2:], pieces_b[2:]), (normed_two_own,) = after(
        (pieces_a[2:], pieces_b[2:]), normed_two_own
    )
    for n in range(2, len(pieces_a), 2):
        shards_a = shards_a + spread_last(pieces_a[n : n + 2], offsets_a[n : n + 2], forth[-1])
        shards_b = shards_b + spread_last(pieces_b[n : n + 2], offsets_b[n : n + 2], back[-1])
    shards_a, shards_b = lay(shards_a), lay(shards_b)
    blocks = [normed_two_own] + [across_heads(normed_two_own, k) for k in range(1, mp)]
    made = []
    for k in range(mp):
        if k > 0:
            blocks[k], (made[k - 1],) = after(blocks[k], made[k - 1])
        made.append(
            feed_block(
                info, blocks[k], grad_blocks[k], shards_a, shards_b, padded, F32 if k == 0 else BF
            )
        )
    hidden, grad_gate, grad_up, feed_parts, back_parts = (
        [made[k][n] for k in range(mp)] for n in range(5)
    )
    back_parts = back_parts[:1] + [across_heads(back_parts[k], k) for k in range(1, mp)]
    grad_up, (back_parts[1],) = after(grad_up, back_parts[1])
    keep_b, send_b = feed_grads(info, grad_blocks, hidden, half, padded, blocks, grad_up)
    grad_gate, (keep_b, back_parts[2:-1]) = after(grad_gate, keep_b, back_parts[2:-1])
    keep_a, send_a = feed_grads(info, grad_blocks, hidden, 0, half, blocks, grad_gate)
    held = (back_parts, feed_parts, keep_a, keep_b, normed, normed_own, mixed, middle, queries)
    held += (keys, values, log_sums, gains, cosine, sine_tab, tables_own, tokens_own, grad_blocks)
    held += (arrays_of(w_queries), arrays_of(contexts), arrays_of(w_outputs))
    (send_a, send_b), held = after((send_a, send_b), *held)
    back_parts, feed_parts, keep_a, keep_b, normed, normed_own, mixed, middle, queries = held[:9]
    keys, values, log_sums, gains, cosine, sine_tab, tables_own, tokens_own, grad_blocks = held[9:18]
    w_queries = list(zip(held[18], offsets_of(w_queries)))
    contexts = list(zip(held[19], offsets_of(contexts)))
    w_outputs = list(zip(held[20], offsets_of(w_outputs)))
    flow_a, flow_b = Halving(keep_a, send_a, forth_first), Halving(keep_b, send_b, back_first)
    flow_a.sent, (flow_b.sent, flow_a.kept, flow_b.kept) = after(
        flow_a.sent, flow_b.sent, flow_a.kept, flow_b.kept
    )
    step_both(flow_a, flow_b)
    feed_parts, (back_parts,) = after(feed_parts, back_parts)
    feed_line = jnp.stack([part.astype(BF) for part in feed_parts])
    feed_line = jnp.stack(
        [lax.dynamic_index_in_dim(feed_line, place ^ k, 0, keepdims=False) for k in range(mp)]
    )
    feed_line = lax.all_to_all(feed_line, "mp", 0, 0, tiled=True)
    back_parts, (flow_a.kept, flow_b.kept) = after(back_parts, flow_a.kept, flow_b.kept)

    grad_middle, middle_low, gain_two, grad_query, grad_context = attend_back(
        info,
        back_parts,
        middle,
        grad_blocks[0],
        gains,
        queries,
        keys,
        values,
        log_sums,
        (cosine, sine_tab, *tables_own),
        w_outputs,
    )

    w_shards = (w_queries, contexts)
    keep_a, send_a, keep_b, send_b = mixer_grads(
        info, normed, normed_own, grad_query, grad_context, middle_low, mixed, gain_two, w_shards
    )
    (send_a, send_b), (flow_a.sent, flow_b.sent) = after((send_a, send_b), flow_a.sent, flow_b.sent)
    step_both(flow_a, flow_b)
    mixer_a, mixer_b = Halving(keep_a, send_a, forth_first), Halving(keep_b, send_b, back_first)
    mixer_a.sent, (mixer_b.sent, flow_a.kept, flow_b.kept) = after(
        mixer_a.sent, mixer_b.sent, flow_a.kept, flow_b.kept
    )
    step_both(mixer_a, mixer_b)
    mixer_a.sent, (mixer_b.sent, mixer_a.kept, mixer_b.kept, flow_a.sent, flow_b.sent) = after(
        mixer_a.sent, mixer_b.sent, mixer_a.kept, mixer_b.kept, flow_a.sent, flow_b.sent
    )
    step_both(mixer_a, mixer_b)
    (flow_a.sent, flow_b.sent), (mixer_a.sent, mixer_b.sent) = after(
        (flow_a.sent, flow_b.sent), mixer_a.sent, mixer_b.sent
    )
    context_line, (feed_line,) = after(grad_context, feed_line)
    context_line = context_line.reshape(mp, own_count, 2 * HD)
    context_line = lax.all_to_all(context_line, "mp", 0, 0, tiled=True)
    feed_one, feed_two = flow_a.done(), flow_b.done()
    mixer_one, mixer_two = mixer_a.done(), mixer_b.done()
    across, halfway = grad_query.shape[1], mp // 2
    shares = [
        (mixer_one if k < halfway else mixer_two)[
            :, (k % halfway) * 2 * HD : (k % halfway + 1) * 2 * HD
        ]
        for k in range(mp)
    ]
    share_context = jnp.concatenate([mixer_one[:, across:], mixer_two[:, across:]], axis=1)
    wide = share_context.shape[1]
    total = shares[0]
    for k in range(1, mp):
        total = total + across_heads(shares[k].astype(BF), k).astype(F32)
    sum_context = rows_at(share_context, 0, piece)
    for k in range(1, mp):
        sent = across_heads(rows_at(share_context, k, piece).astype(BF), k)
        sum_context = sum_context + sent.astype(F32)
    context_own = jnp.sum(context_line.astype(F32), axis=0)
    tokens_grad = finish(info, grad_query, [context_own], grad_middle, tokens_own, gains, w_shards)
    block_out = middle + jnp.sum(feed_line.astype(F32), axis=0)

    total, (tokens_grad,) = after(total, tokens_grad)
    sum_query, sum_output = total[:, :HD], total[:, HD:].T
    sum_gains = jnp.stack([sum_context[:, HD] / gains_weight[0], sum_context[:, HD + 1]])
    sum_context = jnp.stack([sum_context[:, :HD], sum_context[:, wide - HD :]])
    sum_gating = jnp.stack([feed_one[:, :units], feed_two[:, :units]])
    sum_down = jnp.concatenate([feed_one[:, padded:], feed_two[:, padded:]], axis=1)[:, :units].T

    query_grads, query_moments, query_averages, query_updated = advance(
        sum_query, query_moment, query_average, query_weight, rates[0]
    )
    output_grads, output_moments, output_averages, output_updated = advance(
        sum_output, output_moment, output_average, output_weight, rates[1]
    )
    gating_grads, gating_moments, gating_averages, gating_updated = advance(
        sum_gating, gating_moment, gating_average, gating_weight, rates[2]
    )
    down_grads, down_moments, down_averages, down_updated = advance(
        sum_down, down_moment, down_average, down_weight, rates[3]
    )
    context_grads, context_moments, context_averages, context_updated = advance(
        sum_context, context_moment, context_average, context_weight, rates[4]
    )
    gains_grads, gains_moments, gains_averages, gains_updated = advance(
        sum_gains, gains_moment, gains_average, gains_weight, rates[5]
    )
    return (
        block_out,
        tokens_grad,
        query_grads,
        query_moments,
        query_averages,
        query_updated,
        output_grads,
        output_moments,
        output_averages,
        output_updated,
        gating_grads,
        gating_moments,
        gating_averages,
        gating_updated,
        down_grads,
        down_moments,
        down_averages,
        down_updated,
        context_grads,
        context_moments,
        context_averages,
        context_updated,
        gains_grads,
        gains_moments,
        gains_averages,
        gains_updated,
    )


def solution(mesh):
    return jax.shard_map(
        local,
        mesh=mesh,
        in_specs=(
            P("dp", None),
            P("dp", None),
            P("dp"),
            P(),
            P("dp", "mp"),
            P("dp", "mp"),
            P("dp", "mp"),
            P("mp", "dp"),
            P("mp", "dp"),
            P("mp", "dp"),
            P(None, "dp", "mp"),
            P(None, "dp", "mp"),
            P(None, "dp", "mp"),
            P("mp", "dp"),
            P("mp", "dp"),
            P("mp", "dp"),
            P(None, ("dp", "mp"), None),
            P(None, ("dp", "mp"), None),
            P(None, ("dp", "mp"), None),
            P(None, ("dp", "mp")),
            P(None, ("dp", "mp")),
            P(None, ("dp", "mp")),
        ),
        out_specs=(
            P(("dp", "mp"), None),
            P(("dp", "mp"), None),
            P("dp", "mp"),
            P("dp", "mp"),
            P("dp", "mp"),
            P("dp", "mp"),
            P("mp", "dp"),
            P("mp", "dp"),
            P("mp", "dp"),
            P("mp", "dp"),
            P(None, "dp", "mp"),
            P(None, "dp", "mp"),
            P(None, "dp", "mp"),
            P(None, "dp", "mp"),
            P("mp", "dp"),
            P("mp", "dp"),
            P("mp", "dp"),
            P("mp", "dp"),
            P(None, ("dp", "mp"), None),
            P(None, ("dp", "mp"), None),
            P(None, ("dp", "mp"), None),
            P(None, ("dp", "mp"), None),
            P(None, ("dp", "mp")),
            P(None, ("dp", "mp")),
            P(None, ("dp", "mp")),
            P(None, ("dp", "mp")),
        ),
        check_vma=False,
    )
```
